512 devices in a mesh: row: 32 (over y, x, core), col: 16 (over z).
Axes of the slice: x: 4, y: 4, z: 16, core: 2. Of those that a mesh axis runs over, the one named last changes fastest.
Arguments:
- ancestor_inverse: bfloat16 [8192, 8192], P('row', 'col'), may hold values from -6 to 6
- panel_one: bfloat16 [8192, 512], P(('row', 'col')), may hold values from -0.0625 to 0.0625
- ancestors_one: int32 [2, 28], replicated, may hold values from 0 to 31, as said below
- diag_inverse_one: bfloat16 [2, 256, 256], replicated, may hold values from -6 to 6
- panel_two: bfloat16 [8192, 512], P(('row', 'col')), may hold values from -0.0625 to 0.0625
- link_two: bfloat16 [2, 256, 256], replicated, may hold values from -0.375 to 0.375
- ancestors_two: int32 [2, 24], replicated, may hold values from 0 to 31, as said below
- diag_inverse_two: bfloat16 [2, 256, 256], replicated, may hold values from -6 to 6
- widths: int32 [4], replicated, may hold values from 128 to 256, as said below
Outputs:
- column_one: bfloat16 [8192, 512], P(('row', 'col'))
- block_one: bfloat16 [2, 256, 256], replicated
- column_two: bfloat16 [8192, 512], P(('row', 'col'))
- parent_rows_two: bfloat16 [2, 256, 256], replicated
- block_two: bfloat16 [2, 256, 256], replicated
The draws below stay inside these ranges and needn't reach their ends.
Inputs may be any that keep to these rules, and one draw needn't show every extreme that they name: `ancestors_one`: each row lists 28 distinct tiles in ascending order; 0 and 31 are always among them. `ancestors_two`: row s lists 24 distinct entries of row s of ancestors_one in ascending order; 0 and 31 are always among them. `widths`: at least one supernode uses all 256 columns.
All inputs are finite; a program needn't handle non-finite values.
Results may differ from the reference program's by a relative error of at most 0.0055.
Values may be sent and summed in bfloat16 or wider, within the bound.
No kernel may reach another device: no remote copies, remote signals or barrier semaphores. Data moves between devices by JAX's collectives and lax.ppermute only.
A program may use at most 64 MiB of HBM per device.

```python
import jax
import jax.numpy as jnp

W = 256
TILES = 32
M = 8192
R_ONE = 28
R_TWO = 24


def ancestor_rows(key):
    base_key = jax.random.fold_in(key, 11)
    chosen_rows = []
    for sibling in range(2):
        sibling_key = jax.random.fold_in(base_key, sibling)
        middle_rows = jax.random.permutation(sibling_key, TILES - 2)[:R_ONE - 2].astype(jnp.int32) + 1
        picked = jnp.concatenate([jnp.zeros((1,), jnp.int32), middle_rows, jnp.full((1,), TILES - 1, jnp.int32)])
        chosen_rows.append(jnp.sort(picked))
    return jnp.stack(chosen_rows).astype(jnp.int32)


def draw_ancestors_one(key, part):
    return ancestor_rows(key)


def draw_ancestors_two(key, part):
    parent_rows = ancestor_rows(key)
    base_key = jax.random.fold_in(key, 23)
    chosen_rows = []
    for sibling in range(2):
        sibling_key = jax.random.fold_in(base_key, sibling)
        middle_index = jax.random.permutation(sibling_key, R_ONE - 2)[:R_TWO - 2].astype(jnp.int32) + 1
        picked = jnp.concatenate([parent_rows[sibling, 0:1], parent_rows[sibling][middle_index], parent_rows[sibling, R_ONE - 1:R_ONE]])
        chosen_rows.append(jnp.sort(picked))
    return jnp.stack(chosen_rows).astype(jnp.int32)


def draw_widths(key, part):
    width_key = jax.random.fold_in(key, 31)
    place_key = jax.random.fold_in(key, 37)
    drawn_widths = jax.random.randint(width_key, (4,), W // 2, W + 1, dtype=jnp.int32)
    full_index = jax.random.randint(place_key, (), 0, 4, dtype=jnp.int32)
    return jnp.where(jnp.arange(4, dtype=jnp.int32) == full_index, W, drawn_widths).astype(jnp.int32)


def spiked(result, stream_key, source, target, shards_of, factor):
    def block_of(dim):
        return (jnp.arange(result.shape[dim]) // (result.shape[dim] // shards_of)).reshape((-1,) + (1,) * (result.ndim - 1 - dim))

    first = jax.random.permutation(stream_key, shards_of)[block_of(target)]
    second = (block_of(target) + shards_of // 2) % shards_of
    return jnp.where((block_of(source) == first) | (block_of(source) == second), factor * result, result)


def shard_levels(own_key, dims, shards, low, largest):
    level = 1.0
    for position, shards_of in shards:
        heights = jax.random.uniform(jax.random.fold_in(jax.random.fold_in(own_key, 6), position), (shards_of,), jnp.float32, low / len(shards), largest / len(shards))
        level = level * jnp.repeat(jnp.exp(heights), dims[position] // shards_of).reshape((-1,) + (1,) * (len(dims) - 1 - position))
    return level


def normal_values(rng, extent, spread, limit, split=(), held_as=jnp.bfloat16):
    drawn = jax.random.normal(rng, extent, jnp.float32) * spread
    if len(split) > 0:
        drawn = shard_levels(rng, extent, split, -0.22, 0.18) * drawn
    return jnp.clip(drawn, min=-limit, max=limit).astype(held_as)


def bell_draw_with(own_key, shape, deviation, bound, shards, heavy, kind=jnp.bfloat16):
    array = deviation * jax.random.normal(own_key, shape, jnp.float32)
    if shards:
        array = array * shard_levels(own_key, shape, shards, -0.22, 0.18)
    return jnp.clip(spiked(array, jax.random.fold_in(own_key, 3), *heavy), -bound, bound).astype(kind)


def setup_inputs(seed: int = 0) -> dict:
    key_list = jax.random.split(jax.random.key(seed), 10)
    ancestor_inverse = bell_draw_with(key_list[0], (M, M), 1.0, 6.0, ((0, 32), (1, 16)), (1, 0, 32, 2.75))
    panel_one = normal_values(key_list[1], (M, 2 * W), M ** -0.5, 0.0625, ((0, 512),))
    ancestors_one = draw_ancestors_one(jax.random.fold_in(key_list[9], 71), 0)
    diag_inverse_one = normal_values(key_list[3], (2, W, W), 1.0, 6.0)
    panel_two = normal_values(key_list[4], (M, 2 * W), M ** -0.5, 0.0625, ((0, 512),))
    link_two = normal_values(key_list[5], (2, W, W), W ** -0.5, 0.375)
    ancestors_two = draw_ancestors_two(jax.random.fold_in(key_list[9], 71), 0)
    diag_inverse_two = normal_values(key_list[7], (2, W, W), 1.0, 6.0)
    widths = draw_widths(jax.random.fold_in(key_list[9], 71), 0)
    return {"ancestor_inverse": ancestor_inverse, "panel_one": panel_one, "ancestors_one": ancestors_one, "diag_inverse_one": diag_inverse_one, "panel_two": panel_two, "link_two": link_two, "ancestors_two": ancestors_two, "diag_inverse_two": diag_inverse_two, "widths": widths}


def row_members(ancestors, tile_count, tile_width):
    tile_ids = jnp.arange(tile_count, dtype=jnp.int32)
    matches = (ancestors[:, :, None] == tile_ids[None, None, :]).astype(jnp.int32)
    member = jnp.sum(matches, axis=1)
    return jnp.repeat(member, tile_width, axis=1).astype(jnp.bfloat16)


def reference(ancestor_inverse, panel_one, ancestors_one, diag_inverse_one, panel_two, link_two, ancestors_two, diag_inverse_two, widths):
    tile_width = diag_inverse_one.shape[-1]
    matrix_order = ancestor_inverse.shape[0]
    tile_count = matrix_order // tile_width
    columns = jnp.arange(tile_width, dtype=jnp.int32)
    keep_columns = (columns[None, :] < widths[:, None]).astype(jnp.bfloat16)
    member_one = row_members(ancestors_one, tile_count, tile_width)
    member_two = row_members(ancestors_two, tile_count, tile_width)
    mask_one = (member_one.T[:, :, None] * keep_columns[0:2][None, :, :]).reshape(matrix_order, 2 * tile_width)
    mask_two = (member_two.T[:, :, None] * keep_columns[2:4][None, :, :]).reshape(matrix_order, 2 * tile_width)
    lower_one = panel_one * mask_one
    lower_two = panel_two * mask_two
    product = jnp.dot(ancestor_inverse, jnp.concatenate([lower_one, lower_two], axis=1), preferred_element_type=jnp.float32)
    columns_first = []
    blocks_first = []
    columns_second = []
    parent_blocks = []
    blocks_second = []
    for sibling in range(2):
        low = sibling * tile_width
        high = (sibling + 1) * tile_width
        keep_parent = keep_columns[sibling]
        keep_child = keep_columns[2 + sibling]
        pivot_one = diag_inverse_one[sibling].astype(jnp.float32) * (keep_parent[:, None] * keep_parent[None, :]).astype(jnp.float32)
        pivot_two = diag_inverse_two[sibling].astype(jnp.float32) * (keep_child[:, None] * keep_child[None, :]).astype(jnp.float32)
        link_masked = link_two[sibling] * keep_parent[:, None] * keep_child[None, :]
        lower_first = lower_one[:, low:high]
        lower_second = lower_two[:, low:high]
        column_first = (-(product[:, low:high] * member_one[sibling][:, None].astype(jnp.float32))).astype(jnp.bfloat16)
        block_first = (pivot_one - jnp.dot(lower_first.T, column_first, preferred_element_type=jnp.float32)).astype(jnp.bfloat16)
        second_total = product[:, 2 * tile_width + low:2 * tile_width + high] + jnp.dot(column_first, link_masked, preferred_element_type=jnp.float32)
        column_second = (-(second_total * member_two[sibling][:, None].astype(jnp.float32))).astype(jnp.bfloat16)
        cross_total = jnp.dot(column_first.T, lower_second, preferred_element_type=jnp.float32)
        parent_block = (-(jnp.dot(block_first, link_masked, preferred_element_type=jnp.float32) + cross_total)).astype(jnp.bfloat16)
        lower_total = jnp.dot(lower_second.T, column_second, preferred_element_type=jnp.float32)
        block_second = (pivot_two - jnp.dot(link_masked.T, parent_block, preferred_element_type=jnp.float32) - lower_total).astype(jnp.bfloat16)
        columns_first.append(column_first)
        blocks_first.append(block_first)
        columns_second.append(column_second)
        parent_blocks.append(parent_block)
        blocks_second.append(block_second)
    return (jnp.concatenate(columns_first, axis=1), jnp.stack(blocks_first), jnp.concatenate(columns_second, axis=1), jnp.stack(parent_blocks), jnp.stack(blocks_second))
```

```python
import jax
import jax.numpy as jnp
from jax import lax
from jax.sharding import PartitionSpec as P

F32 = jnp.float32
BF16 = jnp.bfloat16


def exchange(blocks, axis):
    return lax.all_to_all(blocks, axis, split_axis=0, concat_axis=0, tiled=True)


def spread(block, axis):
    copies = jnp.broadcast_to(block[None], (lax.axis_size(axis),) + block.shape)
    return exchange(copies, axis)


def tile_members(ancestors, first_row, row_count, tile_width):
    row_ids = first_row + jnp.arange(row_count, dtype=jnp.int32)
    tile_of_row = row_ids // tile_width
    matches = (ancestors[:, None, :] == tile_of_row[None, :, None]).astype(jnp.int32)
    return jnp.sum(matches, axis=2).astype(BF16)


def row_mask(members, keep_pair):
    combined = members.T[:, :, None] * keep_pair[None, :, :]
    return combined.reshape(members.shape[1], -1)


def dot_t(left, right):
    return lax.dot_general(left, right, (((0,), (0,)), ((), ())), preferred_element_type=F32)


def local(
    ancestor_inverse,
    panel_one,
    ancestors_one,
    diag_inverse_one,
    panel_two,
    link_two,
    ancestors_two,
    diag_inverse_two,
    widths,
):
    w = diag_inverse_one.shape[-1]
    rows_n = lax.axis_size("row")
    cols_n = lax.axis_size("col")
    local_rows = ancestor_inverse.shape[0]
    share = panel_one.shape[0]
    start = lax.axis_index("row") * local_rows + lax.axis_index("col") * share
    columns = jnp.arange(w, dtype=jnp.int32)
    keep = (columns[None, :] < widths[:, None]).astype(BF16)
    member_one = tile_members(ancestors_one, start, share, w)
    member_two = tile_members(ancestors_two, start, share, w)
    lower = jnp.concatenate(
        [panel_one * row_mask(member_one, keep[0:2]), panel_two * row_mask(member_two, keep[2:4])],
        axis=1,
    )
    group = rows_n // cols_n
    pairs = []
    for r in range(rows_n):
        for c in range(cols_n):
            pairs.append((r * cols_n + c, ((r % group) * cols_n + c) * cols_n + r // group))
    moved = lax.ppermute(lower, ("row", "col"), pairs)
    lower_rows = spread(lower, "col").reshape(local_rows, 4 * w)
    lower_cols = spread(moved, "row").reshape(rows_n * share, 4 * w)

    part = jnp.dot(ancestor_inverse, lower_cols, preferred_element_type=F32).astype(BF16)
    blocks = []
    for s in range(2):
        first = slice(s * w, (s + 1) * w)
        second = slice((2 + s) * w, (3 + s) * w)
        blocks.append(dot_t(lower_rows[:, first], part[:, first]))
        blocks.append(dot_t(lower_rows[:, second], part[:, first]))
        blocks.append(dot_t(lower_rows[:, second], part[:, second]))
    sums = jnp.stack(blocks).astype(BF16).reshape(rows_n, -1, w)
    sums = jnp.sum(exchange(sums, "row").astype(F32), axis=0).astype(BF16)
    chunk = sums.shape[0]

    part4 = part.reshape(cols_n, share, 4, w).transpose(0, 2, 1, 3).reshape(cols_n, 4 * share, w)
    packed = jnp.concatenate([jnp.broadcast_to(sums[None], (cols_n, chunk, w)), part4], axis=1)
    packed = jnp.sum(exchange(packed, "col").astype(F32), axis=0)
    total = spread(packed[:chunk].astype(BF16), "row").reshape(6, w, w)
    product = packed[chunk:].reshape(4, share, w)

    keep_parent, keep_child = keep[0:2], keep[2:4]
    link = link_two * keep_parent[:, :, None] * keep_child[:, None, :]
    column_one = []
    column_two = []
    block_one = []
    parent_rows = []
    block_two = []
    for s in range(2):
        one = -(product[s] * member_one[s][:, None].astype(F32))
        one = one.astype(BF16)
        two = product[2 + s] + jnp.dot(one, link[s], preferred_element_type=F32)
        two = (-(two * member_two[s][:, None].astype(F32))).astype(BF16)
        column_one.append(one)
        column_two.append(two)
        pivot_one = diag_inverse_one[s] * keep_parent[s][:, None] * keep_parent[s][None, :]
        pivot_two = diag_inverse_two[s] * keep_child[s][:, None] * keep_child[s][None, :]
        corner = total[3 * s].astype(F32)
        cross_t = total[3 * s + 1]
        last = total[3 * s + 2].astype(F32)
        block = (pivot_one.astype(F32) + corner).astype(BF16)
        parent = jnp.dot(block, link[s], preferred_element_type=F32) - cross_t.T.astype(F32)
        parent = (-parent).astype(BF16)
        child = pivot_two.astype(F32) + last
        child = child - jnp.dot(cross_t, link[s], preferred_element_type=F32)
        child = (child - dot_t(link[s], parent)).astype(BF16)
        block_one.append(block)
        parent_rows.append(parent)
        block_two.append(child)
    return (
        jnp.concatenate(column_one, axis=1),
        jnp.stack(block_one),
        jnp.concatenate(column_two, axis=1),
        jnp.stack(parent_rows),
        jnp.stack(block_two),
    )


def solution(mesh):
    shared = P(("row", "col"), None)
    in_specs = (P("row", "col"), shared, P(), P(), shared, P(), P(), P(), P())
    out_specs = (shared, P(), shared, P(), P())
    return jax.shard_map(local, mesh=mesh, in_specs=in_specs, out_specs=out_specs, check_vma=False)
```

```python
import functools

import jax
import jax.numpy as jnp
from jax import lax
from jax.experimental import pallas as pl
from jax.experimental.pallas import tpu as pltpu
from jax.sharding import PartitionSpec as P

F32 = jnp.float32
BF16 = jnp.bfloat16
VMEM = pl.BlockSpec(memory_space=pltpu.VMEM)
SMEM = pl.BlockSpec(memory_space=pltpu.SMEM)


def kernel_call(body, name, specs, outs, cost=(0, 0)):
    return pl.pallas_call(
        body,
        name=name,
        in_specs=specs,
        out_specs=[VMEM] * len(outs),
        out_shape=[jax.ShapeDtypeStruct(shape, BF16) for shape in outs],
        compiler_params=pltpu.CompilerParams(vmem_limit_bytes=40 * 1024 * 1024),
        cost_estimate=pl.CostEstimate(flops=cost[0], bytes_accessed=cost[1], transcendentals=0),
    )


def exchange(blocks, axis):
    return lax.all_to_all(blocks, axis, split_axis=0, concat_axis=0, tiled=True)


def dot(left, right):
    return jnp.dot(left, right, preferred_element_type=F32)


def dot_t(left, right):
    return lax.dot_general(left, right, (((0,), (0,)), ((), ())), preferred_element_type=F32)


def is_member(table, s, tile):
    found = table[s, 0] == tile
    for i in range(1, table.shape[1]):
        found = found | (table[s, i] == tile)
    return found


def mask_body(w, tile, one, two, anc_one, anc_two, widths, lower):
    column = lax.broadcasted_iota(jnp.int32, (one.shape[0], w), 1)
    for k in range(4):
        source, table, s = (one, anc_one, k) if k < 2 else (two, anc_two, k - 2)
        width = jnp.where(is_member(table, s, tile[0]), widths[k], 0)
        value = source[:, s * w : (s + 1) * w]
        lower[:, k * w : (k + 1) * w] = jnp.where(column < width, value, jnp.zeros_like(value))


def product_body(w, core, same, other, lower, part):
    share = part.shape[1]
    half = same.shape[0] // share
    for source, place in ((same, core[0] * half), (other, (1 - core[0]) * half)):
        for k in range(4):
            span = slice(k * w, (k + 1) * w)
            value = dot(source[...], lower[:, span]).astype(BF16)
            part[pl.ds(place, half), :, span] = value.reshape(half, share, w)


def reduced(received):
    total = received[0].astype(F32)
    for i in range(1, received.shape[0]):
        total = total + received[i].astype(F32)
    return total


def row_sum_body(received, copies):
    value = reduced(received).astype(BF16)
    for i in range(copies.shape[0]):
        copies[i] = value


def col_sum_body(received, pivot, copies):
    value = (reduced(received) + pivot[...].astype(F32)).astype(BF16)
    for i in range(copies.shape[0]):
        copies[i] = value


def masked_link(w, link, widths, s):
    row = lax.broadcasted_iota(jnp.int32, (w, w), 0)
    column = lax.broadcasted_iota(jnp.int32, (w, w), 1)
    value = link[s]
    inside = (row < widths[s]) & (column < widths[2 + s])
    return jnp.where(inside, value, jnp.zeros_like(value))


def column_body(w, tile, received, lower, link, anc_one, anc_two, widths, columns, sums):
    total = reduced(received)
    for s in range(2):
        first = slice(s * w, (s + 1) * w)
        second = slice((2 + s) * w, (3 + s) * w)
        here_one = jnp.where(is_member(anc_one, s, tile[0]), 1.0, 0.0)
        here_two = jnp.where(is_member(anc_two, s, tile[0]), 1.0, 0.0)
        one = (-(total[:, first] * here_one)).astype(BF16)
        two = total[:, second] + dot(one, masked_link(w, link, widths, s))
        two = (-(two * here_two)).astype(BF16)
        columns[:, first] = one
        columns[:, second] = two
        sums[3 * s] = (-dot_t(lower[:, first], one)).astype(BF16)
        sums[3 * s + 1] = dot_t(one, lower[:, second]).astype(BF16)
        sums[3 * s + 2] = (-dot_t(lower[:, second], two)).astype(BF16)


def final_body(w, total, link, widths, block_one, parent_rows, block_two):
    for s in range(2):
        tie = masked_link(w, link, widths, s)
        block = total[3 * s]
        block_one[s] = block
        parent = (-(dot(block, tie) + total[3 * s + 1].astype(F32))).astype(BF16)
        parent_rows[s] = parent
        block_two[s] = (total[3 * s + 2].astype(F32) - dot_t(tie, parent)).astype(BF16)


def local(
    ancestor_inverse,
    panel_one,
    ancestors_one,
    diag_inverse_one,
    panel_two,
    link_two,
    ancestors_two,
    diag_inverse_two,
    widths,
):
    w = diag_inverse_one.shape[-1]
    rows_n = lax.axis_size("row")
    cols_n = lax.axis_size("col")
    local_rows = ancestor_inverse.shape[0]
    share = panel_one.shape[0]
    group = rows_n // cols_n
    row, col = lax.axis_index("row"), lax.axis_index("col")
    core = (row % group).astype(jnp.int32)
    home_tile = row.astype(jnp.int32).reshape(1)
    away_tile = (col * group + row // cols_n).astype(jnp.int32).reshape(1)

    same_pairs, other_pairs, out_pairs, back_pairs = [], [], [], []
    for r in range(rows_n):
        for c in range(cols_n):
            here, core_r = r * cols_n + c, r % group
            same_pairs.append((here, (c * group + core_r) * cols_n + r // group))
            other_pairs.append((here, (c * group + 1 - core_r) * cols_n + r // group))
            away = (core_r * cols_n + c) * cols_n + r // group
            out_pairs.append((here, away))
            back_pairs.append((away, here))
    both = ("row", "col")
    same = lax.dynamic_slice_in_dim(ancestor_inverse, core * w, w, axis=1)
    other = lax.dynamic_slice_in_dim(ancestor_inverse, (1 - core) * w, w, axis=1)
    same = lax.ppermute(same, both, same_pairs)
    other = lax.ppermute(other, both, other_pairs)

    (lower,) = kernel_call(
        functools.partial(mask_body, w),
        "mask",
        [SMEM, VMEM, VMEM, SMEM, SMEM, SMEM],
        [(share, 4 * w)],
    )(home_tile, panel_one, panel_two, ancestors_one, ancestors_two, widths)
    moved = lax.ppermute(lower, both, out_pairs)
    lower_tile = lax.all_gather(lower, "col", axis=0, tiled=True)

    (part,) = kernel_call(
        functools.partial(product_body, w),
        "product",
        [SMEM] + [VMEM] * 3,
        [(rows_n, share, 4 * w)],
    )(core.reshape(1), same, other, lower_tile)
    part = exchange(part, "row")
    columns, sums = kernel_call(
        functools.partial(column_body, w),
        "columns",
        [SMEM, VMEM, VMEM, VMEM, SMEM, SMEM, SMEM],
        [(share, 4 * w), (6, w, w)],
    )(away_tile, part, moved, link_two, ancestors_one, ancestors_two, widths)
    columns = lax.ppermute(columns, both, back_pairs)

    chunk = 6 * w // rows_n
    sums = exchange(sums.reshape(rows_n, chunk, w), "row")
    (sum_copies,) = kernel_call(row_sum_body, "row_sum", [VMEM], [(cols_n, chunk, w)])(sums)
    sums = exchange(sum_copies, "col")

    keep = (jnp.arange(w, dtype=jnp.int32)[None, :] < widths[:, None]).astype(BF16)
    pivot_one = diag_inverse_one * keep[0:2, :, None] * keep[0:2, None, :]
    pivot_two = diag_inverse_two * keep[2:4, :, None] * keep[2:4, None, :]
    pivots = jnp.stack([pivot_one, jnp.zeros_like(pivot_one), pivot_two], axis=1)
    pivot = lax.dynamic_slice_in_dim(
        pivots.reshape(6 * w, w), lax.axis_index("row") * chunk, chunk, axis=0
    )
    (total_copies,) = kernel_call(col_sum_body, "col_sum", [VMEM] * 2, [(rows_n, chunk, w)])(
        sums, pivot
    )
    total = exchange(total_copies, "row").reshape(6, w, w)

    block_one, parent_rows, block_two = kernel_call(
        functools.partial(final_body, w), "final", [VMEM, VMEM, SMEM], [(2, w, w)] * 3
    )(total, link_two, widths)
    return columns[:, : 2 * w], block_one, columns[:, 2 * w :], parent_rows, block_two


def solution(mesh):
    shared = P(("row", "col"), None)
    in_specs = (P("row", "col"), shared, P(), P(), shared, P(), P(), P(), P())
    out_specs = (shared, P(), shared, P(), P())
    return jax.shard_map(local, mesh=mesh, in_specs=in_specs, out_specs=out_specs, check_vma=False)
```

```python
import functools

import jax
import jax.numpy as jnp
from jax import lax
from jax.experimental import pallas as pl
from jax.experimental.pallas import tpu as pltpu
from jax.sharding import Mesh
from jax.sharding import PartitionSpec as P

F32 = jnp.float32
BF16 = jnp.bfloat16
VMEM = pl.BlockSpec(memory_space=pltpu.VMEM)
SMEM = pl.BlockSpec(memory_space=pltpu.SMEM)
NEAR = 4
CORES = 2
GRID = ("chip", "core", "far", "near")


def kernel_call(body, name, specs, outs):
    return pl.pallas_call(
        body,
        name=name,
        in_specs=specs,
        out_specs=[VMEM] * len(outs),
        out_shape=[jax.ShapeDtypeStruct(shape, kind) for shape, kind in outs],
        compiler_params=pltpu.CompilerParams(vmem_limit_bytes=40 * 1024 * 1024),
    )


def exchange(blocks, axis):
    return lax.all_to_all(blocks, axis, split_axis=0, concat_axis=0, tiled=True)


def swap_cores(block):
    return lax.ppermute(block, "core", [(0, 1), (1, 0)])


def dot(left, right):
    return jnp.dot(left, right, preferred_element_type=F32)


def dot_t(left, right):
    return lax.dot_general(left, right, (((0,), (0,)), ((), ())), preferred_element_type=F32)


def reduced(received):
    total = received[0].astype(F32)
    for i in range(1, received.shape[0]):
        total = total + received[i].astype(F32)
    return total


def is_member(table, s, tile):
    found = table[s, 0] == tile
    for i in range(1, table.shape[1]):
        found = found | (table[s, i] == tile)
    return found


def masked_link(w, link, widths, s):
    row = lax.broadcasted_iota(jnp.int32, (w, w), 0)
    column = lax.broadcasted_iota(jnp.int32, (w, w), 1)
    value = link[s]
    inside = (row < widths[s]) & (column < widths[2 + s])
    return jnp.where(inside, value, jnp.zeros_like(value))


def mask_body(w, tile, one, two, anc_one, anc_two, widths, lower):
    column = lax.broadcasted_iota(jnp.int32, (one.shape[0], w), 1)
    for k in range(4):
        source, table, s = (one, anc_one, k) if k < 2 else (two, anc_two, k - 2)
        width = jnp.where(is_member(table, s, tile[0]), widths[k], 0)
        value = source[:, s * w : (s + 1) * w]
        lower[:, k * w : (k + 1) * w] = jnp.where(column < width, value, jnp.zeros_like(value))


def copy_body(source, copies):
    value = source[...]
    for i in range(copies.shape[0]):
        copies[i] = value


def product_body(w, core, inverse, mine, other, part):
    near, far, share, _ = part.shape
    half = mine.shape[0]
    left = inverse[:, pl.ds(pl.multiple_of(core[0] * half, half), half)]
    right = inverse[:, pl.ds(pl.multiple_of((1 - core[0]) * half, half), half)]
    for k in range(4):
        span = slice(k * w, (k + 1) * w)
        value = (dot(left, mine[:, span]) + dot(right, other[:, span])).astype(BF16)
        for i in range(near * far):
            part[i % near, i // near, :, span] = value[i * share : (i + 1) * share]


def quad_body(w, core, received, rows, block, mine, other, held):
    far, _, share = block.shape[0], block.shape[1], received.shape[2]
    for f in range(far):
        total = received[0, f].astype(F32)
        for i in range(1, received.shape[0]):
            total = total + received[i, f].astype(F32)
        total = total.astype(BF16)
        held[f * share : (f + 1) * share, :] = total
        for k in range(4):
            block[f, k * share : (k + 1) * share, :] = total[:, k * w : (k + 1) * w]
    for out, sibling in ((mine, core[0]), (other, 1 - core[0])):
        first = pl.ds(pl.multiple_of(sibling * w, w), w)
        second = pl.ds(pl.multiple_of((2 + sibling) * w, w), w)
        out[0] = dot_t(rows[:, first], held[:, first])
        out[1] = dot_t(held[:, first], rows[:, second])
        out[2] = dot_t(rows[:, second], held[:, second])


def core_sum_body(mine, other, sums):
    sums[...] = (mine[...] + other[...]).astype(BF16)


def chip_sum_body(received, copies):
    value = reduced(received)
    for i in range(copies.shape[0]):
        copies[i] = value


def near_sum_body(received, block, packed):
    chunk = received.shape[1]
    value = reduced(received).astype(BF16)
    for i in range(packed.shape[0]):
        packed[i, :chunk, :] = value
        packed[i, chunk:, :] = block[i]


def far_sum_body(received, pivot, copies):
    total = pivot[...].astype(F32)
    for i in range(received.shape[0]):
        total = total + received[i, : pivot.shape[0], :].astype(F32)
    total = total.astype(BF16)
    for i in range(copies.shape[0]):
        copies[i] = total


def column_body(w, chunk, tile, received, link, anc_one, anc_two, widths, column_one, column_two):
    total = received[0, chunk:, :].astype(F32)
    for i in range(1, received.shape[0]):
        total = total + received[i, chunk:, :].astype(F32)
    share = column_one.shape[0]
    for s in range(2):
        span = slice(s * w, (s + 1) * w)
        here_one = jnp.where(is_member(anc_one, s, tile[0]), 1.0, 0.0)
        here_two = jnp.where(is_member(anc_two, s, tile[0]), 1.0, 0.0)
        one = (-(total[s * share : (s + 1) * share] * here_one)).astype(BF16)
        column_one[:, span] = one
        two = total[(2 + s) * share : (3 + s) * share] + dot(one, masked_link(w, link, widths, s))
        column_two[:, span] = (-(two * here_two)).astype(BF16)


def final_body(w, core, mine, other, link, widths, block_one, parent_rows, block_two):
    for total, sibling in ((mine, core[0]), (other, 1 - core[0])):
        tie = masked_link(w, link, widths, sibling)
        block = total[0]
        cross = total[1]
        block_one[sibling] = block
        parent = (cross.astype(F32) - dot(block, tie)).astype(BF16)
        parent_rows[sibling] = parent
        rest = total[2].astype(F32) - dot_t(cross, tie) - dot_t(tie, parent)
        block_two[sibling] = rest.astype(BF16)


def local(
    ancestor_inverse,
    panel_one,
    ancestors_one,
    diag_inverse_one,
    panel_two,
    link_two,
    ancestors_two,
    diag_inverse_two,
    widths,
):
    w = diag_inverse_one.shape[-1]
    chips, far_n = lax.axis_size("chip"), lax.axis_size("far")
    planes = far_n * NEAR
    local_rows = ancestor_inverse.shape[0]
    share = panel_one.shape[0]
    chip = lax.axis_index("chip").astype(jnp.int32)
    core = lax.axis_index("core").astype(jnp.int32)
    tile = (chip * CORES + core).reshape(1)
    core_ref = core.reshape(1)
    whole = (share, 4 * w)

    (lower,) = kernel_call(
        functools.partial(mask_body, w),
        "mask",
        [SMEM, VMEM, VMEM, SMEM, SMEM, SMEM],
        [(whole, BF16)],
    )(tile, panel_one, panel_two, ancestors_one, ancestors_two, widths)

    pairs = []
    for q in range(chips):
        for k in range(CORES):
            for z in range(planes):
                pairs.append(((q * CORES + k) * planes + z, (z * CORES + k) * planes + q))
    moved = lax.ppermute(lower, GRID, pairs)
    rows = lax.all_gather(lower, "far", axis=0, tiled=True)
    (moved,) = kernel_call(copy_body, "copies", [VMEM], [((chips,) + whole, BF16)])(moved)
    mine = exchange(moved, "chip").reshape(chips * share, 4 * w)
    other = swap_cores(mine)

    (part,) = kernel_call(
        functools.partial(product_body, w),
        "product",
        [SMEM] + [VMEM] * 3,
        [((NEAR, far_n) + whole, BF16)],
    )(core_ref, ancestor_inverse, mine, other)
    part = exchange(part, "near")

    block, mine, other = pl.pallas_call(
        functools.partial(quad_body, w),
        name="quad",
        in_specs=[SMEM, VMEM, VMEM],
        out_specs=[VMEM] * 3,
        out_shape=[
            jax.ShapeDtypeStruct((far_n, 4 * share, w), BF16),
            jax.ShapeDtypeStruct((3, w, w), F32),
            jax.ShapeDtypeStruct((3, w, w), F32),
        ],
        scratch_shapes=[pltpu.VMEM((far_n * share, 4 * w), BF16)],
        compiler_params=pltpu.CompilerParams(vmem_limit_bytes=40 * 1024 * 1024),
    )(core_ref, part, rows)
    other = swap_cores(other)
    chunk = 3 * w // chips
    (sums,) = kernel_call(core_sum_body, "core_sum", [VMEM] * 2, [((3, w, w), BF16)])(mine, other)
    sums = exchange(sums.reshape(chips, chunk, w), "chip")
    (sums,) = kernel_call(chip_sum_body, "chip_sum", [VMEM], [((NEAR, chunk, w), F32)])(sums)
    sums = exchange(sums, "near")
    (packed,) = kernel_call(
        near_sum_body, "near_sum", [VMEM] * 2, [((far_n, chunk + 4 * share, w), BF16)]
    )(sums, block)
    packed = exchange(packed, "far")

    keep = (jnp.arange(w, dtype=jnp.int32)[None, :] < widths[:, None]).astype(BF16)
    pivot_one = diag_inverse_one * keep[0:2, :, None] * keep[0:2, None, :]
    pivot_two = diag_inverse_two * keep[2:4, :, None] * keep[2:4, None, :]
    pivots = jnp.stack([pivot_one, jnp.zeros_like(pivot_one), pivot_two], axis=1)
    pivot = lax.dynamic_slice_in_dim(
        pivots.reshape(6 * w, w), core * (3 * w) + chip * chunk, chunk, axis=0
    )
    (total,) = kernel_call(far_sum_body, "far_sum", [VMEM] * 2, [((chips, chunk, w), BF16)])(
        packed, pivot
    )
    mine = exchange(total, "chip").reshape(3, w, w)
    other = swap_cores(mine)
    column_one, column_two = kernel_call(
        functools.partial(column_body, w, chunk),
        "columns",
        [SMEM, VMEM, VMEM, SMEM, SMEM, SMEM],
        [((share, 2 * w), BF16)] * 2,
    )(tile, packed, link_two, ancestors_one, ancestors_two, widths)
    block_one, parent_rows, block_two = kernel_call(
        functools.partial(final_body, w),
        "final",
        [SMEM, VMEM, VMEM, VMEM, SMEM],
        [((2, w, w), BF16)] * 3,
    )(core_ref, mine, other, link_two, widths)
    return column_one, block_one, column_two, parent_rows, block_two


def solution(mesh):
    rows_n, cols_n = mesh.devices.shape
    fine = Mesh(mesh.devices.reshape(rows_n // CORES, CORES, cols_n // NEAR, NEAR), GRID)
    row, col = ("chip", "core"), ("far", "near")
    shared = P(GRID, None)
    in_specs = (P(row, col), shared, P(), P(), shared, P(), P(), P(), P())
    out_specs = (shared, P(), shared, P(), P())
    return jax.shard_map(local, mesh=fine, in_specs=in_specs, out_specs=out_specs, check_vma=False)
```

```python
import functools

import jax
import jax.numpy as jnp
from jax import lax
from jax.experimental import pallas as pl
from jax.experimental.pallas import tpu as pltpu
from jax.sharding import Mesh
from jax.sharding import PartitionSpec as P

F32 = jnp.float32
BF16 = jnp.bfloat16
VMEM = pl.BlockSpec(memory_space=pltpu.VMEM)
SMEM = pl.BlockSpec(memory_space=pltpu.SMEM)
NEAR = 4
CORES = 2
GRID = ("chip", "core", "far", "near")


def kernel_call(body, name, specs, outs):
    return pl.pallas_call(
        body,
        name=name,
        in_specs=specs,
        out_specs=[VMEM] * len(outs),
        out_shape=[jax.ShapeDtypeStruct(shape, kind) for shape, kind in outs],
        compiler_params=pltpu.CompilerParams(vmem_limit_bytes=40 * 1024 * 1024),
    )


def exchange(blocks, axis):
    return lax.all_to_all(blocks, axis, split_axis=0, concat_axis=0, tiled=True)


def swap_cores(block):
    return lax.ppermute(block, "core", [(0, 1), (1, 0)])


def dot(left, right):
    return jnp.dot(left, right, preferred_element_type=F32)


def dot_t(left, right):
    return lax.dot_general(left, right, (((0,), (0,)), ((), ())), preferred_element_type=F32)


def reduced(received):
    total = received[0].astype(F32)
    for i in range(1, received.shape[0]):
        total = total + received[i].astype(F32)
    return total


def is_member(table, s, tile):
    found = table[s, 0] == tile
    for i in range(1, table.shape[1]):
        found = found | (table[s, i] == tile)
    return found


def masked_link(w, link, widths, s):
    row = lax.broadcasted_iota(jnp.int32, (w, w), 0)
    column = lax.broadcasted_iota(jnp.int32, (w, w), 1)
    value = link[s]
    inside = (row < widths[s]) & (column < widths[2 + s])
    return jnp.where(inside, value, jnp.zeros_like(value))


def mask_body(w, tile, one, two, anc_one, anc_two, widths, lower, copies):
    column = lax.broadcasted_iota(jnp.int32, (one.shape[0], w), 1)
    for k in range(4):
        source, table, s = (one, anc_one, k) if k < 2 else (two, anc_two, k - 2)
        width = jnp.where(is_member(table, s, tile[0]), widths[k], 0)
        value = source[:, s * w : (s + 1) * w]
        value = jnp.where(column < width, value, jnp.zeros_like(value))
        lower[:, k * w : (k + 1) * w] = value
        for i in range(copies.shape[0]):
            copies[i, :, k * w : (k + 1) * w] = value


def copy_body(source, copies):
    value = source[...]
    for i in range(copies.shape[0]):
        copies[i] = value


def product_body(w, core, inverse, mine, other, part):
    near, far, share, _ = part.shape
    half = mine.shape[0]
    left = inverse[:, pl.ds(pl.multiple_of(core[0] * half, half), half)]
    right = inverse[:, pl.ds(pl.multiple_of((1 - core[0]) * half, half), half)]
    for k in range(4):
        span = slice(k * w, (k + 1) * w)
        value = (dot(left, mine[:, span]) + dot(right, other[:, span])).astype(BF16)
        for i in range(near * far):
            part[i % near, i // near, :, span] = value[i * share : (i + 1) * share]


def quad_body(w, core, received, rows, block, mine, other, held):
    far, _, share = block.shape[0], block.shape[1], received.shape[2]
    for f in range(far):
        total = received[0, f].astype(F32)
        for i in range(1, received.shape[0]):
            total = total + received[i, f].astype(F32)
        total = total.astype(BF16)
        held[f * share : (f + 1) * share, :] = total
        for k in range(4):
            block[f, k * share : (k + 1) * share, :] = total[:, k * w : (k + 1) * w]
    for out, sibling in ((mine, core[0]), (other, 1 - core[0])):
        first = pl.ds(pl.multiple_of(sibling * w, w), w)
        second = pl.ds(pl.multiple_of((2 + sibling) * w, w), w)
        out[0] = dot_t(rows[:, first], held[:, first])
        out[1] = dot_t(held[:, first], rows[:, second])
        out[2] = dot_t(rows[:, second], held[:, second])


def core_sum_body(mine, other, sums):
    sums[...] = (mine[...] + other[...]).astype(BF16)


def chip_sum_body(received, copies):
    value = reduced(received)
    for i in range(copies.shape[0]):
        copies[i] = value


def near_sum_body(received, block, packed):
    chunk = received.shape[1]
    value = reduced(received).astype(BF16)
    for i in range(packed.shape[0]):
        packed[i, :chunk, :] = value
        packed[i, chunk:, :] = block[i]


def far_sum_body(received, pivot, copies):
    total = pivot[...].astype(F32)
    for i in range(received.shape[0]):
        total = total + received[i, : pivot.shape[0], :].astype(F32)
    total = total.astype(BF16)
    for i in range(copies.shape[0]):
        copies[i] = total


def column_body(w, chunk, tile, received, link, anc_one, anc_two, widths, column_one, column_two):
    total = received[0, chunk:, :].astype(F32)
    for i in range(1, received.shape[0]):
        total = total + received[i, chunk:, :].astype(F32)
    share = column_one.shape[0]
    for s in range(2):
        span = slice(s * w, (s + 1) * w)
        here_one = jnp.where(is_member(anc_one, s, tile[0]), 1.0, 0.0)
        here_two = jnp.where(is_member(anc_two, s, tile[0]), 1.0, 0.0)
        one = (-(total[s * share : (s + 1) * share] * here_one)).astype(BF16)
        column_one[:, span] = one
        two = total[(2 + s) * share : (3 + s) * share] + dot(one, masked_link(w, link, widths, s))
        column_two[:, span] = (-(two * here_two)).astype(BF16)


def final_body(w, core, mine, other, link, widths, block_one, parent_rows, block_two):
    for total, sibling in ((mine, core[0]), (other, 1 - core[0])):
        tie = masked_link(w, link, widths, sibling)
        block = total[0]
        cross = total[1]
        block_one[sibling] = block
        parent = (cross.astype(F32) - dot(block, tie)).astype(BF16)
        parent_rows[sibling] = parent
        rest = total[2].astype(F32) - dot_t(cross, tie) - dot_t(tie, parent)
        block_two[sibling] = rest.astype(BF16)


def local(
    ancestor_inverse,
    panel_one,
    ancestors_one,
    diag_inverse_one,
    panel_two,
    link_two,
    ancestors_two,
    diag_inverse_two,
    widths,
):
    w = diag_inverse_one.shape[-1]
    chips, far_n = lax.axis_size("chip"), lax.axis_size("far")
    planes = far_n * NEAR
    local_rows = ancestor_inverse.shape[0]
    share = panel_one.shape[0]
    chip = lax.axis_index("chip").astype(jnp.int32)
    core = lax.axis_index("core").astype(jnp.int32)
    tile = (chip * CORES + core).reshape(1)
    core_ref = core.reshape(1)
    whole = (share, 4 * w)

    lower, lower_copies = kernel_call(
        functools.partial(mask_body, w),
        "mask",
        [SMEM, VMEM, VMEM, SMEM, SMEM, SMEM],
        [(whole, BF16), ((far_n,) + whole, BF16)],
    )(tile, panel_one, panel_two, ancestors_one, ancestors_two, widths)

    pairs = []
    for q in range(chips):
        for k in range(CORES):
            for z in range(planes):
                pairs.append(((q * CORES + k) * planes + z, (z * CORES + k) * planes + q))
    moved = lax.ppermute(lower, GRID, pairs)
    rows = exchange(lower_copies, "far").reshape(far_n * share, 4 * w)
    moved, rows = lax.optimization_barrier((moved, rows))
    (moved,) = kernel_call(copy_body, "copies", [VMEM], [((chips,) + whole, BF16)])(moved)
    mine = exchange(moved, "chip").reshape(chips * share, 4 * w)
    other = swap_cores(mine)

    (part,) = kernel_call(
        functools.partial(product_body, w),
        "product",
        [SMEM] + [VMEM] * 3,
        [((NEAR, far_n) + whole, BF16)],
    )(core_ref, ancestor_inverse, mine, other)
    part = exchange(part, "near")

    block, mine, other = pl.pallas_call(
        functools.partial(quad_body, w),
        name="quad",
        in_specs=[SMEM, VMEM, VMEM],
        out_specs=[VMEM] * 3,
        out_shape=[
            jax.ShapeDtypeStruct((far_n, 4 * share, w), BF16),
            jax.ShapeDtypeStruct((3, w, w), F32),
            jax.ShapeDtypeStruct((3, w, w), F32),
        ],
        scratch_shapes=[pltpu.VMEM((far_n * share, 4 * w), BF16)],
        compiler_params=pltpu.CompilerParams(vmem_limit_bytes=40 * 1024 * 1024),
    )(core_ref, part, rows)
    other = swap_cores(other)
    chunk = 3 * w // chips
    (sums,) = kernel_call(core_sum_body, "core_sum", [VMEM] * 2, [((3, w, w), BF16)])(mine, other)
    sums = exchange(sums.reshape(chips, chunk, w), "chip")
    (sums,) = kernel_call(chip_sum_body, "chip_sum", [VMEM], [((NEAR, chunk, w), F32)])(sums)
    sums = exchange(sums, "near")
    (packed,) = kernel_call(
        near_sum_body, "near_sum", [VMEM] * 2, [((far_n, chunk + 4 * share, w), BF16)]
    )(sums, block)
    packed = exchange(packed, "far")

    keep = (jnp.arange(w, dtype=jnp.int32)[None, :] < widths[:, None]).astype(BF16)
    pivot_one = diag_inverse_one * keep[0:2, :, None] * keep[0:2, None, :]
    pivot_two = diag_inverse_two * keep[2:4, :, None] * keep[2:4, None, :]
    pivots = jnp.stack([pivot_one, jnp.zeros_like(pivot_one), pivot_two], axis=1)
    pivot = lax.dynamic_slice_in_dim(
        pivots.reshape(6 * w, w), core * (3 * w) + chip * chunk, chunk, axis=0
    )
    (total,) = kernel_call(far_sum_body, "far_sum", [VMEM] * 2, [((chips, chunk, w), BF16)])(
        packed, pivot
    )
    mine = exchange(total, "chip").reshape(3, w, w)
    other = swap_cores(mine)
    column_one, column_two = kernel_call(
        functools.partial(column_body, w, chunk),
        "columns",
        [SMEM, VMEM, VMEM, SMEM, SMEM, SMEM],
        [((share, 2 * w), BF16)] * 2,
    )(tile, packed, link_two, ancestors_one, ancestors_two, widths)
    block_one, parent_rows, block_two = kernel_call(
        functools.partial(final_body, w),
        "final",
        [SMEM, VMEM, VMEM, VMEM, SMEM],
        [((2, w, w), BF16)] * 3,
    )(core_ref, mine, other, link_two, widths)
    return column_one, block_one, column_two, parent_rows, block_two


def solution(mesh):
    rows_n, cols_n = mesh.devices.shape
    fine = Mesh(mesh.devices.reshape(rows_n // CORES, CORES, cols_n // NEAR, NEAR), GRID)
    row, col = ("chip", "core"), ("far", "near")
    shared = P(GRID, None)
    in_specs = (P(row, col), shared, P(), P(), shared, P(), P(), P(), P())
    out_specs = (shared, P(), shared, P(), P())
    return jax.shard_map(local, mesh=fine, in_specs=in_specs, out_specs=out_specs, check_vma=False)
```

```python
import functools

import jax
import jax.numpy as jnp
from jax import lax
from jax.experimental import pallas as pl
from jax.experimental.pallas import tpu as pltpu
from jax.sharding import Mesh
from jax.sharding import PartitionSpec as P

F32 = jnp.float32
BF16 = jnp.bfloat16
VMEM = pl.BlockSpec(memory_space=pltpu.VMEM)
SMEM = pl.BlockSpec(memory_space=pltpu.SMEM)
NEAR = 4
CORES = 2
LANES = 128
GRID = ("chip", "core", "far", "near")


def kernel_call(body, name, specs, outs):
    return pl.pallas_call(
        body,
        name=name,
        in_specs=specs,
        out_specs=[VMEM] * len(outs),
        out_shape=[jax.ShapeDtypeStruct(shape, kind) for shape, kind in outs],
        compiler_params=pltpu.CompilerParams(vmem_limit_bytes=40 * 1024 * 1024),
    )


def exchange(blocks, axis):
    return lax.all_to_all(blocks, axis, split_axis=0, concat_axis=0, tiled=True)


def swap_cores(block):
    return lax.ppermute(block, "core", [(0, 1), (1, 0)])


def swap_far(block, m):
    return lax.ppermute(block, "far", [(i, i ^ m) for i in range(lax.axis_size("far"))])


def dot(left, right):
    return jnp.dot(left, right, preferred_element_type=F32)


def dot_t(left, right):
    return lax.dot_general(left, right, (((0,), (0,)), ((), ())), preferred_element_type=F32)


def reduced(received):
    total = received[0].astype(F32)
    for i in range(1, received.shape[0]):
        total = total + received[i].astype(F32)
    return total


def is_member(table, s, tile):
    found = table[s, 0] == tile
    for i in range(1, table.shape[1]):
        found = found | (table[s, i] == tile)
    return found


def masked_link(w, link, widths, s):
    row = lax.broadcasted_iota(jnp.int32, (w, w), 0)
    column = lax.broadcasted_iota(jnp.int32, (w, w), 1)
    value = link[s]
    inside = (row < widths[s]) & (column < widths[2 + s])
    return jnp.where(inside, value, jnp.zeros_like(value))


def mask_body(w, tile, one, two, anc_one, anc_two, widths, lower):
    column = lax.broadcasted_iota(jnp.int32, (one.shape[0], w), 1)
    for k in range(4):
        source, table, s = (one, anc_one, k) if k < 2 else (two, anc_two, k - 2)
        width = jnp.where(is_member(table, s, tile[0]), widths[k], 0)
        value = source[:, s * w : (s + 1) * w]
        lower[:, k * w : (k + 1) * w] = jnp.where(column < width, value, jnp.zeros_like(value))


def copy_body(source, copies):
    value = source[...]
    for i in range(copies.shape[0]):
        copies[i] = value


def product_body(w, core, inverse, mine, other, part):
    near, far, share, _ = part.shape
    half = mine.shape[0]
    left = inverse[:, pl.ds(pl.multiple_of(core[0] * half, half), half)]
    right = inverse[:, pl.ds(pl.multiple_of((1 - core[0]) * half, half), half)]
    for k in range(4):
        span = slice(k * w, (k + 1) * w)
        value = (dot(left, mine[:, span]) + dot(right, other[:, span])).astype(BF16)
        for i in range(near * far):
            part[i % near, i // near, :, span] = value[i * share : (i + 1) * share]


def quad_body(w, place, received, *refs):
    far, share = received.shape[1], received.shape[2]
    lowers, parts, (mine, other, rows, held) = refs[:far], refs[far : 2 * far], refs[2 * far :]
    for m in range(far):
        block = place[1] ^ m
        total = received[0, block].astype(F32)
        for i in range(1, received.shape[0]):
            total = total + received[i, block].astype(F32)
        total = total.astype(BF16)
        parts[m][...] = total
        held[m * share : (m + 1) * share, :] = total
        rows[m * share : (m + 1) * share, :] = lowers[m][...]
    for out, sibling in ((mine, place[0]), (other, 1 - place[0])):
        first = pl.ds(pl.multiple_of(sibling * w, w), w)
        second = pl.ds(pl.multiple_of((2 + sibling) * w, w), w)
        out[0] = dot_t(rows[:, first], held[:, first])
        out[1] = dot_t(held[:, first], rows[:, second])
        out[2] = dot_t(rows[:, second], held[:, second])


def core_sum_body(w, mine, other, sums):
    lanes = sums.shape[2]
    for b in range(3):
        value = (mine[b] + other[b]).astype(BF16)
        for h in range(w // lanes):
            sums[h, b * w : (b + 1) * w, :] = value[:, h * lanes : (h + 1) * lanes]


def chunk_sum_body(received, copies):
    value = reduced(received)
    for i in range(copies.shape[0]):
        copies[i] = value


def pivot_body(w, place, one, two, widths, pivot, stack):
    row = lax.broadcasted_iota(jnp.int32, (w, w), 0)
    column = lax.broadcasted_iota(jnp.int32, (w, w), 1)
    lanes = stack.shape[1]
    for b, source, width in (
        (0, one, widths[place[0]]),
        (1, None, 0),
        (2, two, widths[2 + place[0]]),
    ):
        value = jnp.zeros((w, w), F32)
        if source is not None:
            value = jnp.where((row < width) & (column < width), source[place[0]].astype(F32), value)
        for h in range(w // lanes):
            start = (3 * h + b) * w
            stack[start : start + w, :] = value[:, h * lanes : (h + 1) * lanes]
    size = pivot.shape[0]
    pivot[...] = stack[pl.ds(pl.multiple_of(place[2] * size, size), size), :]


def all_sum_body(received, pivot, copies):
    near, chunk = NEAR, received.shape[1]
    for n in range(near):
        total = pivot[n * chunk : (n + 1) * chunk, :]
        for i in range(n, received.shape[0], near):
            total = total + received[i]
        total = total.astype(BF16)
        for i in range(copies.shape[0]):
            copies[i, n * chunk : (n + 1) * chunk, :] = total


def column_body(w, tile, *refs):
    parts, (link, anc_one, anc_two, widths, column_one, column_two) = refs[:-6], refs[-6:]
    total = parts[0][...].astype(F32)
    for part in parts[1:]:
        total = total + part[...].astype(F32)
    for s in range(2):
        span = slice(s * w, (s + 1) * w)
        here_one = jnp.where(is_member(anc_one, s, tile[0]), 1.0, 0.0)
        here_two = jnp.where(is_member(anc_two, s, tile[0]), 1.0, 0.0)
        one = (-(total[:, span] * here_one)).astype(BF16)
        column_one[:, span] = one
        two = total[:, (2 + s) * w : (3 + s) * w] + dot(one, masked_link(w, link, widths, s))
        column_two[:, span] = (-(two * here_two)).astype(BF16)


def side_by_side(total, b, w):
    span = slice(b * w, (b + 1) * w)
    return jnp.concatenate([total[h, span, :] for h in range(total.shape[0])], axis=1)


def final_body(w, core, mine, other, link, widths, block_one, parent_rows, block_two):
    for total, sibling in ((mine, core[0]), (other, 1 - core[0])):
        tie = masked_link(w, link, widths, sibling)
        block = side_by_side(total, 0, w)
        cross = side_by_side(total, 1, w)
        block_one[sibling] = block
        parent = (cross.astype(F32) - dot(block, tie)).astype(BF16)
        parent_rows[sibling] = parent
        rest = side_by_side(total, 2, w).astype(F32) - dot_t(cross, tie) - dot_t(tie, parent)
        block_two[sibling] = rest.astype(BF16)


def local(
    ancestor_inverse,
    panel_one,
    ancestors_one,
    diag_inverse_one,
    panel_two,
    link_two,
    ancestors_two,
    diag_inverse_two,
    widths,
):
    w = diag_inverse_one.shape[-1]
    chips, far_n = lax.axis_size("chip"), lax.axis_size("far")
    planes = far_n * NEAR
    local_rows = ancestor_inverse.shape[0]
    share = panel_one.shape[0]
    chip = lax.axis_index("chip").astype(jnp.int32)
    core = lax.axis_index("core").astype(jnp.int32)
    tile = (chip * CORES + core).reshape(1)
    core_ref = core.reshape(1)
    whole = (share, 4 * w)

    (lower,) = kernel_call(
        functools.partial(mask_body, w),
        "mask",
        [SMEM, VMEM, VMEM, SMEM, SMEM, SMEM],
        [(whole, BF16)],
    )(tile, panel_one, panel_two, ancestors_one, ancestors_two, widths)

    pairs = []
    for q in range(chips):
        for k in range(CORES):
            for z in range(planes):
                pairs.append(((q * CORES + k) * planes + z, (z * CORES + k) * planes + q))
    moved = lax.ppermute(lower, GRID, pairs)
    lowers = [lower] + [swap_far(lower, m) for m in range(1, far_n)]
    (moved,) = kernel_call(copy_body, "copies", [VMEM], [((chips,) + whole, BF16)])(moved)
    mine, *lowers[:-1] = lax.optimization_barrier((exchange(moved, "chip"), *lowers[:-1]))
    mine = mine.reshape(chips * share, 4 * w)
    other = swap_cores(mine)

    (part,) = kernel_call(
        functools.partial(product_body, w),
        "product",
        [SMEM] + [VMEM] * 3,
        [((NEAR, far_n) + whole, BF16)],
    )(core_ref, ancestor_inverse, mine, other)
    part = exchange(part, "near")

    place = jnp.stack([core, lax.axis_index("far").astype(jnp.int32), chip])
    *parts, mine, other = pl.pallas_call(
        functools.partial(quad_body, w),
        name="quad",
        in_specs=[SMEM] + [VMEM] * (1 + far_n),
        out_specs=[VMEM] * (far_n + 2),
        out_shape=[jax.ShapeDtypeStruct(whole, BF16)] * far_n
        + [jax.ShapeDtypeStruct((3, w, w), F32)] * 2,
        scratch_shapes=[pltpu.VMEM((far_n * share, 4 * w), BF16)] * 2,
        compiler_params=pltpu.CompilerParams(vmem_limit_bytes=40 * 1024 * 1024),
    )(place, part, *lowers)
    parts = parts[:1] + [swap_far(parts[m], m) for m in range(1, far_n)]
    other = swap_cores(other)
    flat = (w // LANES, 3 * w, LANES)
    chunk = 3 * w * w // LANES // (chips * NEAR)
    (sums,) = kernel_call(
        functools.partial(core_sum_body, w), "core_sum", [VMEM] * 2, [(flat, BF16)]
    )(mine, other)
    sums = exchange(sums.reshape(chips * NEAR, chunk, LANES), ("chip", "near"))
    sums, *parts[:-1] = lax.optimization_barrier((sums, *parts[:-1]))
    (sums,) = kernel_call(chunk_sum_body, "chunk_sum", [VMEM], [((planes, chunk, LANES), F32)])(
        sums
    )
    sums, parts[-1] = lax.optimization_barrier((exchange(sums, ("far", "near")), parts[-1]))
    pivot = pl.pallas_call(
        functools.partial(pivot_body, w),
        name="pivot",
        in_specs=[SMEM, VMEM, VMEM, SMEM],
        out_specs=VMEM,
        out_shape=jax.ShapeDtypeStruct((NEAR * chunk, LANES), F32),
        scratch_shapes=[pltpu.VMEM((3 * w * w // LANES, LANES), F32)],
    )(place, diag_inverse_one, diag_inverse_two, widths)
    (total,) = kernel_call(
        all_sum_body, "all_sum", [VMEM] * 2, [((chips, NEAR * chunk, LANES), BF16)]
    )(sums, pivot)
    mine = exchange(total, "chip").reshape(flat)
    other = swap_cores(mine)
    column_one, column_two = kernel_call(
        functools.partial(column_body, w),
        "columns",
        [SMEM] + [VMEM] * (far_n + 1) + [SMEM] * 3,
        [((share, 2 * w), BF16)] * 2,
    )(tile, *parts, link_two, ancestors_one, ancestors_two, widths)
    block_one, parent_rows, block_two = kernel_call(
        functools.partial(final_body, w),
        "final",
        [SMEM, VMEM, VMEM, VMEM, SMEM],
        [((2, w, w), BF16)] * 3,
    )(core_ref, mine, other, link_two, widths)
    return column_one, block_one, column_two, parent_rows, block_two


def solution(mesh):
    rows_n, cols_n = mesh.devices.shape
    fine = Mesh(mesh.devices.reshape(rows_n // CORES, CORES, cols_n // NEAR, NEAR), GRID)
    row, col = ("chip", "core"), ("far", "near")
    shared = P(GRID, None)
    in_specs = (P(row, col), shared, P(), P(), shared, P(), P(), P(), P())
    out_specs = (shared, P(), shared, P(), P())
    return jax.shard_map(local, mesh=fine, in_specs=in_specs, out_specs=out_specs, check_vma=False)
```

```python
import functools

import jax
import jax.numpy as jnp
from jax import lax
from jax.experimental import pallas as pl
from jax.experimental.pallas import tpu as pltpu
from jax.sharding import Mesh
from jax.sharding import PartitionSpec as P

F32 = jnp.float32
BF16 = jnp.bfloat16
VMEM = pl.BlockSpec(memory_space=pltpu.VMEM)
SMEM = pl.BlockSpec(memory_space=pltpu.SMEM)
NEAR = 4
CORES = 2
LANES = 128
GRID = ("chip", "core", "far", "near")


def kernel_call(body, name, specs, outs):
    return pl.pallas_call(
        body,
        name=name,
        in_specs=specs,
        out_specs=[VMEM] * len(outs),
        out_shape=[jax.ShapeDtypeStruct(shape, kind) for shape, kind in outs],
        compiler_params=pltpu.CompilerParams(vmem_limit_bytes=40 * 1024 * 1024),
    )


def exchange(blocks, axis):
    return lax.all_to_all(blocks, axis, split_axis=0, concat_axis=0, tiled=True)


def swap_cores(block):
    return lax.ppermute(block, "core", [(0, 1), (1, 0)])


def dot(left, right):
    return jnp.dot(left, right, preferred_element_type=F32)


def dot_t(left, right):
    return lax.dot_general(left, right, (((0,), (0,)), ((), ())), preferred_element_type=F32)


def reduced(received):
    total = received[0].astype(F32)
    for i in range(1, received.shape[0]):
        total = total + received[i].astype(F32)
    return total


def is_member(table, s, tile):
    found = table[s, 0] == tile
    for i in range(1, table.shape[1]):
        found = found | (table[s, i] == tile)
    return found


def masked_link(w, link, widths, s):
    row = lax.broadcasted_iota(jnp.int32, (w, w), 0)
    column = lax.broadcasted_iota(jnp.int32, (w, w), 1)
    value = link[s]
    inside = (row < widths[s]) & (column < widths[2 + s])
    return jnp.where(inside, value, jnp.zeros_like(value))


def mask_body(w, tile, one, two, anc_one, anc_two, widths, lower):
    column = lax.broadcasted_iota(jnp.int32, (one.shape[0], w), 1)
    for k in range(4):
        source, table, s = (one, anc_one, k) if k < 2 else (two, anc_two, k - 2)
        width = jnp.where(is_member(table, s, tile[0]), widths[k], 0)
        value = source[:, s * w : (s + 1) * w]
        lower[:, k * w : (k + 1) * w] = jnp.where(column < width, value, jnp.zeros_like(value))


def copy_body(source, copies):
    value = source[...]
    for i in range(copies.shape[0]):
        copies[i] = value


def product_body(w, core, inverse, mine, other, part):
    near, far, share, _ = part.shape
    half = mine.shape[0]
    left = inverse[:, pl.ds(pl.multiple_of(core[0] * half, half), half)]
    right = inverse[:, pl.ds(pl.multiple_of((1 - core[0]) * half, half), half)]
    for k in range(4):
        span = slice(k * w, (k + 1) * w)
        value = (dot(left, mine[:, span]) + dot(right, other[:, span])).astype(BF16)
        for i in range(near * far):
            part[i % near, i // near, :, span] = value[i * share : (i + 1) * share]


def near_sum_body(received, sums):
    for f in range(sums.shape[0]):
        total = received[0, f].astype(F32)
        for i in range(1, received.shape[0]):
            total = total + received[i, f].astype(F32)
        sums[f] = total.astype(BF16)


def column_body(
    w, tile, place, received, lower, link, anc_one, anc_two, widths, column_one, column_two, mine, other
):
    total = reduced(received)
    for s in range(2):
        span = slice(s * w, (s + 1) * w)
        here_one = jnp.where(is_member(anc_one, s, tile[0]), 1.0, 0.0)
        here_two = jnp.where(is_member(anc_two, s, tile[0]), 1.0, 0.0)
        one = (-(total[:, span] * here_one)).astype(BF16)
        column_one[:, span] = one
        two = total[:, (2 + s) * w : (3 + s) * w] + dot(one, masked_link(w, link, widths, s))
        column_two[:, span] = (-(two * here_two)).astype(BF16)
    for out, sibling in ((mine, place[0]), (other, 1 - place[0])):
        first = pl.ds(pl.multiple_of(sibling * w, w), w)
        second = pl.ds(pl.multiple_of((2 + sibling) * w, w), w)
        out[0] = -dot_t(lower[:, first], column_one[:, first])
        out[1] = dot_t(column_one[:, first], lower[:, second])
        out[2] = -dot_t(lower[:, second], column_two[:, first])


def core_sum_body(w, mine, other, sums):
    lanes = sums.shape[2]
    for b in range(3):
        value = (mine[b] + other[b]).astype(BF16)
        for h in range(w // lanes):
            sums[h, b * w : (b + 1) * w, :] = value[:, h * lanes : (h + 1) * lanes]


def chunk_sum_body(received, copies):
    value = reduced(received)
    for i in range(copies.shape[0]):
        copies[i] = value


def pivot_body(w, place, one, two, widths, pivot, stack):
    row = lax.broadcasted_iota(jnp.int32, (w, w), 0)
    column = lax.broadcasted_iota(jnp.int32, (w, w), 1)
    lanes = stack.shape[1]
    for b, source, width in (
        (0, one, widths[place[0]]),
        (1, None, 0),
        (2, two, widths[2 + place[0]]),
    ):
        value = jnp.zeros((w, w), F32)
        if source is not None:
            value = jnp.where((row < width) & (column < width), source[place[0]].astype(F32), value)
        for h in range(w // lanes):
            start = (3 * h + b) * w
            stack[start : start + w, :] = value[:, h * lanes : (h + 1) * lanes]
    size = pivot.shape[0]
    pivot[...] = stack[pl.ds(pl.multiple_of(place[1] * size, size), size), :]


def all_sum_body(received, pivot, copies):
    near, chunk = NEAR, received.shape[1]
    for n in range(near):
        total = pivot[n * chunk : (n + 1) * chunk, :]
        for i in range(n, received.shape[0], near):
            total = total + received[i]
        total = total.astype(BF16)
        for i in range(copies.shape[0]):
            copies[i, n * chunk : (n + 1) * chunk, :] = total


def side_by_side(total, b, w):
    span = slice(b * w, (b + 1) * w)
    return jnp.concatenate([total[h, span, :] for h in range(total.shape[0])], axis=1)


def final_body(w, core, mine, other, link, widths, block_one, parent_rows, block_two):
    for total, sibling in ((mine, core[0]), (other, 1 - core[0])):
        tie = masked_link(w, link, widths, sibling)
        block = side_by_side(total, 0, w)
        cross = side_by_side(total, 1, w).astype(F32)
        block_one[sibling] = block
        parent = (-(dot(block, tie) + cross)).astype(BF16)
        parent_rows[sibling] = parent
        rest = side_by_side(total, 2, w).astype(F32) - dot_t(tie, parent)
        block_two[sibling] = rest.astype(BF16)


def local(
    ancestor_inverse,
    panel_one,
    ancestors_one,
    diag_inverse_one,
    panel_two,
    link_two,
    ancestors_two,
    diag_inverse_two,
    widths,
):
    w = diag_inverse_one.shape[-1]
    chips, far_n = lax.axis_size("chip"), lax.axis_size("far")
    planes = far_n * NEAR
    local_rows = ancestor_inverse.shape[0]
    share = panel_one.shape[0]
    chip = lax.axis_index("chip").astype(jnp.int32)
    core = lax.axis_index("core").astype(jnp.int32)
    tile = (chip * CORES + core).reshape(1)
    core_ref = core.reshape(1)
    whole = (share, 4 * w)

    (lower,) = kernel_call(
        functools.partial(mask_body, w),
        "mask",
        [SMEM, VMEM, VMEM, SMEM, SMEM, SMEM],
        [(whole, BF16)],
    )(tile, panel_one, panel_two, ancestors_one, ancestors_two, widths)

    pairs = []
    for q in range(chips):
        for k in range(CORES):
            for z in range(planes):
                pairs.append(((q * CORES + k) * planes + z, (z * CORES + k) * planes + q))
    moved = lax.ppermute(lower, GRID, pairs)
    (moved,) = kernel_call(copy_body, "copies", [VMEM], [((chips,) + whole, BF16)])(moved)
    mine = exchange(moved, "chip").reshape(chips * share, 4 * w)
    other = swap_cores(mine)

    (part,) = kernel_call(
        functools.partial(product_body, w),
        "product",
        [SMEM] + [VMEM] * 3,
        [((NEAR, far_n) + whole, BF16)],
    )(core_ref, ancestor_inverse, mine, other)
    part = exchange(part, "near")

    (part,) = kernel_call(near_sum_body, "near_sum", [VMEM], [((far_n,) + whole, BF16)])(part)
    part = exchange(part, "far")
    place = jnp.stack([core, chip])
    column_one, column_two, mine, other = kernel_call(
        functools.partial(column_body, w),
        "columns",
        [SMEM, SMEM, VMEM, VMEM, VMEM, SMEM, SMEM, SMEM],
        [((share, 2 * w), BF16)] * 2 + [((3, w, w), F32)] * 2,
    )(tile, place, part, lower, link_two, ancestors_one, ancestors_two, widths)
    other = swap_cores(other)
    flat = (w // LANES, 3 * w, LANES)
    chunk = 3 * w * w // LANES // (chips * NEAR)
    (sums,) = kernel_call(
        functools.partial(core_sum_body, w), "core_sum", [VMEM] * 2, [(flat, BF16)]
    )(mine, other)
    sums = exchange(sums.reshape(chips * NEAR, chunk, LANES), ("chip", "near"))
    (sums,) = kernel_call(chunk_sum_body, "chunk_sum", [VMEM], [((planes, chunk, LANES), F32)])(
        sums
    )
    pivot = pl.pallas_call(
        functools.partial(pivot_body, w),
        name="pivot",
        in_specs=[SMEM, VMEM, VMEM, SMEM],
        out_specs=VMEM,
        out_shape=jax.ShapeDtypeStruct((NEAR * chunk, LANES), F32),
        scratch_shapes=[pltpu.VMEM((3 * w * w // LANES, LANES), F32)],
    )(place, diag_inverse_one, diag_inverse_two, widths)
    sums, pivot = lax.optimization_barrier((sums, pivot))
    sums = exchange(sums, ("far", "near"))
    (total,) = kernel_call(
        all_sum_body, "all_sum", [VMEM] * 2, [((chips, NEAR * chunk, LANES), BF16)]
    )(sums, pivot)
    mine = exchange(total, "chip").reshape(flat)
    other = swap_cores(mine)
    block_one, parent_rows, block_two = kernel_call(
        functools.partial(final_body, w),
        "final",
        [SMEM, VMEM, VMEM, VMEM, SMEM],
        [((2, w, w), BF16)] * 3,
    )(core_ref, mine, other, link_two, widths)
    return column_one, block_one, column_two, parent_rows, block_two


def solution(mesh):
    rows_n, cols_n = mesh.devices.shape
    fine = Mesh(mesh.devices.reshape(rows_n // CORES, CORES, cols_n // NEAR, NEAR), GRID)
    row, col = ("chip", "core"), ("far", "near")
    shared = P(GRID, None)
    in_specs = (P(row, col), shared, P(), P(), shared, P(), P(), P(), P())
    out_specs = (shared, P(), shared, P(), P())
    return jax.shard_map(local, mesh=fine, in_specs=in_specs, out_specs=out_specs, check_vma=False)
```

```python
import functools

import jax
import jax.numpy as jnp
from jax import lax
from jax.experimental import pallas as pl
from jax.experimental.pallas import tpu as pltpu
from jax.sharding import Mesh
from jax.sharding import PartitionSpec as P

F32 = jnp.float32
BF16 = jnp.bfloat16
VMEM = pl.BlockSpec(memory_space=pltpu.VMEM)
ANY = pl.BlockSpec(memory_space=pl.ANY)
SMEM = pl.BlockSpec(memory_space=pltpu.SMEM)
NEAR = 4
CORES = 2
LANES = 128
GRID = ("chip", "core", "far", "near")


def kernel_call(body, name, specs, outs):
    return pl.pallas_call(
        body,
        name=name,
        in_specs=specs,
        out_specs=[VMEM] * len(outs),
        out_shape=[jax.ShapeDtypeStruct(shape, kind) for shape, kind in outs],
        compiler_params=pltpu.CompilerParams(vmem_limit_bytes=40 * 1024 * 1024),
    )


def exchange(blocks, axis):
    return lax.all_to_all(blocks, axis, split_axis=0, concat_axis=0, tiled=True)


def landing_places(chips, planes):
    side = int(chips**0.5)

    def steps(a, b):
        return abs(a // side - b // side) + abs(a % side - b % side)

    places = []
    for q in range(chips):
        far_first = sorted(range(planes), key=lambda z: (-abs(z - q), z))
        close_first = sorted(range(chips), key=lambda p: (steps(p, q), p))
        spots = dict(zip(far_first, close_first))
        places.append([spots[z] for z in range(planes)])
    return places


def swap_cores(block):
    return lax.ppermute(block, "core", [(0, 1), (1, 0)])


def dot(left, right):
    return jnp.dot(left, right, preferred_element_type=F32)


def dot_t(left, right):
    return lax.dot_general(left, right, (((0,), (0,)), ((), ())), preferred_element_type=F32)


def reduced(received):
    total = received[0].astype(F32)
    for i in range(1, received.shape[0]):
        total = total + received[i].astype(F32)
    return total


def is_member(table, s, tile):
    found = table[s, 0] == tile
    for i in range(1, table.shape[1]):
        found = found | (table[s, i] == tile)
    return found


def masked_link(w, link, widths, s):
    row = lax.broadcasted_iota(jnp.int32, (w, w), 0)
    column = lax.broadcasted_iota(jnp.int32, (w, w), 1)
    value = link[s]
    inside = (row < widths[s]) & (column < widths[2 + s])
    return jnp.where(inside, value, jnp.zeros_like(value))


def mask_body(w, tile, one, two, anc_one, anc_two, widths, lower, held_one, held_two, sems):
    copies = [
        pltpu.make_async_copy(one, held_one, sems.at[0]),
        pltpu.make_async_copy(two, held_two, sems.at[1]),
    ]
    for copy in copies:
        copy.start()
    column = lax.broadcasted_iota(jnp.int32, (one.shape[0], w), 1)
    limits = [
        jnp.where(is_member(anc_one if k < 2 else anc_two, k % 2, tile[0]), widths[k], 0)
        for k in range(4)
    ]
    for copy in copies:
        copy.wait()
    for k in range(4):
        value = (held_one if k < 2 else held_two)[:, (k % 2) * w : (k % 2 + 1) * w]
        value = jnp.where(column < limits[k], value, jnp.zeros_like(value))
        lower[:, k * w : (k + 1) * w] = value


def copy_body(source, copies):
    value = source[...]
    for i in range(copies.shape[0]):
        copies[i] = value


def product_body(w, core, order, inverse, mine, other, part, held):
    blocks, share, _ = mine.shape
    half = blocks * share
    for i in range(blocks):
        held[i * share : (i + 1) * share, :] = mine[order[i]]
        held[half + i * share : half + (i + 1) * share, :] = other[order[i]]
    left = inverse[:, pl.ds(pl.multiple_of(core[0] * half, half), half)]
    right = inverse[:, pl.ds(pl.multiple_of((1 - core[0]) * half, half), half)]
    for k in range(4):
        span = slice(k * w, (k + 1) * w)
        value = (dot(left, held[:half, span]) + dot(right, held[half:, span])).astype(BF16)
        for i in range(part.shape[0]):
            part[i, :, span] = value[i * share : (i + 1) * share]


def column_body(
    w, tile, place, received, lower, link, anc_one, anc_two, widths, column_one, column_two, mine, other
):
    total = reduced(received)
    for s in range(2):
        span = slice(s * w, (s + 1) * w)
        here_one = jnp.where(is_member(anc_one, s, tile[0]), 1.0, 0.0)
        here_two = jnp.where(is_member(anc_two, s, tile[0]), 1.0, 0.0)
        one = (-(total[:, span] * here_one)).astype(BF16)
        column_one[:, span] = one
        two = total[:, (2 + s) * w : (3 + s) * w] + dot(one, masked_link(w, link, widths, s))
        column_two[:, span] = (-(two * here_two)).astype(BF16)
    for out, sibling in ((mine, place[0]), (other, 1 - place[0])):
        first = pl.ds(pl.multiple_of(sibling * w, w), w)
        second = pl.ds(pl.multiple_of((2 + sibling) * w, w), w)
        out[0] = -dot_t(lower[:, first], column_one[:, first])
        out[1] = dot_t(column_one[:, first], lower[:, second])
        out[2] = -dot_t(lower[:, second], column_two[:, first])


def core_sum_body(w, mine, other, sums):
    lanes = sums.shape[2]
    for b in range(3):
        value = (mine[b] + other[b]).astype(BF16)
        for h in range(w // lanes):
            sums[h, b * w : (b + 1) * w, :] = value[:, h * lanes : (h + 1) * lanes]


def chunk_sum_body(received, copies):
    value = reduced(received).astype(BF16)
    for i in range(copies.shape[0]):
        copies[i] = value


def pivot_body(w, place, one, two, widths, pivot, stack):
    row = lax.broadcasted_iota(jnp.int32, (w, w), 0)
    column = lax.broadcasted_iota(jnp.int32, (w, w), 1)
    lanes = stack.shape[1]
    for b, source, width in (
        (0, one, widths[place[0]]),
        (1, None, 0),
        (2, two, widths[2 + place[0]]),
    ):
        value = jnp.zeros((w, w), F32)
        if source is not None:
            value = jnp.where((row < width) & (column < width), source[place[0]].astype(F32), value)
        for h in range(w // lanes):
            start = (3 * h + b) * w
            stack[start : start + w, :] = value[:, h * lanes : (h + 1) * lanes]
    size = pivot.shape[0]
    pivot[...] = stack[pl.ds(pl.multiple_of(place[1] * size, size), size), :]


def all_sum_body(received, pivot, copies):
    near, chunk = NEAR, received.shape[1]
    for n in range(near):
        total = pivot[n * chunk : (n + 1) * chunk, :]
        for i in range(n, received.shape[0], near):
            total = total + received[i].astype(F32)
        total = total.astype(BF16)
        for i in range(copies.shape[0]):
            copies[i, n * chunk : (n + 1) * chunk, :] = total


def side_by_side(total, b, w):
    span = slice(b * w, (b + 1) * w)
    return jnp.concatenate([total[h, span, :] for h in range(total.shape[0])], axis=1)


def final_body(w, core, mine, other, link, widths, block_one, parent_rows, block_two):
    for total, sibling in ((mine, core[0]), (other, 1 - core[0])):
        tie = masked_link(w, link, widths, sibling)
        block = side_by_side(total, 0, w)
        cross = side_by_side(total, 1, w).astype(F32)
        block_one[sibling] = block
        parent = (-(dot(block, tie) + cross)).astype(BF16)
        parent_rows[sibling] = parent
        rest = side_by_side(total, 2, w).astype(F32) - dot_t(tie, parent)
        block_two[sibling] = rest.astype(BF16)


def local(
    ancestor_inverse,
    panel_one,
    ancestors_one,
    diag_inverse_one,
    panel_two,
    link_two,
    ancestors_two,
    diag_inverse_two,
    widths,
):
    w = diag_inverse_one.shape[-1]
    chips, far_n = lax.axis_size("chip"), lax.axis_size("far")
    planes = far_n * NEAR
    local_rows = ancestor_inverse.shape[0]
    share = panel_one.shape[0]
    chip = lax.axis_index("chip").astype(jnp.int32)
    core = lax.axis_index("core").astype(jnp.int32)
    tile = (chip * CORES + core).reshape(1)
    core_ref = core.reshape(1)
    whole = (share, 4 * w)

    lower = pl.pallas_call(
        functools.partial(mask_body, w),
        name="mask",
        in_specs=[SMEM, ANY, ANY, SMEM, SMEM, SMEM],
        out_specs=VMEM,
        out_shape=jax.ShapeDtypeStruct(whole, BF16),
        scratch_shapes=[pltpu.VMEM(panel_one.shape, BF16)] * 2 + [pltpu.SemaphoreType.DMA((2,))],
    )(tile, panel_one, panel_two, ancestors_one, ancestors_two, widths)

    places = landing_places(chips, planes)
    pairs = []
    for q in range(chips):
        for k in range(CORES):
            for z in range(planes):
                pairs.append(((q * CORES + k) * planes + z, (places[q][z] * CORES + k) * planes + q))
    moved = lax.ppermute(lower, GRID, pairs)
    plane = lax.axis_index("far") * NEAR + lax.axis_index("near")
    order = lax.dynamic_index_in_dim(jnp.array(places, jnp.int32), plane, 0, keepdims=False)
    (moved,) = kernel_call(copy_body, "copies", [VMEM], [((chips,) + whole, BF16)])(moved)
    mine = exchange(moved, "chip")
    other = swap_cores(mine)

    part = pl.pallas_call(
        functools.partial(product_body, w),
        name="product",
        in_specs=[SMEM, SMEM] + [VMEM] * 3,
        out_specs=VMEM,
        out_shape=jax.ShapeDtypeStruct((planes,) + whole, BF16),
        scratch_shapes=[pltpu.VMEM((CORES * chips * share, 4 * w), BF16)],
        compiler_params=pltpu.CompilerParams(vmem_limit_bytes=40 * 1024 * 1024),
    )(core_ref, order, ancestor_inverse, mine, other)
    part = exchange(part, ("far", "near"))
    place = jnp.stack([core, chip])
    column_one, column_two, mine, other = kernel_call(
        functools.partial(column_body, w),
        "columns",
        [SMEM, SMEM, VMEM, VMEM, VMEM, SMEM, SMEM, SMEM],
        [((share, 2 * w), BF16)] * 2 + [((3, w, w), F32)] * 2,
    )(tile, place, part, lower, link_two, ancestors_one, ancestors_two, widths)
    other = swap_cores(other)
    flat = (w // LANES, 3 * w, LANES)
    chunk = 3 * w * w // LANES // (chips * NEAR)
    (sums,) = kernel_call(
        functools.partial(core_sum_body, w), "core_sum", [VMEM] * 2, [(flat, BF16)]
    )(mine, other)
    sums = exchange(sums.reshape(chips * NEAR, chunk, LANES), ("chip", "near"))
    (sums,) = kernel_call(chunk_sum_body, "chunk_sum", [VMEM], [((planes, chunk, LANES), BF16)])(
        sums
    )
    pivot = pl.pallas_call(
        functools.partial(pivot_body, w),
        name="pivot",
        in_specs=[SMEM, VMEM, VMEM, SMEM],
        out_specs=VMEM,
        out_shape=jax.ShapeDtypeStruct((NEAR * chunk, LANES), F32),
        scratch_shapes=[pltpu.VMEM((3 * w * w // LANES, LANES), F32)],
    )(place, diag_inverse_one, diag_inverse_two, widths)
    sums, pivot = lax.optimization_barrier((sums, pivot))
    sums = exchange(sums, ("far", "near"))
    (total,) = kernel_call(
        all_sum_body, "all_sum", [VMEM] * 2, [((chips, NEAR * chunk, LANES), BF16)]
    )(sums, pivot)
    mine = exchange(total, "chip").reshape(flat)
    other = swap_cores(mine)
    block_one, parent_rows, block_two = kernel_call(
        functools.partial(final_body, w),
        "final",
        [SMEM, VMEM, VMEM, VMEM, SMEM],
        [((2, w, w), BF16)] * 3,
    )(core_ref, mine, other, link_two, widths)
    return column_one, block_one, column_two, parent_rows, block_two


def solution(mesh):
    rows_n, cols_n = mesh.devices.shape
    fine = Mesh(mesh.devices.reshape(rows_n // CORES, CORES, cols_n // NEAR, NEAR), GRID)
    row, col = ("chip", "core"), ("far", "near")
    shared = P(GRID, None)
    in_specs = (P(row, col), shared, P(), P(), shared, P(), P(), P(), P())
    out_specs = (shared, P(), shared, P(), P())
    return jax.shard_map(local, mesh=fine, in_specs=in_specs, out_specs=out_specs, check_vma=False)
```

```python
import functools

import jax
import jax.numpy as jnp
from jax import lax
from jax.experimental import pallas as pl
from jax.experimental.pallas import tpu as pltpu
from jax.sharding import Mesh
from jax.sharding import PartitionSpec as P

F32 = jnp.float32
BF16 = jnp.bfloat16
VMEM = pl.BlockSpec(memory_space=pltpu.VMEM)
ANY = pl.BlockSpec(memory_space=pl.ANY)
SMEM = pl.BlockSpec(memory_space=pltpu.SMEM)
NEAR = 4
CORES = 2
LANES = 128
GRID = ("chip", "core", "far", "near")


def kernel_call(body, name, specs, outs):
    return pl.pallas_call(
        body,
        name=name,
        in_specs=specs,
        out_specs=[VMEM] * len(outs),
        out_shape=[jax.ShapeDtypeStruct(shape, kind) for shape, kind in outs],
        compiler_params=pltpu.CompilerParams(vmem_limit_bytes=40 * 1024 * 1024),
    )


def exchange(blocks, axis):
    return lax.all_to_all(blocks, axis, split_axis=0, concat_axis=0, tiled=True)


def landing_places(chips, planes):
    side = int(chips**0.5)

    def steps(a, b):
        return abs(a // side - b // side) + abs(a % side - b % side)

    places = []
    for q in range(chips):
        far_first = sorted(range(planes), key=lambda z: (-abs(z - q), z))
        close_first = sorted(range(chips), key=lambda p: (steps(p, q), p))
        spots = dict(zip(far_first, close_first))
        places.append([spots[z] for z in range(planes)])
    return places


def swap_cores(block):
    return lax.ppermute(block, "core", [(0, 1), (1, 0)])


def dot(left, right):
    return jnp.dot(left, right, preferred_element_type=F32)


def dot_t(left, right):
    return lax.dot_general(left, right, (((0,), (0,)), ((), ())), preferred_element_type=F32)


def reduced(received):
    total = received[0].astype(F32)
    for i in range(1, received.shape[0]):
        total = total + received[i].astype(F32)
    return total


def is_member(table, s, tile):
    found = table[s, 0] == tile
    for i in range(1, table.shape[1]):
        found = found | (table[s, i] == tile)
    return found


def masked_link(w, link, widths, s):
    row = lax.broadcasted_iota(jnp.int32, (w, w), 0)
    column = lax.broadcasted_iota(jnp.int32, (w, w), 1)
    value = link[s]
    inside = (row < widths[s]) & (column < widths[2 + s])
    return jnp.where(inside, value, jnp.zeros_like(value))


def mask_body(w, tile, one, two, anc_one, anc_two, widths, lower, held_one, held_two, sems):
    copies = [
        pltpu.make_async_copy(one, held_one, sems.at[0]),
        pltpu.make_async_copy(two, held_two, sems.at[1]),
    ]
    for copy in copies:
        copy.start()
    column = lax.broadcasted_iota(jnp.int32, (one.shape[0], w), 1)
    limits = [
        jnp.where(is_member(anc_one if k < 2 else anc_two, k % 2, tile[0]), widths[k], 0)
        for k in range(4)
    ]
    for copy in copies:
        copy.wait()
    for k in range(4):
        value = (held_one if k < 2 else held_two)[:, (k % 2) * w : (k % 2 + 1) * w]
        value = jnp.where(column < limits[k], value, jnp.zeros_like(value))
        lower[:, k * w : (k + 1) * w] = value


def copy_body(source, copies):
    value = source[...]
    for i in range(copies.shape[0]):
        copies[i] = value


def product_body(w, core, order, inverse, mine, other, part, held):
    blocks, share, _ = mine.shape
    half = blocks * share
    for i in range(blocks):
        held[i * share : (i + 1) * share, :] = mine[order[i]]
        held[half + i * share : half + (i + 1) * share, :] = other[order[i]]
    left = inverse[:, pl.ds(pl.multiple_of(core[0] * half, half), half)]
    right = inverse[:, pl.ds(pl.multiple_of((1 - core[0]) * half, half), half)]
    for k in range(4):
        span = slice(k * w, (k + 1) * w)
        value = (dot(left, held[:half, span]) + dot(right, held[half:, span])).astype(BF16)
        for i in range(part.shape[0]):
            part[i, :, span] = value[i * share : (i + 1) * share]


def column_body(
    w, tile, place, received, lower, link, anc_one, anc_two, widths, column_one, column_two, mine, other
):
    total = reduced(received)
    for s in range(2):
        span = slice(s * w, (s + 1) * w)
        here_one = jnp.where(is_member(anc_one, s, tile[0]), 1.0, 0.0)
        here_two = jnp.where(is_member(anc_two, s, tile[0]), 1.0, 0.0)
        one = (-(total[:, span] * here_one)).astype(BF16)
        column_one[:, span] = one
        two = total[:, (2 + s) * w : (3 + s) * w] + dot(one, masked_link(w, link, widths, s))
        column_two[:, span] = (-(two * here_two)).astype(BF16)
    for out, sibling in ((mine, place[0]), (other, 1 - place[0])):
        first = pl.ds(pl.multiple_of(sibling * w, w), w)
        second = pl.ds(pl.multiple_of((2 + sibling) * w, w), w)
        out[0] = -dot_t(lower[:, first], column_one[:, first])
        out[1] = dot_t(column_one[:, first], lower[:, second])
        out[2] = -dot_t(lower[:, second], column_two[:, first])


def core_sum_body(w, mine, other, sums):
    lanes = sums.shape[2]
    for b in range(3):
        value = (mine[b] + other[b]).astype(BF16)
        for h in range(w // lanes):
            sums[h, b * w : (b + 1) * w, :] = value[:, h * lanes : (h + 1) * lanes]


def chunk_sum_body(received, copies):
    value = reduced(received).astype(BF16)
    for i in range(copies.shape[0]):
        copies[i] = value


def pivot_body(w, place, one, two, widths, pivot, stack):
    row = lax.broadcasted_iota(jnp.int32, (w, w), 0)
    column = lax.broadcasted_iota(jnp.int32, (w, w), 1)
    lanes = stack.shape[1]
    for b, source, width in (
        (0, one, widths[place[0]]),
        (1, None, 0),
        (2, two, widths[2 + place[0]]),
    ):
        value = jnp.zeros((w, w), F32)
        if source is not None:
            value = jnp.where((row < width) & (column < width), source[place[0]].astype(F32), value)
        for h in range(w // lanes):
            start = (3 * h + b) * w
            stack[start : start + w, :] = value[:, h * lanes : (h + 1) * lanes]
    size = pivot.shape[0]
    pivot[...] = stack[pl.ds(pl.multiple_of(place[1] * size, size), size), :]


def all_sum_body(received, pivot, copies):
    near, chunk = NEAR, received.shape[1]
    for n in range(near):
        total = pivot[n * chunk : (n + 1) * chunk, :]
        for i in range(n, received.shape[0], near):
            total = total + received[i].astype(F32)
        total = total.astype(BF16)
        for i in range(copies.shape[0]):
            copies[i, n * chunk : (n + 1) * chunk, :] = total


def side_by_side(total, b, w):
    span = slice(b * w, (b + 1) * w)
    return jnp.concatenate([total[h, span, :] for h in range(total.shape[0])], axis=1)


def final_body(w, core, mine, other, link, widths, block_one, parent_rows, block_two):
    for total, sibling in ((mine, core[0]), (other, 1 - core[0])):
        tie = masked_link(w, link, widths, sibling)
        block = side_by_side(total, 0, w)
        cross = side_by_side(total, 1, w).astype(F32)
        block_one[sibling] = block
        parent = (-(dot(block, tie) + cross)).astype(BF16)
        parent_rows[sibling] = parent
        rest = side_by_side(total, 2, w).astype(F32) - dot_t(tie, parent)
        block_two[sibling] = rest.astype(BF16)


def local(
    ancestor_inverse,
    panel_one,
    ancestors_one,
    diag_inverse_one,
    panel_two,
    link_two,
    ancestors_two,
    diag_inverse_two,
    widths,
):
    w = diag_inverse_one.shape[-1]
    chips, far_n = lax.axis_size("chip"), lax.axis_size("far")
    planes = far_n * NEAR
    local_rows = ancestor_inverse.shape[0]
    share = panel_one.shape[0]
    chip = lax.axis_index("chip").astype(jnp.int32)
    core = lax.axis_index("core").astype(jnp.int32)
    tile = (chip * CORES + core).reshape(1)
    core_ref = core.reshape(1)
    whole = (share, 4 * w)

    lower = pl.pallas_call(
        functools.partial(mask_body, w),
        name="mask",
        in_specs=[SMEM, ANY, ANY, SMEM, SMEM, SMEM],
        out_specs=VMEM,
        out_shape=jax.ShapeDtypeStruct(whole, BF16),
        scratch_shapes=[pltpu.VMEM(panel_one.shape, BF16)] * 2 + [pltpu.SemaphoreType.DMA((2,))],
    )(tile, panel_one, panel_two, ancestors_one, ancestors_two, widths)

    places = landing_places(chips, planes)
    pairs = []
    for q in range(chips):
        for k in range(CORES):
            for z in range(planes):
                pairs.append(((q * CORES + k) * planes + z, (places[q][z] * CORES + k) * planes + q))
    moved = lax.ppermute(lower, GRID, pairs)
    plane = lax.axis_index("far") * NEAR + lax.axis_index("near")
    order = lax.dynamic_index_in_dim(jnp.array(places, jnp.int32), plane, 0, keepdims=False)
    place = jnp.stack([core, chip])
    flat = (w // LANES, 3 * w, LANES)
    chunk = 3 * w * w // LANES // (chips * NEAR)
    pivot = pl.pallas_call(
        functools.partial(pivot_body, w),
        name="pivot",
        in_specs=[SMEM, VMEM, VMEM, SMEM],
        out_specs=VMEM,
        out_shape=jax.ShapeDtypeStruct((NEAR * chunk, LANES), F32),
        scratch_shapes=[pltpu.VMEM((3 * w * w // LANES, LANES), F32)],
    )(place, diag_inverse_one, diag_inverse_two, widths)
    moved, order, place, pivot = lax.optimization_barrier((moved, order, place, pivot))
    (moved,) = kernel_call(copy_body, "copies", [VMEM], [((chips,) + whole, BF16)])(moved)
    mine = exchange(moved, "chip")
    other = swap_cores(mine)

    part = pl.pallas_call(
        functools.partial(product_body, w),
        name="product",
        in_specs=[SMEM, SMEM] + [VMEM] * 3,
        out_specs=VMEM,
        out_shape=jax.ShapeDtypeStruct((planes,) + whole, BF16),
        scratch_shapes=[pltpu.VMEM((CORES * chips * share, 4 * w), BF16)],
        compiler_params=pltpu.CompilerParams(vmem_limit_bytes=40 * 1024 * 1024),
    )(core_ref, order, ancestor_inverse, mine, other)
    part = exchange(part, ("far", "near"))
    column_one, column_two, mine, other = kernel_call(
        functools.partial(column_body, w),
        "columns",
        [SMEM, SMEM, VMEM, VMEM, VMEM, SMEM, SMEM, SMEM],
        [((share, 2 * w), BF16)] * 2 + [((3, w, w), F32)] * 2,
    )(tile, place, part, lower, link_two, ancestors_one, ancestors_two, widths)
    other = swap_cores(other)
    (sums,) = kernel_call(
        functools.partial(core_sum_body, w), "core_sum", [VMEM] * 2, [(flat, BF16)]
    )(mine, other)
    sums = exchange(sums.reshape(chips * NEAR, chunk, LANES), ("chip", "near"))
    (sums,) = kernel_call(chunk_sum_body, "chunk_sum", [VMEM], [((planes, chunk, LANES), BF16)])(
        sums
    )
    sums = exchange(sums, ("far", "near"))
    (total,) = kernel_call(
        all_sum_body, "all_sum", [VMEM] * 2, [((chips, NEAR * chunk, LANES), BF16)]
    )(sums, pivot)
    mine = exchange(total, "chip").reshape(flat)
    other = swap_cores(mine)
    block_one, parent_rows, block_two = kernel_call(
        functools.partial(final_body, w),
        "final",
        [SMEM, VMEM, VMEM, VMEM, SMEM],
        [((2, w, w), BF16)] * 3,
    )(core_ref, mine, other, link_two, widths)
    return column_one, block_one, column_two, parent_rows, block_two


def solution(mesh):
    rows_n, cols_n = mesh.devices.shape
    fine = Mesh(mesh.devices.reshape(rows_n // CORES, CORES, cols_n // NEAR, NEAR), GRID)
    row, col = ("chip", "core"), ("far", "near")
    shared = P(GRID, None)
    in_specs = (P(row, col), shared, P(), P(), shared, P(), P(), P(), P())
    out_specs = (shared, P(), shared, P(), P())
    return jax.shard_map(local, mesh=fine, in_specs=in_specs, out_specs=out_specs, check_vma=False)
```

```python
import functools

import jax
import jax.numpy as jnp
from jax import lax
from jax.experimental import pallas as pl
from jax.experimental.pallas import tpu as pltpu
from jax.sharding import Mesh
from jax.sharding import PartitionSpec as P

F32 = jnp.float32
BF16 = jnp.bfloat16
VMEM = pl.BlockSpec(memory_space=pltpu.VMEM)
ANY = pl.BlockSpec(memory_space=pl.ANY)
SMEM = pl.BlockSpec(memory_space=pltpu.SMEM)
NEAR = 4
CORES = 2
LANES = 128
GRID = ("chip", "core", "far", "near")


def kernel_call(body, name, specs, outs):
    return pl.pallas_call(
        body,
        name=name,
        in_specs=specs,
        out_specs=[VMEM] * len(outs),
        out_shape=[jax.ShapeDtypeStruct(shape, kind) for shape, kind in outs],
        compiler_params=pltpu.CompilerParams(vmem_limit_bytes=40 * 1024 * 1024),
    )


def exchange(blocks, axis):
    return lax.all_to_all(blocks, axis, split_axis=0, concat_axis=0, tiled=True)


def landing_places(chips, planes):
    side = int(chips**0.5)

    def steps(a, b):
        return abs(a // side - b // side) + abs(a % side - b % side)

    places = []
    for q in range(chips):
        far_first = sorted(range(planes), key=lambda z: (-abs(z - q), z))
        close_first = sorted(range(chips), key=lambda p: (steps(p, q), p))
        spots = dict(zip(far_first, close_first))
        places.append([spots[z] for z in range(planes)])
    return places


def swap_cores(block):
    return lax.ppermute(block, "core", [(0, 1), (1, 0)])


def dot(left, right):
    return jnp.dot(left, right, preferred_element_type=F32)


def dot_t(left, right):
    return lax.dot_general(left, right, (((0,), (0,)), ((), ())), preferred_element_type=F32)


def reduced(received):
    total = received[0].astype(F32)
    for i in range(1, received.shape[0]):
        total = total + received[i].astype(F32)
    return total


def is_member(table, s, tile):
    found = table[s, 0] == tile
    for i in range(1, table.shape[1]):
        found = found | (table[s, i] == tile)
    return found


def masked_link(w, link, widths, s):
    row = lax.broadcasted_iota(jnp.int32, (w, w), 0)
    column = lax.broadcasted_iota(jnp.int32, (w, w), 1)
    value = link[s]
    inside = (row < widths[s]) & (column < widths[2 + s])
    return jnp.where(inside, value, jnp.zeros_like(value))


def mask_body(w, tile, one, two, anc_one, anc_two, widths, lower, held_one, held_two, sems):
    copies = [
        pltpu.make_async_copy(one, held_one, sems.at[0]),
        pltpu.make_async_copy(two, held_two, sems.at[1]),
    ]
    for copy in copies:
        copy.start()
    column = lax.broadcasted_iota(jnp.int32, (one.shape[0], w), 1)
    limits = [
        jnp.where(is_member(anc_one if k < 2 else anc_two, k % 2, tile[0]), widths[k], 0)
        for k in range(4)
    ]
    for copy in copies:
        copy.wait()
    for k in range(4):
        value = (held_one if k < 2 else held_two)[:, (k % 2) * w : (k % 2 + 1) * w]
        value = jnp.where(column < limits[k], value, jnp.zeros_like(value))
        lower[:, k * w : (k + 1) * w] = value


def copy_body(source, copies):
    value = source[...]
    for i in range(copies.shape[0]):
        copies[i] = value


def product_body(w, core, order, inverse, mine, other, rows, part, keep, give, held, dense):
    blocks, share, _ = mine.shape
    half = blocks * share
    for i in range(blocks):
        held[i * share : (i + 1) * share, :] = mine[order[i]]
        held[half + i * share : half + (i + 1) * share, :] = other[order[i]]
    left = inverse[:, pl.ds(pl.multiple_of(core[0] * half, half), half)]
    right = inverse[:, pl.ds(pl.multiple_of((1 - core[0]) * half, half), half)]
    for k in range(4):
        span = slice(k * w, (k + 1) * w)
        value = (dot(left, held[:half, span]) + dot(right, held[half:, span])).astype(BF16)
        dense[:, span] = value
        for i in range(part.shape[0]):
            for h in range(w // LANES):
                place = (k * (w // LANES) + h) * share
                piece = value[i * share : (i + 1) * share, h * LANES : (h + 1) * LANES]
                part[i, place : place + share, :] = piece
    for out, sibling in ((keep, core[0]), (give, 1 - core[0])):
        first = pl.ds(pl.multiple_of(sibling * w, w), w)
        second = pl.ds(pl.multiple_of((2 + sibling) * w, w), w)
        out[0] = dot_t(rows[:, first], dense[:, first])
        out[1] = dot_t(dense[:, first], rows[:, second])
        out[2] = dot_t(rows[:, second], dense[:, second])


def column_body(w, chunk, tile, received, link, anc_one, anc_two, widths, column_one, column_two):
    total = received[0, chunk:, :].astype(F32)
    for i in range(1, received.shape[0]):
        total = total + received[i, chunk:, :].astype(F32)
    share, pieces = column_one.shape[0], w // LANES

    def group(k):
        starts = [(k * pieces + h) * share for h in range(pieces)]
        return jnp.concatenate([total[a : a + share] for a in starts], axis=1)

    for s in range(2):
        span = slice(s * w, (s + 1) * w)
        here_one = jnp.where(is_member(anc_one, s, tile[0]), 1.0, 0.0)
        here_two = jnp.where(is_member(anc_two, s, tile[0]), 1.0, 0.0)
        one = (-(group(s) * here_one)).astype(BF16)
        column_one[:, span] = one
        two = group(2 + s) + dot(one, masked_link(w, link, widths, s))
        column_two[:, span] = (-(two * here_two)).astype(BF16)


def core_sum_body(w, mine, other, sums):
    lanes = sums.shape[2]
    for b in range(3):
        value = (mine[b] + other[b]).astype(BF16)
        for h in range(w // lanes):
            sums[h, b * w : (b + 1) * w, :] = value[:, h * lanes : (h + 1) * lanes]


def chunk_sum_body(received, part, packed):
    chunk = received.shape[1]
    value = reduced(received).astype(BF16)
    for i in range(packed.shape[0]):
        packed[i, :chunk, :] = value
        packed[i, chunk:, :] = part[i]


def pivot_body(w, place, one, two, widths, pivot, stack):
    row = lax.broadcasted_iota(jnp.int32, (w, w), 0)
    column = lax.broadcasted_iota(jnp.int32, (w, w), 1)
    lanes = stack.shape[1]
    for b, source, width in (
        (0, one, widths[place[0]]),
        (1, None, 0),
        (2, two, widths[2 + place[0]]),
    ):
        value = jnp.zeros((w, w), F32)
        if source is not None:
            value = jnp.where((row < width) & (column < width), source[place[0]].astype(F32), value)
        for h in range(w // lanes):
            start = (3 * h + b) * w
            stack[start : start + w, :] = value[:, h * lanes : (h + 1) * lanes]
    size = pivot.shape[0]
    pivot[...] = stack[pl.ds(pl.multiple_of(place[1] * size, size), size), :]


def all_sum_body(received, pivot, copies):
    near, chunk = NEAR, pivot.shape[0] // NEAR
    for n in range(near):
        total = pivot[n * chunk : (n + 1) * chunk, :]
        for i in range(n, received.shape[0], near):
            total = total + received[i, :chunk, :].astype(F32)
        total = total.astype(BF16)
        for i in range(copies.shape[0]):
            copies[i, n * chunk : (n + 1) * chunk, :] = total


def side_by_side(total, b, w):
    span = slice(b * w, (b + 1) * w)
    return jnp.concatenate([total[h, span, :] for h in range(total.shape[0])], axis=1)


def final_body(w, core, mine, other, link, widths, block_one, parent_rows, block_two):
    for total, sibling in ((mine, core[0]), (other, 1 - core[0])):
        tie = masked_link(w, link, widths, sibling)
        block = side_by_side(total, 0, w)
        cross = side_by_side(total, 1, w)
        block_one[sibling] = block
        parent = (cross.astype(F32) - dot(block, tie)).astype(BF16)
        parent_rows[sibling] = parent
        rest = side_by_side(total, 2, w).astype(F32) - dot_t(cross, tie) - dot_t(tie, parent)
        block_two[sibling] = rest.astype(BF16)


def local(
    ancestor_inverse,
    panel_one,
    ancestors_one,
    diag_inverse_one,
    panel_two,
    link_two,
    ancestors_two,
    diag_inverse_two,
    widths,
):
    w = diag_inverse_one.shape[-1]
    chips, far_n = lax.axis_size("chip"), lax.axis_size("far")
    planes = far_n * NEAR
    local_rows = ancestor_inverse.shape[0]
    share = panel_one.shape[0]
    chip = lax.axis_index("chip").astype(jnp.int32)
    core = lax.axis_index("core").astype(jnp.int32)
    tile = (chip * CORES + core).reshape(1)
    core_ref = core.reshape(1)
    whole = (share, 4 * w)

    lower = pl.pallas_call(
        functools.partial(mask_body, w),
        name="mask",
        in_specs=[SMEM, ANY, ANY, SMEM, SMEM, SMEM],
        out_specs=VMEM,
        out_shape=jax.ShapeDtypeStruct(whole, BF16),
        scratch_shapes=[pltpu.VMEM(panel_one.shape, BF16)] * 2 + [pltpu.SemaphoreType.DMA((2,))],
    )(tile, panel_one, panel_two, ancestors_one, ancestors_two, widths)

    places = landing_places(chips, planes)
    pairs = []
    for q in range(chips):
        for k in range(CORES):
            for z in range(planes):
                pairs.append(((q * CORES + k) * planes + z, (places[q][z] * CORES + k) * planes + q))
    moved = lax.ppermute(lower, GRID, pairs)
    plane = lax.axis_index("far") * NEAR + lax.axis_index("near")
    order = lax.dynamic_index_in_dim(jnp.array(places, jnp.int32), plane, 0, keepdims=False)
    place = jnp.stack([core, chip])
    flat = (w // LANES, 3 * w, LANES)
    chunk = 3 * w * w // LANES // (chips * NEAR)
    pivot = pl.pallas_call(
        functools.partial(pivot_body, w),
        name="pivot",
        in_specs=[SMEM, VMEM, VMEM, SMEM],
        out_specs=VMEM,
        out_shape=jax.ShapeDtypeStruct((NEAR * chunk, LANES), F32),
        scratch_shapes=[pltpu.VMEM((3 * w * w // LANES, LANES), F32)],
    )(place, diag_inverse_one, diag_inverse_two, widths)
    rows = lax.all_gather(lower, ("far", "near"), axis=0, tiled=True)
    moved, rows = lax.optimization_barrier((moved, rows))
    (moved,) = kernel_call(copy_body, "copies", [VMEM], [((chips,) + whole, BF16)])(moved)
    mine = exchange(moved, "chip")
    other = swap_cores(mine)

    part, mine, other = pl.pallas_call(
        functools.partial(product_body, w),
        name="product",
        in_specs=[SMEM, SMEM] + [VMEM] * 4,
        out_specs=[VMEM] * 3,
        out_shape=[jax.ShapeDtypeStruct((planes, share * 4 * w // LANES, LANES), BF16)]
        + [jax.ShapeDtypeStruct((3, w, w), F32)] * 2,
        scratch_shapes=[
            pltpu.VMEM((CORES * chips * share, 4 * w), BF16),
            pltpu.VMEM((local_rows, 4 * w), BF16),
        ],
        compiler_params=pltpu.CompilerParams(vmem_limit_bytes=40 * 1024 * 1024),
    )(core_ref, order, ancestor_inverse, mine, other, rows)
    other, pivot = lax.optimization_barrier((swap_cores(other), pivot))
    (sums,) = kernel_call(
        functools.partial(core_sum_body, w), "core_sum", [VMEM] * 2, [(flat, BF16)]
    )(mine, other)
    sums = exchange(sums.reshape(chips * NEAR, chunk, LANES), ("chip", "near"))
    (packed,) = kernel_call(
        chunk_sum_body, "chunk_sum", [VMEM] * 2, [((planes, chunk + part.shape[1], LANES), BF16)]
    )(sums, part)
    packed = exchange(packed, ("far", "near"))
    (total,) = kernel_call(
        all_sum_body, "all_sum", [VMEM] * 2, [((chips, NEAR * chunk, LANES), BF16)]
    )(
        packed, pivot
    )
    mine = exchange(total, "chip").reshape(flat)
    other = swap_cores(mine)
    column_one, column_two = kernel_call(
        functools.partial(column_body, w, chunk),
        "columns",
        [SMEM, VMEM, VMEM, SMEM, SMEM, SMEM],
        [((share, 2 * w), BF16)] * 2,
    )(tile, packed, link_two, ancestors_one, ancestors_two, widths)
    block_one, parent_rows, block_two = kernel_call(
        functools.partial(final_body, w),
        "final",
        [SMEM, VMEM, VMEM, VMEM, SMEM],
        [((2, w, w), BF16)] * 3,
    )(core_ref, mine, other, link_two, widths)
    return column_one, block_one, column_two, parent_rows, block_two


def solution(mesh):
    rows_n, cols_n = mesh.devices.shape
    fine = Mesh(mesh.devices.reshape(rows_n // CORES, CORES, cols_n // NEAR, NEAR), GRID)
    row, col = ("chip", "core"), ("far", "near")
    shared = P(GRID, None)
    in_specs = (P(row, col), shared, P(), P(), shared, P(), P(), P(), P())
    out_specs = (shared, P(), shared, P(), P())
    return jax.shard_map(local, mesh=fine, in_specs=in_specs, out_specs=out_specs, check_vma=False)
```

```python
import functools

import jax
import jax.numpy as jnp
from jax import lax
from jax.experimental import pallas as pl
from jax.experimental.pallas import tpu as pltpu
from jax.sharding import Mesh
from jax.sharding import PartitionSpec as P

F32 = jnp.float32
BF16 = jnp.bfloat16
VMEM = pl.BlockSpec(memory_space=pltpu.VMEM)
ANY = pl.BlockSpec(memory_space=pl.ANY)
SMEM = pl.BlockSpec(memory_space=pltpu.SMEM)
NEAR = 4
PAIR = 2
CORES = 2
LANES = 128
GRID = ("chip", "core", "far", "mid", "pair")


def kernel_call(body, name, specs, outs):
    return pl.pallas_call(
        body,
        name=name,
        in_specs=specs,
        out_specs=[VMEM] * len(outs),
        out_shape=[jax.ShapeDtypeStruct(shape, kind) for shape, kind in outs],
        compiler_params=pltpu.CompilerParams(vmem_limit_bytes=40 * 1024 * 1024),
    )


def exchange(blocks, axis):
    return lax.all_to_all(blocks, axis, split_axis=0, concat_axis=0, tiled=True)


def landing_places(chips, planes):
    side = int(chips**0.5)

    def steps(a, b):
        return abs(a // side - b // side) + abs(a % side - b % side)

    places = []
    for q in range(chips):
        far_first = sorted(range(planes), key=lambda z: (-abs(z - q), z))
        close_first = sorted(range(chips), key=lambda p: (steps(p, q), p))
        spots = dict(zip(far_first, close_first))
        places.append([spots[z] for z in range(planes)])
    return places


def swap_cores(block):
    return lax.ppermute(block, "core", [(0, 1), (1, 0)])


def dot(left, right):
    return jnp.dot(left, right, preferred_element_type=F32)


def dot_t(left, right):
    return lax.dot_general(left, right, (((0,), (0,)), ((), ())), preferred_element_type=F32)


def reduced(received):
    total = received[0].astype(F32)
    for i in range(1, received.shape[0]):
        total = total + received[i].astype(F32)
    return total


def is_member(table, s, tile):
    found = table[s, 0] == tile
    for i in range(1, table.shape[1]):
        found = found | (table[s, i] == tile)
    return found


def masked_link(w, link, widths, s):
    row = lax.broadcasted_iota(jnp.int32, (w, w), 0)
    column = lax.broadcasted_iota(jnp.int32, (w, w), 1)
    value = link[s]
    inside = (row < widths[s]) & (column < widths[2 + s])
    return jnp.where(inside, value, jnp.zeros_like(value))


def mask_body(w, tile, one, two, anc_one, anc_two, widths, lower, held_one, held_two, sems):
    copies = [
        pltpu.make_async_copy(one, held_one, sems.at[0]),
        pltpu.make_async_copy(two, held_two, sems.at[1]),
    ]
    for copy in copies:
        copy.start()
    column = lax.broadcasted_iota(jnp.int32, (one.shape[0], w), 1)
    limits = [
        jnp.where(is_member(anc_one if k < 2 else anc_two, k % 2, tile[0]), widths[k], 0)
        for k in range(4)
    ]
    for copy in copies:
        copy.wait()
    for k in range(4):
        value = (held_one if k < 2 else held_two)[:, (k % 2) * w : (k % 2 + 1) * w]
        value = jnp.where(column < limits[k], value, jnp.zeros_like(value))
        lower[:, k * w : (k + 1) * w] = value


def copy_body(source, copies):
    value = source[...]
    for i in range(copies.shape[0]):
        copies[i] = value


def product_body(w, core, parity, order, inverse, mine, other, keep, give, held, part):
    blocks, share, _ = mine.shape
    half = blocks * share
    for i in range(blocks):
        held[i * share : (i + 1) * share, :] = mine[order[i]]
        held[half + i * share : half + (i + 1) * share, :] = other[order[i]]
    left = inverse[:, pl.ds(pl.multiple_of(core[0] * half, half), half)]
    right = inverse[:, pl.ds(pl.multiple_of((1 - core[0]) * half, half), half)]
    for k in range(4):
        span = slice(k * w, (k + 1) * w)
        value = (dot(left, held[:half, span]) + dot(right, held[half:, span])).astype(BF16)
        for i in range(part.shape[0]):
            part[i, :, span] = value[i * share : (i + 1) * share]
    for i in range(keep.shape[0]):
        keep[i] = part[PAIR * i + parity[0]]
        give[i] = part[PAIR * i + 1 - parity[0]]


def pair_sum_body(keep, got, sums):
    for i in range(sums.shape[0]):
        sums[i] = (keep[i].astype(F32) + got[i].astype(F32)).astype(BF16)


def column_body(
    w, tile, place, received, lower, link, anc_one, anc_two, widths, column_one, column_two, mine, other
):
    total = reduced(received)
    for s in range(2):
        span = slice(s * w, (s + 1) * w)
        here_one = jnp.where(is_member(anc_one, s, tile[0]), 1.0, 0.0)
        here_two = jnp.where(is_member(anc_two, s, tile[0]), 1.0, 0.0)
        one = (-(total[:, span] * here_one)).astype(BF16)
        column_one[:, span] = one
        two = total[:, (2 + s) * w : (3 + s) * w] + dot(one, masked_link(w, link, widths, s))
        column_two[:, span] = (-(two * here_two)).astype(BF16)
    for out, sibling in ((mine, place[0]), (other, 1 - place[0])):
        first = pl.ds(pl.multiple_of(sibling * w, w), w)
        second = pl.ds(pl.multiple_of((2 + sibling) * w, w), w)
        out[0] = -dot_t(lower[:, first], column_one[:, first])
        out[1] = dot_t(column_one[:, first], lower[:, second])
        out[2] = -dot_t(lower[:, second], column_two[:, first])


def core_sum_body(w, mine, other, sums):
    lanes = sums.shape[2]
    for b in range(3):
        value = (mine[b] + other[b]).astype(BF16)
        for h in range(w // lanes):
            sums[h, b * w : (b + 1) * w, :] = value[:, h * lanes : (h + 1) * lanes]


def chunk_sum_body(received, copies):
    value = reduced(received).astype(BF16)
    for i in range(copies.shape[0]):
        copies[i] = value


def pivot_body(w, place, one, two, widths, pivot, stack):
    row = lax.broadcasted_iota(jnp.int32, (w, w), 0)
    column = lax.broadcasted_iota(jnp.int32, (w, w), 1)
    lanes = stack.shape[1]
    for b, source, width in (
        (0, one, widths[place[0]]),
        (1, None, 0),
        (2, two, widths[2 + place[0]]),
    ):
        value = jnp.zeros((w, w), F32)
        if source is not None:
            value = jnp.where((row < width) & (column < width), source[place[0]].astype(F32), value)
        for h in range(w // lanes):
            start = (3 * h + b) * w
            stack[start : start + w, :] = value[:, h * lanes : (h + 1) * lanes]
    size = pivot.shape[0]
    pivot[...] = stack[pl.ds(pl.multiple_of(place[1] * size, size), size), :]


def all_sum_body(received, pivot, copies):
    near, chunk = NEAR, received.shape[1]
    for n in range(near):
        total = pivot[n * chunk : (n + 1) * chunk, :]
        for i in range(n, received.shape[0], near):
            total = total + received[i].astype(F32)
        total = total.astype(BF16)
        for i in range(copies.shape[0]):
            copies[i, n * chunk : (n + 1) * chunk, :] = total


def side_by_side(total, b, w):
    span = slice(b * w, (b + 1) * w)
    return jnp.concatenate([total[h, span, :] for h in range(total.shape[0])], axis=1)


def final_body(w, core, mine, other, link, widths, block_one, parent_rows, block_two):
    for total, sibling in ((mine, core[0]), (other, 1 - core[0])):
        tie = masked_link(w, link, widths, sibling)
        block = side_by_side(total, 0, w)
        cross = side_by_side(total, 1, w).astype(F32)
        block_one[sibling] = block
        parent = (-(dot(block, tie) + cross)).astype(BF16)
        parent_rows[sibling] = parent
        rest = side_by_side(total, 2, w).astype(F32) - dot_t(tie, parent)
        block_two[sibling] = rest.astype(BF16)


def local(
    ancestor_inverse,
    panel_one,
    ancestors_one,
    diag_inverse_one,
    panel_two,
    link_two,
    ancestors_two,
    diag_inverse_two,
    widths,
):
    w = diag_inverse_one.shape[-1]
    chips, far_n = lax.axis_size("chip"), lax.axis_size("far")
    planes = far_n * NEAR
    local_rows = ancestor_inverse.shape[0]
    share = panel_one.shape[0]
    chip = lax.axis_index("chip").astype(jnp.int32)
    core = lax.axis_index("core").astype(jnp.int32)
    tile = (chip * CORES + core).reshape(1)
    core_ref = core.reshape(1)
    whole = (share, 4 * w)

    lower = pl.pallas_call(
        functools.partial(mask_body, w),
        name="mask",
        in_specs=[SMEM, ANY, ANY, SMEM, SMEM, SMEM],
        out_specs=VMEM,
        out_shape=jax.ShapeDtypeStruct(whole, BF16),
        scratch_shapes=[pltpu.VMEM(panel_one.shape, BF16)] * 2 + [pltpu.SemaphoreType.DMA((2,))],
    )(tile, panel_one, panel_two, ancestors_one, ancestors_two, widths)

    places = landing_places(chips, planes)
    pairs = []
    for q in range(chips):
        for k in range(CORES):
            for z in range(planes):
                pairs.append(((q * CORES + k) * planes + z, (places[q][z] * CORES + k) * planes + q))
    moved = lax.ppermute(lower, GRID, pairs)
    parity = lax.axis_index("pair").astype(jnp.int32)
    plane = lax.axis_index("far") * NEAR + lax.axis_index("mid") * PAIR + parity
    order = lax.dynamic_index_in_dim(jnp.array(places, jnp.int32), plane, 0, keepdims=False)
    place = jnp.stack([core, chip])
    flat = (w // LANES, 3 * w, LANES)
    chunk = 3 * w * w // LANES // (chips * NEAR)
    pivot = pl.pallas_call(
        functools.partial(pivot_body, w),
        name="pivot",
        in_specs=[SMEM, VMEM, VMEM, SMEM],
        out_specs=VMEM,
        out_shape=jax.ShapeDtypeStruct((NEAR * chunk, LANES), F32),
        scratch_shapes=[pltpu.VMEM((3 * w * w // LANES, LANES), F32)],
    )(place, diag_inverse_one, diag_inverse_two, widths)
    moved, order, place, pivot = lax.optimization_barrier((moved, order, place, pivot))
    (moved,) = kernel_call(copy_body, "copies", [VMEM], [((chips,) + whole, BF16)])(moved)
    mine = exchange(moved, "chip")
    other = swap_cores(mine)

    half = (planes // PAIR,) + whole
    keep, give = pl.pallas_call(
        functools.partial(product_body, w),
        name="product",
        in_specs=[SMEM] * 3 + [VMEM] * 3,
        out_specs=[VMEM] * 2,
        out_shape=[jax.ShapeDtypeStruct(half, BF16)] * 2,
        scratch_shapes=[
            pltpu.VMEM((CORES * chips * share, 4 * w), BF16),
            pltpu.VMEM((planes,) + whole, BF16),
        ],
        compiler_params=pltpu.CompilerParams(vmem_limit_bytes=40 * 1024 * 1024),
    )(core_ref, parity.reshape(1), order, ancestor_inverse, mine, other)
    got = lax.ppermute(give, "pair", [(0, 1), (1, 0)])
    (part,) = kernel_call(pair_sum_body, "pair_sum", [VMEM] * 2, [(half, BF16)])(keep, got)
    part = exchange(part, ("far", "mid"))
    column_one, column_two, mine, other = kernel_call(
        functools.partial(column_body, w),
        "columns",
        [SMEM, SMEM, VMEM, VMEM, VMEM, SMEM, SMEM, SMEM],
        [((share, 2 * w), BF16)] * 2 + [((3, w, w), F32)] * 2,
    )(tile, place, part, lower, link_two, ancestors_one, ancestors_two, widths)
    other = swap_cores(other)
    (sums,) = kernel_call(
        functools.partial(core_sum_body, w), "core_sum", [VMEM] * 2, [(flat, BF16)]
    )(mine, other)
    sums = exchange(sums.reshape(chips * NEAR, chunk, LANES), ("chip", "mid", "pair"))
    (sums,) = kernel_call(chunk_sum_body, "chunk_sum", [VMEM], [((planes, chunk, LANES), BF16)])(
        sums
    )
    sums = exchange(sums, ("far", "mid", "pair"))
    (total,) = kernel_call(
        all_sum_body, "all_sum", [VMEM] * 2, [((chips, NEAR * chunk, LANES), BF16)]
    )(sums, pivot)
    mine = exchange(total, "chip").reshape(flat)
    other = swap_cores(mine)
    block_one, parent_rows, block_two = kernel_call(
        functools.partial(final_body, w),
        "final",
        [SMEM, VMEM, VMEM, VMEM, SMEM],
        [((2, w, w), BF16)] * 3,
    )(core_ref, mine, other, link_two, widths)
    return column_one, block_one, column_two, parent_rows, block_two


def solution(mesh):
    rows_n, cols_n = mesh.devices.shape
    sizes = (rows_n // CORES, CORES, cols_n // NEAR, NEAR // PAIR, PAIR)
    fine = Mesh(mesh.devices.reshape(sizes), GRID)
    row, col = GRID[:2], GRID[2:]
    shared = P(GRID, None)
    in_specs = (P(row, col), shared, P(), P(), shared, P(), P(), P(), P())
    out_specs = (shared, P(), shared, P(), P())
    return jax.shard_map(local, mesh=fine, in_specs=in_specs, out_specs=out_specs, check_vma=False)
```

```python
import functools

import jax
import jax.numpy as jnp
from jax import lax
from jax.experimental import pallas as pl
from jax.experimental.pallas import tpu as pltpu
from jax.sharding import Mesh
from jax.sharding import PartitionSpec as P

F32 = jnp.float32
BF16 = jnp.bfloat16
VMEM = pl.BlockSpec(memory_space=pltpu.VMEM)
ANY = pl.BlockSpec(memory_space=pl.ANY)
SMEM = pl.BlockSpec(memory_space=pltpu.SMEM)
NEAR = 4
PAIR = 2
CORES = 2
LANES = 128
GRID = ("chip", "core", "far", "mid", "pair")


def kernel_call(body, name, specs, outs):
    return pl.pallas_call(
        body,
        name=name,
        in_specs=specs,
        out_specs=[VMEM] * len(outs),
        out_shape=[jax.ShapeDtypeStruct(shape, kind) for shape, kind in outs],
        compiler_params=pltpu.CompilerParams(vmem_limit_bytes=40 * 1024 * 1024),
    )


def exchange(blocks, axis):
    return lax.all_to_all(blocks, axis, split_axis=0, concat_axis=0, tiled=True)


def landing_places(chips, planes):
    side = int(chips**0.5)

    def steps(a, b):
        return abs(a // side - b // side) + abs(a % side - b % side)

    places = []
    for q in range(chips):
        far_first = sorted(range(planes), key=lambda z: (-abs(z - q), z))
        close_first = sorted(range(chips), key=lambda p: (steps(p, q), p))
        spots = dict(zip(far_first, close_first))
        places.append([spots[z] for z in range(planes)])
    return places


def swap_cores(block):
    return lax.ppermute(block, "core", [(0, 1), (1, 0)])


def dot(left, right):
    return jnp.dot(left, right, preferred_element_type=F32)


def dot_t(left, right):
    return lax.dot_general(left, right, (((0,), (0,)), ((), ())), preferred_element_type=F32)


def reduced(received):
    total = received[0].astype(F32)
    for i in range(1, received.shape[0]):
        total = total + received[i].astype(F32)
    return total


def column_limits(ancestors, widths, tile):
    here = [jnp.any(table == tile, axis=1) for table in ancestors]
    return jnp.where(jnp.concatenate(here), widths, 0)


def inside_limits(limits, first, shape, w):
    column = lax.broadcasted_iota(jnp.int32, shape, 1)
    limit = jnp.zeros(shape, jnp.int32)
    for k in range(shape[1] // w):
        limit = jnp.where(column >= k * w, limits[first + k] + k * w, limit)
    return column < limit


def masked_link(w, link, widths, s):
    row = lax.broadcasted_iota(jnp.int32, (w, w), 0)
    column = lax.broadcasted_iota(jnp.int32, (w, w), 1)
    value = link[s]
    inside = (row < widths[s]) & (column < widths[2 + s])
    return jnp.where(inside, value, jnp.zeros_like(value))


def copy_body(source, copies):
    value = source[...]
    for i in range(copies.shape[0]):
        copies[i] = value


def product_body(
    w, core, parity, order, limits, inverse, mine, other, keep, give, held, part
):
    blocks, share, _ = mine.shape
    half = blocks * share
    for source, first, start in ((mine, 0, 0), (other, 4, half)):
        inside = inside_limits(limits, first, (share, 4 * w), w)
        for i in range(blocks):
            value = source[order[i]]
            value = jnp.where(inside, value, jnp.zeros_like(value))
            held[start + i * share : start + (i + 1) * share, :] = value
    left = inverse[:, pl.ds(pl.multiple_of(core[0] * half, half), half)]
    right = inverse[:, pl.ds(pl.multiple_of((1 - core[0]) * half, half), half)]
    for k in range(4):
        span = slice(k * w, (k + 1) * w)
        value = (dot(left, held[:half, span]) + dot(right, held[half:, span])).astype(BF16)
        for i in range(part.shape[0]):
            part[i, :, span] = value[i * share : (i + 1) * share]
    for i in range(keep.shape[0]):
        keep[i] = part[PAIR * i + parity[0]]
        give[i] = part[PAIR * i + 1 - parity[0]]


def pair_sum_body(keep, got, sums):
    for i in range(sums.shape[0]):
        sums[i] = (keep[i].astype(F32) + got[i].astype(F32)).astype(BF16)


def column_body(
    w, place, limits, received, one, two, link, widths, column_one, column_two, mine, other, lower
):
    total = reduced(received)
    inside = inside_limits(limits, 0, lower.shape, w)
    value = jnp.concatenate([one[...], two[...]], axis=1)
    lower[...] = jnp.where(inside, value, jnp.zeros_like(value))
    for s in range(2):
        span = slice(s * w, (s + 1) * w)
        here_one = jnp.where(limits[s] > 0, 1.0, 0.0)
        here_two = jnp.where(limits[2 + s] > 0, 1.0, 0.0)
        column = (-(total[:, span] * here_one)).astype(BF16)
        column_one[:, span] = column
        second = total[:, (2 + s) * w : (3 + s) * w] + dot(column, masked_link(w, link, widths, s))
        column_two[:, span] = (-(second * here_two)).astype(BF16)
    for out, sibling in ((mine, place[0]), (other, 1 - place[0])):
        first = pl.ds(pl.multiple_of(sibling * w, w), w)
        second = pl.ds(pl.multiple_of((2 + sibling) * w, w), w)
        out[0] = -dot_t(lower[:, first], column_one[:, first])
        out[1] = dot_t(column_one[:, first], lower[:, second])
        out[2] = -dot_t(lower[:, second], column_two[:, first])


def core_sum_body(w, mine, other, sums):
    lanes = sums.shape[2]
    for b in range(3):
        value = (mine[b] + other[b]).astype(BF16)
        for h in range(w // lanes):
            sums[h, b * w : (b + 1) * w, :] = value[:, h * lanes : (h + 1) * lanes]


def chunk_sum_body(received, copies):
    value = reduced(received).astype(BF16)
    for i in range(copies.shape[0]):
        copies[i] = value


def pivot_body(w, place, one, two, widths, pivot, stack):
    row = lax.broadcasted_iota(jnp.int32, (w, w), 0)
    column = lax.broadcasted_iota(jnp.int32, (w, w), 1)
    lanes = stack.shape[1]
    for b, source, width in (
        (0, one, widths[place[0]]),
        (1, None, 0),
        (2, two, widths[2 + place[0]]),
    ):
        value = jnp.zeros((w, w), F32)
        if source is not None:
            value = jnp.where((row < width) & (column < width), source[place[0]].astype(F32), value)
        for h in range(w // lanes):
            start = (3 * h + b) * w
            stack[start : start + w, :] = value[:, h * lanes : (h + 1) * lanes]
    size = pivot.shape[0]
    pivot[...] = stack[pl.ds(pl.multiple_of(place[1] * size, size), size), :]


def all_sum_body(received, pivot, copies):
    near, chunk = PAIR, received.shape[1]
    for n in range(near):
        total = pivot[n * chunk : (n + 1) * chunk, :]
        for i in range(n, received.shape[0], near):
            total = total + received[i].astype(F32)
        total = total.astype(BF16)
        for i in range(copies.shape[0]):
            copies[i, n * chunk : (n + 1) * chunk, :] = total


def side_by_side(total, b, w):
    span = slice(b * w, (b + 1) * w)
    return jnp.concatenate([total[h, span, :] for h in range(total.shape[0])], axis=1)


def final_body(w, core, mine, other, link, widths, block_one, parent_rows, block_two):
    for total, sibling in ((mine, core[0]), (other, 1 - core[0])):
        tie = masked_link(w, link, widths, sibling)
        block = side_by_side(total, 0, w)
        cross = side_by_side(total, 1, w).astype(F32)
        block_one[sibling] = block
        parent = (-(dot(block, tie) + cross)).astype(BF16)
        parent_rows[sibling] = parent
        rest = side_by_side(total, 2, w).astype(F32) - dot_t(tie, parent)
        block_two[sibling] = rest.astype(BF16)


def local(
    ancestor_inverse,
    panel_one,
    ancestors_one,
    diag_inverse_one,
    panel_two,
    link_two,
    ancestors_two,
    diag_inverse_two,
    widths,
):
    w = diag_inverse_one.shape[-1]
    chips, far_n = lax.axis_size("chip"), lax.axis_size("far")
    planes = far_n * NEAR
    local_rows = ancestor_inverse.shape[0]
    share = panel_one.shape[0]
    chip = lax.axis_index("chip").astype(jnp.int32)
    core = lax.axis_index("core").astype(jnp.int32)
    core_ref = core.reshape(1)
    whole = (share, 4 * w)

    lower = jnp.concatenate([panel_one, panel_two], axis=1)
    places = landing_places(chips, planes)
    pairs = []
    for q in range(chips):
        for k in range(CORES):
            for z in range(planes):
                pairs.append(((q * CORES + k) * planes + z, (places[q][z] * CORES + k) * planes + q))
    moved = lax.ppermute(lower, GRID, pairs)
    parity = lax.axis_index("pair").astype(jnp.int32)
    plane = lax.axis_index("far") * NEAR + lax.axis_index("mid") * PAIR + parity
    order = lax.dynamic_index_in_dim(jnp.array(places, jnp.int32), plane, 0, keepdims=False)
    place = jnp.stack([core, chip])
    flat = (w // LANES, 3 * w, LANES)
    chunk = 3 * w * w // LANES // (chips * PAIR)
    pivot = pl.pallas_call(
        functools.partial(pivot_body, w),
        name="pivot",
        in_specs=[SMEM, VMEM, VMEM, SMEM],
        out_specs=VMEM,
        out_shape=jax.ShapeDtypeStruct((PAIR * chunk, LANES), F32),
        scratch_shapes=[pltpu.VMEM((3 * w * w // LANES, LANES), F32)],
    )(place, diag_inverse_one, diag_inverse_two, widths)
    ancestors = (ancestors_one, ancestors_two)
    limits = column_limits(ancestors, widths, chip * CORES + core)
    away_limits = jnp.concatenate(
        [
            column_limits(ancestors, widths, plane * CORES + core),
            column_limits(ancestors, widths, plane * CORES + 1 - core),
        ]
    )
    moved, order, place, pivot, limits, away_limits = lax.optimization_barrier(
        (moved, order, place, pivot, limits, away_limits)
    )
    (moved,) = kernel_call(copy_body, "copies", [VMEM], [((chips,) + whole, BF16)])(moved)
    mine = exchange(moved, "chip")
    other = swap_cores(mine)

    half = (planes // PAIR,) + whole
    keep, give = pl.pallas_call(
        functools.partial(product_body, w),
        name="product",
        in_specs=[SMEM] * 4 + [VMEM] * 3,
        out_specs=[VMEM] * 2,
        out_shape=[jax.ShapeDtypeStruct(half, BF16)] * 2,
        scratch_shapes=[
            pltpu.VMEM((CORES * chips * share, 4 * w), BF16),
            pltpu.VMEM((planes,) + whole, BF16),
        ],
        compiler_params=pltpu.CompilerParams(vmem_limit_bytes=40 * 1024 * 1024),
    )(core_ref, parity.reshape(1), order, away_limits, ancestor_inverse, mine, other)
    got = lax.ppermute(give, "pair", [(0, 1), (1, 0)])
    (part,) = kernel_call(pair_sum_body, "pair_sum", [VMEM] * 2, [(half, BF16)])(keep, got)
    part = exchange(part, ("far", "mid"))
    column_one, column_two, mine, other = pl.pallas_call(
        functools.partial(column_body, w),
        name="columns",
        in_specs=[SMEM] * 2 + [VMEM] * 4 + [SMEM],
        out_specs=[VMEM] * 4,
        out_shape=[jax.ShapeDtypeStruct((share, 2 * w), BF16)] * 2
        + [jax.ShapeDtypeStruct((3, w, w), F32)] * 2,
        scratch_shapes=[pltpu.VMEM(whole, BF16)],
        compiler_params=pltpu.CompilerParams(vmem_limit_bytes=40 * 1024 * 1024),
    )(place, limits, part, panel_one, panel_two, link_two, widths)
    other = swap_cores(other)
    (sums,) = kernel_call(
        functools.partial(core_sum_body, w), "core_sum", [VMEM] * 2, [(flat, BF16)]
    )(mine, other)
    sums = exchange(sums.reshape(chips * PAIR, chunk, LANES), ("chip", "pair"))
    (sums,) = kernel_call(chunk_sum_body, "chunk_sum", [VMEM], [((planes, chunk, LANES), BF16)])(
        sums
    )
    sums = exchange(sums, ("far", "mid", "pair"))
    (total,) = kernel_call(
        all_sum_body, "all_sum", [VMEM] * 2, [((chips, PAIR * chunk, LANES), BF16)]
    )(sums, pivot)
    mine = exchange(total, "chip").reshape(flat)
    other = swap_cores(mine)
    block_one, parent_rows, block_two = kernel_call(
        functools.partial(final_body, w),
        "final",
        [SMEM, VMEM, VMEM, VMEM, SMEM],
        [((2, w, w), BF16)] * 3,
    )(core_ref, mine, other, link_two, widths)
    return column_one, block_one, column_two, parent_rows, block_two


def solution(mesh):
    rows_n, cols_n = mesh.devices.shape
    sizes = (rows_n // CORES, CORES, cols_n // NEAR, NEAR // PAIR, PAIR)
    fine = Mesh(mesh.devices.reshape(sizes), GRID)
    row, col = GRID[:2], GRID[2:]
    shared = P(GRID, None)
    in_specs = (P(row, col), shared, P(), P(), shared, P(), P(), P(), P())
    out_specs = (shared, P(), shared, P(), P())
    return jax.shard_map(local, mesh=fine, in_specs=in_specs, out_specs=out_specs, check_vma=False)
```

```python
import functools

import jax
import jax.numpy as jnp
from jax import lax
from jax.experimental import pallas as pl
from jax.experimental.pallas import tpu as pltpu
from jax.sharding import Mesh
from jax.sharding import PartitionSpec as P

F32 = jnp.float32
BF16 = jnp.bfloat16
VMEM = pl.BlockSpec(memory_space=pltpu.VMEM)
ANY = pl.BlockSpec(memory_space=pl.ANY)
SMEM = pl.BlockSpec(memory_space=pltpu.SMEM)
NEAR = 4
PAIR = 2
CORES = 2
LANES = 128
GRID = ("chip", "core", "far", "mid", "pair")


def kernel_call(body, name, specs, outs):
    return pl.pallas_call(
        body,
        name=name,
        in_specs=specs,
        out_specs=[VMEM] * len(outs),
        out_shape=[jax.ShapeDtypeStruct(shape, kind) for shape, kind in outs],
        compiler_params=pltpu.CompilerParams(vmem_limit_bytes=40 * 1024 * 1024),
    )


def exchange(blocks, axis):
    return lax.all_to_all(blocks, axis, split_axis=0, concat_axis=0, tiled=True)


def landing_places(chips, planes):
    side = int(chips**0.5)

    def steps(a, b):
        return abs(a // side - b // side) + abs(a % side - b % side)

    places = []
    for q in range(chips):
        far_first = sorted(range(planes), key=lambda z: (-abs(z - q), z))
        close_first = sorted(range(chips), key=lambda p: (steps(p, q), p))
        spots = dict(zip(far_first, close_first))
        places.append([spots[z] for z in range(planes)])
    return places


def swap_cores(block):
    return lax.ppermute(block, "core", [(0, 1), (1, 0)])


def dot(left, right):
    return jnp.dot(left, right, preferred_element_type=F32)


def dot_t(left, right):
    return lax.dot_general(left, right, (((0,), (0,)), ((), ())), preferred_element_type=F32)


def reduced(received):
    total = received[0].astype(F32)
    for i in range(1, received.shape[0]):
        total = total + received[i].astype(F32)
    return total


def column_limits(ancestors, widths, tile):
    here = [jnp.any(table == tile, axis=1) for table in ancestors]
    return jnp.where(jnp.concatenate(here), widths, 0)


def inside_limits(limits, first, shape, w):
    column = lax.broadcasted_iota(jnp.int32, shape, 1)
    limit = jnp.zeros(shape, jnp.int32)
    for k in range(shape[1] // w):
        limit = jnp.where(column >= k * w, limits[first + k] + k * w, limit)
    return column < limit


def masked_link(w, link, widths, s):
    row = lax.broadcasted_iota(jnp.int32, (w, w), 0)
    column = lax.broadcasted_iota(jnp.int32, (w, w), 1)
    value = link[s]
    inside = (row < widths[s]) & (column < widths[2 + s])
    return jnp.where(inside, value, jnp.zeros_like(value))


def copy_body(source, copies):
    value = source[...]
    for i in range(copies.shape[0]):
        copies[i] = value


def product_body(
    w, core, parity, order, limits, inverse, mine, other, keep, give, held, part
):
    blocks, share, _ = mine.shape
    half = blocks * share
    for source, first, start in ((mine, 0, 0), (other, 4, half)):
        inside = inside_limits(limits, first, (share, 4 * w), w)
        for i in range(blocks):
            value = source[order[i]]
            value = jnp.where(inside, value, jnp.zeros_like(value))
            held[start + i * share : start + (i + 1) * share, :] = value
    left = inverse[:, pl.ds(pl.multiple_of(core[0] * half, half), half)]
    right = inverse[:, pl.ds(pl.multiple_of((1 - core[0]) * half, half), half)]
    for k in range(4):
        span = slice(k * w, (k + 1) * w)
        value = (dot(left, held[:half, span]) + dot(right, held[half:, span])).astype(BF16)
        for i in range(part.shape[0]):
            part[i, :, span] = value[i * share : (i + 1) * share]
    for i in range(keep.shape[0]):
        keep[i] = part[PAIR * i + parity[0]]
        give[i] = part[PAIR * i + 1 - parity[0]]


def pair_sum_body(keep, got, sums):
    for i in range(sums.shape[0]):
        sums[i] = (keep[i].astype(F32) + got[i].astype(F32)).astype(BF16)


def column_body(
    w, place, limits, received, one, two, link, widths, column_one, column_two, mine, other, lower
):
    total = reduced(received)
    inside = inside_limits(limits, 0, lower.shape, w)
    value = jnp.concatenate([one[...], two[...]], axis=1)
    lower[...] = jnp.where(inside, value, jnp.zeros_like(value))
    for s in range(2):
        span = slice(s * w, (s + 1) * w)
        here_one = jnp.where(limits[s] > 0, 1.0, 0.0)
        here_two = jnp.where(limits[2 + s] > 0, 1.0, 0.0)
        column = (-(total[:, span] * here_one)).astype(BF16)
        column_one[:, span] = column
        second = total[:, (2 + s) * w : (3 + s) * w] + dot(column, masked_link(w, link, widths, s))
        column_two[:, span] = (-(second * here_two)).astype(BF16)
    for out, sibling in ((mine, place[0]), (other, 1 - place[0])):
        first = pl.ds(pl.multiple_of(sibling * w, w), w)
        second = pl.ds(pl.multiple_of((2 + sibling) * w, w), w)
        out[0] = -dot_t(lower[:, first], column_one[:, first])
        out[1] = dot_t(column_one[:, first], lower[:, second])
        out[2] = -dot_t(lower[:, second], column_two[:, first])


def core_sum_body(w, mine, other, sums):
    lanes = sums.shape[2]
    for b in range(3):
        value = (mine[b] + other[b]).astype(BF16)
        for h in range(w // lanes):
            sums[h, b * w : (b + 1) * w, :] = value[:, h * lanes : (h + 1) * lanes]


def chunk_sum_body(received, copies):
    value = reduced(received).astype(BF16)
    for i in range(copies.shape[0]):
        copies[i] = value


def pivot_body(w, place, one, two, widths, pivot, stack):
    row = lax.broadcasted_iota(jnp.int32, (w, w), 0)
    column = lax.broadcasted_iota(jnp.int32, (w, w), 1)
    lanes = stack.shape[1]
    for b, source, width in (
        (0, one, widths[place[0]]),
        (1, None, 0),
        (2, two, widths[2 + place[0]]),
    ):
        value = jnp.zeros((w, w), F32)
        if source is not None:
            value = jnp.where((row < width) & (column < width), source[place[0]].astype(F32), value)
        for h in range(w // lanes):
            start = (3 * h + b) * w
            stack[start : start + w, :] = value[:, h * lanes : (h + 1) * lanes]
    size = pivot.shape[0]
    pivot[...] = stack[pl.ds(pl.multiple_of(place[1] * size, size), size), :]


def all_sum_body(received, pivot, copies):
    total = (reduced(received) + pivot[...]).astype(BF16)
    for i in range(copies.shape[0]):
        copies[i] = total


def side_by_side(total, b, w):
    span = slice(b * w, (b + 1) * w)
    return jnp.concatenate([total[h, span, :] for h in range(total.shape[0])], axis=1)


def final_body(w, core, mine, other, link, widths, block_one, parent_rows, block_two):
    for total, sibling in ((mine, core[0]), (other, 1 - core[0])):
        tie = masked_link(w, link, widths, sibling)
        block = side_by_side(total, 0, w)
        cross = side_by_side(total, 1, w).astype(F32)
        block_one[sibling] = block
        parent = (-(dot(block, tie) + cross)).astype(BF16)
        parent_rows[sibling] = parent
        rest = side_by_side(total, 2, w).astype(F32) - dot_t(tie, parent)
        block_two[sibling] = rest.astype(BF16)


def local(
    ancestor_inverse,
    panel_one,
    ancestors_one,
    diag_inverse_one,
    panel_two,
    link_two,
    ancestors_two,
    diag_inverse_two,
    widths,
):
    w = diag_inverse_one.shape[-1]
    chips, far_n = lax.axis_size("chip"), lax.axis_size("far")
    planes = far_n * NEAR
    local_rows = ancestor_inverse.shape[0]
    share = panel_one.shape[0]
    chip = lax.axis_index("chip").astype(jnp.int32)
    core = lax.axis_index("core").astype(jnp.int32)
    core_ref = core.reshape(1)
    whole = (share, 4 * w)

    lower = jnp.concatenate([panel_one, panel_two], axis=1)
    places = landing_places(chips, planes)
    pairs = []
    for q in range(chips):
        for k in range(CORES):
            for z in range(planes):
                pairs.append(((q * CORES + k) * planes + z, (places[q][z] * CORES + k) * planes + q))
    moved = lax.ppermute(lower, GRID, pairs)
    parity = lax.axis_index("pair").astype(jnp.int32)
    plane = lax.axis_index("far") * NEAR + lax.axis_index("mid") * PAIR + parity
    order = lax.dynamic_index_in_dim(jnp.array(places, jnp.int32), plane, 0, keepdims=False)
    place = jnp.stack([core, chip * PAIR + parity])
    flat = (w // LANES, 3 * w, LANES)
    chunk = 3 * w * w // LANES // (chips * PAIR)
    pivot = pl.pallas_call(
        functools.partial(pivot_body, w),
        name="pivot",
        in_specs=[SMEM, VMEM, VMEM, SMEM],
        out_specs=VMEM,
        out_shape=jax.ShapeDtypeStruct((chunk, LANES), F32),
        scratch_shapes=[pltpu.VMEM((3 * w * w // LANES, LANES), F32)],
    )(place, diag_inverse_one, diag_inverse_two, widths)
    ancestors = (ancestors_one, ancestors_two)
    limits = column_limits(ancestors, widths, chip * CORES + core)
    away_limits = jnp.concatenate(
        [
            column_limits(ancestors, widths, plane * CORES + core),
            column_limits(ancestors, widths, plane * CORES + 1 - core),
        ]
    )
    moved, order, place, pivot, limits, away_limits = lax.optimization_barrier(
        (moved, order, place, pivot, limits, away_limits)
    )
    (moved,) = kernel_call(copy_body, "copies", [VMEM], [((chips,) + whole, BF16)])(moved)
    mine = exchange(moved, "chip")
    other = swap_cores(mine)

    half = (planes // PAIR,) + whole
    keep, give = pl.pallas_call(
        functools.partial(product_body, w),
        name="product",
        in_specs=[SMEM] * 4 + [VMEM] * 3,
        out_specs=[VMEM] * 2,
        out_shape=[jax.ShapeDtypeStruct(half, BF16)] * 2,
        scratch_shapes=[
            pltpu.VMEM((CORES * chips * share, 4 * w), BF16),
            pltpu.VMEM((planes,) + whole, BF16),
        ],
        compiler_params=pltpu.CompilerParams(vmem_limit_bytes=40 * 1024 * 1024),
    )(core_ref, parity.reshape(1), order, away_limits, ancestor_inverse, mine, other)
    got = lax.ppermute(give, "pair", [(0, 1), (1, 0)])
    (part,) = kernel_call(pair_sum_body, "pair_sum", [VMEM] * 2, [(half, BF16)])(keep, got)
    part = exchange(part, ("far", "mid"))
    column_one, column_two, mine, other = pl.pallas_call(
        functools.partial(column_body, w),
        name="columns",
        in_specs=[SMEM] * 2 + [VMEM] * 4 + [SMEM],
        out_specs=[VMEM] * 4,
        out_shape=[jax.ShapeDtypeStruct((share, 2 * w), BF16)] * 2
        + [jax.ShapeDtypeStruct((3, w, w), F32)] * 2,
        scratch_shapes=[pltpu.VMEM(whole, BF16)],
        compiler_params=pltpu.CompilerParams(vmem_limit_bytes=40 * 1024 * 1024),
    )(place, limits, part, panel_one, panel_two, link_two, widths)
    other = swap_cores(other)
    (sums,) = kernel_call(
        functools.partial(core_sum_body, w), "core_sum", [VMEM] * 2, [(flat, BF16)]
    )(mine, other)
    sums = exchange(sums.reshape(chips * PAIR, chunk, LANES), ("chip", "pair"))
    (sums,) = kernel_call(chunk_sum_body, "chunk_sum", [VMEM], [((planes // PAIR, chunk, LANES), BF16)])(
        sums
    )
    sums = exchange(sums, ("far", "mid"))
    (total,) = kernel_call(
        all_sum_body, "all_sum", [VMEM] * 2, [((chips * PAIR, chunk, LANES), BF16)]
    )(sums, pivot)
    mine = exchange(total, ("chip", "pair")).reshape(flat)
    other = swap_cores(mine)
    block_one, parent_rows, block_two = kernel_call(
        functools.partial(final_body, w),
        "final",
        [SMEM, VMEM, VMEM, VMEM, SMEM],
        [((2, w, w), BF16)] * 3,
    )(core_ref, mine, other, link_two, widths)
    return column_one, block_one, column_two, parent_rows, block_two


def solution(mesh):
    rows_n, cols_n = mesh.devices.shape
    sizes = (rows_n // CORES, CORES, cols_n // NEAR, NEAR // PAIR, PAIR)
    fine = Mesh(mesh.devices.reshape(sizes), GRID)
    row, col = GRID[:2], GRID[2:]
    shared = P(GRID, None)
    in_specs = (P(row, col), shared, P(), P(), shared, P(), P(), P(), P())
    out_specs = (shared, P(), shared, P(), P())
    return jax.shard_map(local, mesh=fine, in_specs=in_specs, out_specs=out_specs, check_vma=False)
```

```python
import functools

import jax
import jax.numpy as jnp
from jax import lax
from jax.experimental import pallas as pl
from jax.experimental.pallas import tpu as pltpu
from jax.sharding import Mesh
from jax.sharding import PartitionSpec as P

F32 = jnp.float32
BF16 = jnp.bfloat16
VMEM = pl.BlockSpec(memory_space=pltpu.VMEM)
ANY = pl.BlockSpec(memory_space=pl.ANY)
SMEM = pl.BlockSpec(memory_space=pltpu.SMEM)
NEAR = 4
PAIR = 2
CORES = 2
LANES = 128
GRID = ("chip", "core", "far", "mid", "pair")


def kernel_call(body, name, specs, outs):
    return pl.pallas_call(
        body,
        name=name,
        in_specs=specs,
        out_specs=[VMEM] * len(outs),
        out_shape=[jax.ShapeDtypeStruct(shape, kind) for shape, kind in outs],
        compiler_params=pltpu.CompilerParams(vmem_limit_bytes=40 * 1024 * 1024),
    )


def exchange(blocks, axis):
    return lax.all_to_all(blocks, axis, split_axis=0, concat_axis=0, tiled=True)


def landing_places(chips, planes):
    side = int(chips**0.5)

    def steps(a, b):
        return abs(a // side - b // side) + abs(a % side - b % side)

    places = []
    for q in range(chips):
        far_first = sorted(range(planes), key=lambda z: (-abs(z - q), z))
        close_first = sorted(range(chips), key=lambda p: (steps(p, q), p))
        spots = dict(zip(far_first, close_first))
        places.append([spots[z] for z in range(planes)])
    return places


def swap_cores(block):
    return lax.ppermute(block, "core", [(0, 1), (1, 0)])


def dot(left, right):
    return jnp.dot(left, right, preferred_element_type=F32)


def dot_t(left, right):
    return lax.dot_general(left, right, (((0,), (0,)), ((), ())), preferred_element_type=F32)


def reduced(received):
    total = received[0].astype(F32)
    for i in range(1, received.shape[0]):
        total = total + received[i].astype(F32)
    return total


def column_limits(ancestors, widths, tile):
    here = [jnp.any(table == tile, axis=1) for table in ancestors]
    return jnp.where(jnp.concatenate(here), widths, 0)


def inside_limits(limits, first, shape, w):
    column = lax.broadcasted_iota(jnp.int32, shape, 1)
    limit = jnp.zeros(shape, jnp.int32)
    for k in range(shape[1] // w):
        limit = jnp.where(column >= k * w, limits[first + k] + k * w, limit)
    return column < limit


def masked_link(w, link, widths, s):
    row = lax.broadcasted_iota(jnp.int32, (w, w), 0)
    column = lax.broadcasted_iota(jnp.int32, (w, w), 1)
    value = link[s]
    inside = (row < widths[s]) & (column < widths[2 + s])
    return jnp.where(inside, value, jnp.zeros_like(value))


def copy_body(source, copies):
    value = source[...]
    for i in range(copies.shape[0]):
        copies[i] = value


def masked_tile(source, order, limits, first, held):
    blocks, share, wide = source.shape
    inside = inside_limits(limits, first, (share, wide), wide // 4)
    for i in range(blocks):
        value = source[order[i]]
        held[i * share : (i + 1) * share, :] = jnp.where(inside, value, jnp.zeros_like(value))


def own_product_body(w, core, order, limits, inverse, mine, part, held):
    masked_tile(mine, order, limits, 0, held)
    half = held.shape[0]
    left = inverse[:, pl.ds(pl.multiple_of(core[0] * half, half), half)]
    for k in range(4):
        span = slice(k * w, (k + 1) * w)
        part[:, span] = dot(left, held[:, span])


def product_body(
    w, core, parity, order, limits, inverse, other, own, keep, give, held, part
):
    masked_tile(other, order, limits, 4, held)
    half, share = held.shape[0], part.shape[1]
    right = inverse[:, pl.ds(pl.multiple_of((1 - core[0]) * half, half), half)]
    for k in range(4):
        span = slice(k * w, (k + 1) * w)
        value = (own[:, span] + dot(right, held[:, span])).astype(BF16)
        for i in range(part.shape[0]):
            part[i, :, span] = value[i * share : (i + 1) * share]
    for i in range(keep.shape[0]):
        keep[i] = part[PAIR * i + parity[0]]
        give[i] = part[PAIR * i + 1 - parity[0]]


def pair_sum_body(keep, got, sums):
    for i in range(sums.shape[0]):
        sums[i] = (keep[i].astype(F32) + got[i].astype(F32)).astype(BF16)


def column_body(
    w, place, limits, received, one, two, link, widths, column_one, column_two, other, lower
):
    total = reduced(received)
    inside = inside_limits(limits, 0, lower.shape, w)
    value = jnp.concatenate([one[...], two[...]], axis=1)
    lower[...] = jnp.where(inside, value, jnp.zeros_like(value))
    for s in range(2):
        span = slice(s * w, (s + 1) * w)
        here_one = jnp.where(limits[s] > 0, 1.0, 0.0)
        here_two = jnp.where(limits[2 + s] > 0, 1.0, 0.0)
        column = (-(total[:, span] * here_one)).astype(BF16)
        column_one[:, span] = column
        second = total[:, (2 + s) * w : (3 + s) * w] + dot(column, masked_link(w, link, widths, s))
        column_two[:, span] = (-(second * here_two)).astype(BF16)
    sibling_sums(w, 1 - place[0], lower, column_one, column_two, other)


def sibling_sums(w, sibling, lower, column_one, column_two, out):
    first = pl.ds(pl.multiple_of(sibling * w, w), w)
    second = pl.ds(pl.multiple_of((2 + sibling) * w, w), w)
    out[0] = -dot_t(lower[:, first], column_one[:, first])
    out[1] = dot_t(column_one[:, first], lower[:, second])
    out[2] = -dot_t(lower[:, second], column_two[:, first])


def own_sums_body(w, place, lower, column_one, column_two, mine):
    sibling_sums(w, place[0], lower, column_one, column_two, mine)


def core_sum_body(w, mine, other, sums):
    lanes = sums.shape[2]
    for b in range(3):
        value = (mine[b] + other[b]).astype(BF16)
        for h in range(w // lanes):
            sums[h, b * w : (b + 1) * w, :] = value[:, h * lanes : (h + 1) * lanes]


def chunk_sum_body(received, copies):
    value = reduced(received).astype(BF16)
    for i in range(copies.shape[0]):
        copies[i] = value


def pivot_body(w, place, one, two, widths, pivot, stack):
    row = lax.broadcasted_iota(jnp.int32, (w, w), 0)
    column = lax.broadcasted_iota(jnp.int32, (w, w), 1)
    lanes = stack.shape[1]
    for b, source, width in (
        (0, one, widths[place[0]]),
        (1, None, 0),
        (2, two, widths[2 + place[0]]),
    ):
        value = jnp.zeros((w, w), F32)
        if source is not None:
            value = jnp.where((row < width) & (column < width), source[place[0]].astype(F32), value)
        for h in range(w // lanes):
            start = (3 * h + b) * w
            stack[start : start + w, :] = value[:, h * lanes : (h + 1) * lanes]
    size = pivot.shape[0]
    pivot[...] = stack[pl.ds(pl.multiple_of(place[1] * size, size), size), :]


def all_sum_body(received, pivot, copies):
    total = (reduced(received) + pivot[...]).astype(BF16)
    for i in range(copies.shape[0]):
        copies[i] = total


def side_by_side(total, b, w):
    span = slice(b * w, (b + 1) * w)
    return jnp.concatenate([total[h, span, :] for h in range(total.shape[0])], axis=1)


def sibling_blocks(w, total, link, widths, sibling):
    tie = masked_link(w, link, widths, sibling)
    block = side_by_side(total, 0, w)
    cross = side_by_side(total, 1, w).astype(F32)
    parent = (-(dot(block, tie) + cross)).astype(BF16)
    rest = side_by_side(total, 2, w).astype(F32) - dot_t(tie, parent)
    return block, parent, rest.astype(BF16)


def own_final_body(w, core, mine, link, widths, *outs):
    for out, value in zip(outs, sibling_blocks(w, mine, link, widths, core[0])):
        out[...] = value


def final_body(w, core, other, own_one, own_parent, own_two, link, widths, *outs):
    values = sibling_blocks(w, other, link, widths, 1 - core[0])
    for out, own, value in zip(outs, (own_one, own_parent, own_two), values):
        out[core[0]] = own[...]
        out[1 - core[0]] = value


def local(
    ancestor_inverse,
    panel_one,
    ancestors_one,
    diag_inverse_one,
    panel_two,
    link_two,
    ancestors_two,
    diag_inverse_two,
    widths,
):
    w = diag_inverse_one.shape[-1]
    chips, far_n = lax.axis_size("chip"), lax.axis_size("far")
    planes = far_n * NEAR
    local_rows = ancestor_inverse.shape[0]
    share = panel_one.shape[0]
    chip = lax.axis_index("chip").astype(jnp.int32)
    core = lax.axis_index("core").astype(jnp.int32)
    core_ref = core.reshape(1)
    whole = (share, 4 * w)

    lower = jnp.concatenate([panel_one, panel_two], axis=1)
    places = landing_places(chips, planes)
    pairs = []
    for q in range(chips):
        for k in range(CORES):
            for z in range(planes):
                pairs.append(((q * CORES + k) * planes + z, (places[q][z] * CORES + k) * planes + q))
    moved = lax.ppermute(lower, GRID, pairs)
    parity = lax.axis_index("pair").astype(jnp.int32)
    plane = lax.axis_index("far") * NEAR + lax.axis_index("mid") * PAIR + parity
    order = lax.dynamic_index_in_dim(jnp.array(places, jnp.int32), plane, 0, keepdims=False)
    place = jnp.stack([core, chip * PAIR + parity])
    flat = (w // LANES, 3 * w, LANES)
    chunk = 3 * w * w // LANES // (chips * PAIR)
    pivot = pl.pallas_call(
        functools.partial(pivot_body, w),
        name="pivot",
        in_specs=[SMEM, VMEM, VMEM, SMEM],
        out_specs=VMEM,
        out_shape=jax.ShapeDtypeStruct((chunk, LANES), F32),
        scratch_shapes=[pltpu.VMEM((3 * w * w // LANES, LANES), F32)],
    )(place, diag_inverse_one, diag_inverse_two, widths)
    ancestors = (ancestors_one, ancestors_two)
    limits = column_limits(ancestors, widths, chip * CORES + core)
    away_limits = jnp.concatenate(
        [
            column_limits(ancestors, widths, plane * CORES + core),
            column_limits(ancestors, widths, plane * CORES + 1 - core),
        ]
    )
    moved, order, place, pivot, limits, away_limits = lax.optimization_barrier(
        (moved, order, place, pivot, limits, away_limits)
    )
    (moved,) = kernel_call(copy_body, "copies", [VMEM], [((chips,) + whole, BF16)])(moved)
    mine = exchange(moved, "chip")
    other = swap_cores(mine)

    half = (planes // PAIR,) + whole
    grant = pltpu.CompilerParams(vmem_limit_bytes=40 * 1024 * 1024)
    tile_rows = (chips * share, 4 * w)
    own = pl.pallas_call(
        functools.partial(own_product_body, w),
        name="own_product",
        in_specs=[SMEM] * 3 + [VMEM] * 2,
        out_specs=VMEM,
        out_shape=jax.ShapeDtypeStruct((local_rows, 4 * w), F32),
        scratch_shapes=[pltpu.VMEM(tile_rows, BF16)],
        compiler_params=grant,
    )(core_ref, order, away_limits, ancestor_inverse, mine)
    other, own = lax.optimization_barrier((other, own))
    keep, give = pl.pallas_call(
        functools.partial(product_body, w),
        name="product",
        in_specs=[SMEM] * 4 + [VMEM] * 3,
        out_specs=[VMEM] * 2,
        out_shape=[jax.ShapeDtypeStruct(half, BF16)] * 2,
        scratch_shapes=[pltpu.VMEM(tile_rows, BF16), pltpu.VMEM((planes,) + whole, BF16)],
        compiler_params=grant,
    )(core_ref, parity.reshape(1), order, away_limits, ancestor_inverse, other, own)
    got = lax.ppermute(give, "pair", [(0, 1), (1, 0)])
    (part,) = kernel_call(pair_sum_body, "pair_sum", [VMEM] * 2, [(half, BF16)])(keep, got)
    part = exchange(part, ("far", "mid"))
    column_one, column_two, other, lower = pl.pallas_call(
        functools.partial(column_body, w),
        name="columns",
        in_specs=[SMEM] * 2 + [VMEM] * 4 + [SMEM],
        out_specs=[VMEM] * 4,
        out_shape=[jax.ShapeDtypeStruct((share, 2 * w), BF16)] * 2
        + [jax.ShapeDtypeStruct((3, w, w), F32), jax.ShapeDtypeStruct(whole, BF16)],
        compiler_params=grant,
    )(place, limits, part, panel_one, panel_two, link_two, widths)
    mine = pl.pallas_call(
        functools.partial(own_sums_body, w),
        name="own_sums",
        in_specs=[SMEM] + [VMEM] * 3,
        out_specs=VMEM,
        out_shape=jax.ShapeDtypeStruct((3, w, w), F32),
        compiler_params=grant,
    )(place, lower, column_one, column_two)
    other = swap_cores(other)
    (sums,) = kernel_call(
        functools.partial(core_sum_body, w), "core_sum", [VMEM] * 2, [(flat, BF16)]
    )(mine, other)
    sums = exchange(sums.reshape(chips * PAIR, chunk, LANES), ("chip", "pair"))
    (sums,) = kernel_call(chunk_sum_body, "chunk_sum", [VMEM], [((planes // PAIR, chunk, LANES), BF16)])(
        sums
    )
    sums = exchange(sums, ("far", "mid"))
    (total,) = kernel_call(
        all_sum_body, "all_sum", [VMEM] * 2, [((chips * PAIR, chunk, LANES), BF16)]
    )(sums, pivot)
    mine = exchange(total, ("chip", "pair")).reshape(flat)
    other = swap_cores(mine)
    own_blocks = kernel_call(
        functools.partial(own_final_body, w), "own_final", [SMEM, VMEM, VMEM, SMEM], [((w, w), BF16)] * 3
    )(core_ref, mine, link_two, widths)
    other, *own_blocks = lax.optimization_barrier((other, *own_blocks))
    block_one, parent_rows, block_two = kernel_call(
        functools.partial(final_body, w),
        "final",
        [SMEM] + [VMEM] * 5 + [SMEM],
        [((2, w, w), BF16)] * 3,
    )(core_ref, other, *own_blocks, link_two, widths)
    return column_one, block_one, column_two, parent_rows, block_two


def solution(mesh):
    rows_n, cols_n = mesh.devices.shape
    sizes = (rows_n // CORES, CORES, cols_n // NEAR, NEAR // PAIR, PAIR)
    fine = Mesh(mesh.devices.reshape(sizes), GRID)
    row, col = GRID[:2], GRID[2:]
    shared = P(GRID, None)
    in_specs = (P(row, col), shared, P(), P(), shared, P(), P(), P(), P())
    out_specs = (shared, P(), shared, P(), P())
    return jax.shard_map(local, mesh=fine, in_specs=in_specs, out_specs=out_specs, check_vma=False)
```

```python
import functools

import jax
import jax.numpy as jnp
from jax import lax
from jax.experimental import pallas as pl
from jax.experimental.pallas import tpu as pltpu
from jax.sharding import Mesh
from jax.sharding import PartitionSpec as P

F32 = jnp.float32
BF16 = jnp.bfloat16
VMEM = pl.BlockSpec(memory_space=pltpu.VMEM)
ANY = pl.BlockSpec(memory_space=pl.ANY)
SMEM = pl.BlockSpec(memory_space=pltpu.SMEM)
NEAR = 4
PAIR = 2
CORES = 2
LANES = 128
GRID = ("chip", "core", "far", "mid", "pair")


def kernel_call(body, name, specs, outs):
    return pl.pallas_call(
        body,
        name=name,
        in_specs=specs,
        out_specs=[VMEM] * len(outs),
        out_shape=[jax.ShapeDtypeStruct(shape, kind) for shape, kind in outs],
        compiler_params=pltpu.CompilerParams(vmem_limit_bytes=40 * 1024 * 1024),
    )


def exchange(blocks, axis):
    return lax.all_to_all(blocks, axis, split_axis=0, concat_axis=0, tiled=True)


def landing_places(chips, planes):
    side = int(chips**0.5)

    def steps(a, b):
        return abs(a // side - b // side) + abs(a % side - b % side)

    places = []
    for q in range(chips):
        far_first = sorted(range(planes), key=lambda z: (-abs(z - q), z))
        close_first = sorted(range(chips), key=lambda p: (steps(p, q), p))
        spots = dict(zip(far_first, close_first))
        places.append([spots[z] for z in range(planes)])
    return places


def swap_cores(block):
    return lax.ppermute(block, "core", [(0, 1), (1, 0)])


def dot(left, right):
    return jnp.dot(left, right, preferred_element_type=F32)


def dot_t(left, right):
    return lax.dot_general(left, right, (((0,), (0,)), ((), ())), preferred_element_type=F32)


def reduced(received):
    total = received[0].astype(F32)
    for i in range(1, received.shape[0]):
        total = total + received[i].astype(F32)
    return total


def column_limits(ancestors, widths, tile):
    here = [jnp.any(table == tile, axis=1) for table in ancestors]
    return jnp.where(jnp.concatenate(here), widths, 0)


def inside_limits(limits, first, shape, w):
    column = lax.broadcasted_iota(jnp.int32, shape, 1)
    limit = jnp.zeros(shape, jnp.int32)
    for k in range(shape[1] // w):
        limit = jnp.where(column >= k * w, limits[first + k] + k * w, limit)
    return column < limit


def masked_link(w, link, widths, s):
    row = lax.broadcasted_iota(jnp.int32, (w, w), 0)
    column = lax.broadcasted_iota(jnp.int32, (w, w), 1)
    value = link[s]
    inside = (row < widths[s]) & (column < widths[2 + s])
    return jnp.where(inside, value, jnp.zeros_like(value))


def copy_body(source, copies):
    value = source[...]
    for i in range(copies.shape[0]):
        copies[i] = value


def product_body(
    w, core, parity, order, limits, inverse, mine, other, keep, give, held, part
):
    blocks, share, _ = mine.shape
    half = blocks * share
    for source, first, start in ((mine, 0, 0), (other, 4, half)):
        inside = inside_limits(limits, first, (share, 4 * w), w)
        for i in range(blocks):
            value = source[order[i]]
            value = jnp.where(inside, value, jnp.zeros_like(value))
            held[start + i * share : start + (i + 1) * share, :] = value
    left = inverse[:, pl.ds(pl.multiple_of(core[0] * half, half), half)]
    right = inverse[:, pl.ds(pl.multiple_of((1 - core[0]) * half, half), half)]
    for k in range(4):
        span = slice(k * w, (k + 1) * w)
        value = (dot(left, held[:half, span]) + dot(right, held[half:, span])).astype(BF16)
        for i in range(part.shape[0]):
            part[i, :, span] = value[i * share : (i + 1) * share]
    for i in range(keep.shape[0]):
        keep[i] = part[PAIR * i + parity[0]]
        give[i] = part[PAIR * i + 1 - parity[0]]


def pair_sum_body(keep, got, sums):
    for i in range(sums.shape[0]):
        sums[i] = (keep[i].astype(F32) + got[i].astype(F32)).astype(BF16)


def column_body(w, place, limits, received, link, widths, column_one, column_two, own, give):
    total = reduced(received)
    for s in range(2):
        span = slice(s * w, (s + 1) * w)
        here_one = jnp.where(limits[s] > 0, 1.0, 0.0)
        here_two = jnp.where(limits[2 + s] > 0, 1.0, 0.0)
        column = (-(total[:, span] * here_one)).astype(BF16)
        column_one[:, span] = column
        second = total[:, (2 + s) * w : (3 + s) * w] + dot(column, masked_link(w, link, widths, s))
        column_two[:, span] = (-(second * here_two)).astype(BF16)
    for out, sibling in ((own, place[0]), (give, 1 - place[0])):
        span = pl.ds(pl.multiple_of(sibling * w, w), w)
        out[:, :w] = column_one[:, span]
        out[:, w:] = column_two[:, span]


def sums_body(w, place, limits, own, got, lower, partner, sums, columns, panels):
    share, lanes, sibling = own.shape[0], sums.shape[2], place[0]
    column = lax.broadcasted_iota(jnp.int32, (share, w), 1)
    for n, (new, panel) in enumerate(((own, lower), (got, partner))):
        rows = slice(n * share, (n + 1) * share)
        columns[rows, :] = new[...]
        for b in range(2):
            value = panel[:, pl.ds(pl.multiple_of((2 * b + sibling) * w, w), w)]
            inside = column < limits[4 * n + 2 * b + sibling]
            panels[rows, b * w : (b + 1) * w] = jnp.where(inside, value, jnp.zeros_like(value))
    first, second = slice(0, w), slice(w, 2 * w)
    totals = (
        -dot_t(panels[:, first], columns[:, first]),
        dot_t(columns[:, first], panels[:, second]),
        -dot_t(panels[:, second], columns[:, second]),
    )
    for b in range(3):
        value = totals[b].astype(BF16)
        for h in range(w // lanes):
            sums[h, b * w : (b + 1) * w, :] = value[:, h * lanes : (h + 1) * lanes]


def chunk_sum_body(received, copies):
    value = reduced(received).astype(BF16)
    for i in range(copies.shape[0]):
        copies[i] = value


def pivot_body(w, place, one, two, widths, pivot, stack):
    row = lax.broadcasted_iota(jnp.int32, (w, w), 0)
    column = lax.broadcasted_iota(jnp.int32, (w, w), 1)
    lanes = stack.shape[1]
    for b, source, width in (
        (0, one, widths[place[0]]),
        (1, None, 0),
        (2, two, widths[2 + place[0]]),
    ):
        value = jnp.zeros((w, w), F32)
        if source is not None:
            value = jnp.where((row < width) & (column < width), source[place[0]].astype(F32), value)
        for h in range(w // lanes):
            start = (3 * h + b) * w
            stack[start : start + w, :] = value[:, h * lanes : (h + 1) * lanes]
    size = pivot.shape[0]
    pivot[...] = stack[pl.ds(pl.multiple_of(place[1] * size, size), size), :]


def all_sum_body(received, pivot, copies):
    total = (reduced(received) + pivot[...]).astype(BF16)
    for i in range(copies.shape[0]):
        copies[i] = total


def side_by_side(total, b, w):
    span = slice(b * w, (b + 1) * w)
    return jnp.concatenate([total[h, span, :] for h in range(total.shape[0])], axis=1)


def final_body(w, core, mine, other, link, widths, block_one, parent_rows, block_two):
    for total, sibling in ((mine, core[0]), (other, 1 - core[0])):
        tie = masked_link(w, link, widths, sibling)
        block = side_by_side(total, 0, w)
        cross = side_by_side(total, 1, w).astype(F32)
        block_one[sibling] = block
        parent = (-(dot(block, tie) + cross)).astype(BF16)
        parent_rows[sibling] = parent
        rest = side_by_side(total, 2, w).astype(F32) - dot_t(tie, parent)
        block_two[sibling] = rest.astype(BF16)


def local(
    ancestor_inverse,
    panel_one,
    ancestors_one,
    diag_inverse_one,
    panel_two,
    link_two,
    ancestors_two,
    diag_inverse_two,
    widths,
):
    w = diag_inverse_one.shape[-1]
    chips, far_n = lax.axis_size("chip"), lax.axis_size("far")
    planes = far_n * NEAR
    local_rows = ancestor_inverse.shape[0]
    share = panel_one.shape[0]
    chip = lax.axis_index("chip").astype(jnp.int32)
    core = lax.axis_index("core").astype(jnp.int32)
    core_ref = core.reshape(1)
    whole = (share, 4 * w)

    lower = jnp.concatenate([panel_one, panel_two], axis=1)
    places = landing_places(chips, planes)
    pairs = []
    for q in range(chips):
        for k in range(CORES):
            for z in range(planes):
                pairs.append(((q * CORES + k) * planes + z, (places[q][z] * CORES + k) * planes + q))
    moved = lax.ppermute(lower, GRID, pairs)
    parity = lax.axis_index("pair").astype(jnp.int32)
    plane = lax.axis_index("far") * NEAR + lax.axis_index("mid") * PAIR + parity
    order = lax.dynamic_index_in_dim(jnp.array(places, jnp.int32), plane, 0, keepdims=False)
    place = jnp.stack([core, chip * PAIR + parity])
    flat = (w // LANES, 3 * w, LANES)
    chunk = 3 * w * w // LANES // (chips * PAIR)
    pivot = pl.pallas_call(
        functools.partial(pivot_body, w),
        name="pivot",
        in_specs=[SMEM, VMEM, VMEM, SMEM],
        out_specs=VMEM,
        out_shape=jax.ShapeDtypeStruct((chunk, LANES), F32),
        scratch_shapes=[pltpu.VMEM((3 * w * w // LANES, LANES), F32)],
    )(place, diag_inverse_one, diag_inverse_two, widths)
    ancestors = (ancestors_one, ancestors_two)
    limits = jnp.concatenate(
        [
            column_limits(ancestors, widths, chip * CORES + core),
            column_limits(ancestors, widths, chip * CORES + 1 - core),
        ]
    )
    away_limits = jnp.concatenate(
        [
            column_limits(ancestors, widths, plane * CORES + core),
            column_limits(ancestors, widths, plane * CORES + 1 - core),
        ]
    )
    moved, order, place, pivot, limits, away_limits = lax.optimization_barrier(
        (moved, order, place, pivot, limits, away_limits)
    )
    (moved,) = kernel_call(copy_body, "copies", [VMEM], [((chips,) + whole, BF16)])(moved)
    mine = exchange(moved, "chip")
    other = swap_cores(mine)

    half = (planes // PAIR,) + whole
    keep, give = pl.pallas_call(
        functools.partial(product_body, w),
        name="product",
        in_specs=[SMEM] * 4 + [VMEM] * 3,
        out_specs=[VMEM] * 2,
        out_shape=[jax.ShapeDtypeStruct(half, BF16)] * 2,
        scratch_shapes=[
            pltpu.VMEM((CORES * chips * share, 4 * w), BF16),
            pltpu.VMEM((planes,) + whole, BF16),
        ],
        compiler_params=pltpu.CompilerParams(vmem_limit_bytes=40 * 1024 * 1024),
    )(core_ref, parity.reshape(1), order, away_limits, ancestor_inverse, mine, other)
    got = lax.ppermute(give, "pair", [(0, 1), (1, 0)])
    got, partner = lax.optimization_barrier((got, swap_cores(lower)))
    (part,) = kernel_call(pair_sum_body, "pair_sum", [VMEM] * 2, [(half, BF16)])(keep, got)
    part = exchange(part, ("far", "mid"))
    column_one, column_two, own, give = kernel_call(
        functools.partial(column_body, w),
        "columns",
        [SMEM] * 2 + [VMEM] * 2 + [SMEM],
        [((share, 2 * w), BF16)] * 4,
    )(place, limits, part, link_two, widths)
    sums = pl.pallas_call(
        functools.partial(sums_body, w),
        name="sums",
        in_specs=[SMEM] * 2 + [VMEM] * 4,
        out_specs=VMEM,
        out_shape=jax.ShapeDtypeStruct(flat, BF16),
        scratch_shapes=[pltpu.VMEM((CORES * share, 2 * w), BF16)] * 2,
        compiler_params=pltpu.CompilerParams(vmem_limit_bytes=40 * 1024 * 1024),
    )(place, limits, own, swap_cores(give), lower, partner)
    sums = exchange(sums.reshape(chips * PAIR, chunk, LANES), ("chip", "pair"))
    (sums,) = kernel_call(chunk_sum_body, "chunk_sum", [VMEM], [((planes // PAIR, chunk, LANES), BF16)])(
        sums
    )
    sums = exchange(sums, ("far", "mid"))
    (total,) = kernel_call(
        all_sum_body, "all_sum", [VMEM] * 2, [((chips * PAIR, chunk, LANES), BF16)]
    )(sums, pivot)
    mine = exchange(total, ("chip", "pair")).reshape(flat)
    other = swap_cores(mine)
    block_one, parent_rows, block_two = kernel_call(
        functools.partial(final_body, w),
        "final",
        [SMEM, VMEM, VMEM, VMEM, SMEM],
        [((2, w, w), BF16)] * 3,
    )(core_ref, mine, other, link_two, widths)
    return column_one, block_one, column_two, parent_rows, block_two


def solution(mesh):
    rows_n, cols_n = mesh.devices.shape
    sizes = (rows_n // CORES, CORES, cols_n // NEAR, NEAR // PAIR, PAIR)
    fine = Mesh(mesh.devices.reshape(sizes), GRID)
    row, col = GRID[:2], GRID[2:]
    shared = P(GRID, None)
    in_specs = (P(row, col), shared, P(), P(), shared, P(), P(), P(), P())
    out_specs = (shared, P(), shared, P(), P())
    return jax.shard_map(local, mesh=fine, in_specs=in_specs, out_specs=out_specs, check_vma=False)
```

```python
import functools

import jax
import jax.numpy as jnp
from jax import lax
from jax.experimental import pallas as pl
from jax.experimental.pallas import tpu as pltpu
from jax.sharding import Mesh
from jax.sharding import PartitionSpec as P

F32 = jnp.float32
BF16 = jnp.bfloat16
VMEM = pl.BlockSpec(memory_space=pltpu.VMEM)
ANY = pl.BlockSpec(memory_space=pl.ANY)
SMEM = pl.BlockSpec(memory_space=pltpu.SMEM)
NEAR = 4
PAIR = 2
CORES = 2
LANES = 128
GRID = ("chip", "core", "far", "mid", "pair")


def kernel_call(body, name, specs, outs):
    return pl.pallas_call(
        body,
        name=name,
        in_specs=specs,
        out_specs=[VMEM] * len(outs),
        out_shape=[jax.ShapeDtypeStruct(shape, kind) for shape, kind in outs],
        compiler_params=pltpu.CompilerParams(vmem_limit_bytes=40 * 1024 * 1024),
    )


def exchange(blocks, axis):
    return lax.all_to_all(blocks, axis, split_axis=0, concat_axis=0, tiled=True)


def landing_places(chips, planes):
    side = int(chips**0.5)

    def steps(a, b):
        return abs(a // side - b // side) + abs(a % side - b % side)

    places = []
    for q in range(chips):
        far_first = sorted(range(planes), key=lambda z: (-abs(z - q), z))
        close_first = sorted(range(chips), key=lambda p: (steps(p, q), p))
        spots = dict(zip(far_first, close_first))
        places.append([spots[z] for z in range(planes)])
    return places


def swap_cores(block):
    return lax.ppermute(block, "core", [(0, 1), (1, 0)])


def dot(left, right):
    return jnp.dot(left, right, preferred_element_type=F32)


def dot_t(left, right):
    return lax.dot_general(left, right, (((0,), (0,)), ((), ())), preferred_element_type=F32)


def reduced(received):
    total = received[0].astype(F32)
    for i in range(1, received.shape[0]):
        total = total + received[i].astype(F32)
    return total


def column_limits(ancestors, widths, tile):
    here = [jnp.any(table == tile, axis=1) for table in ancestors]
    return jnp.where(jnp.concatenate(here), widths, 0)


def inside_limits(limits, first, shape, w):
    column = lax.broadcasted_iota(jnp.int32, shape, 1)
    limit = jnp.zeros(shape, jnp.int32)
    for k in range(shape[1] // w):
        limit = jnp.where(column >= k * w, limits[first + k] + k * w, limit)
    return column < limit


def masked_link(w, link, widths, s):
    row = lax.broadcasted_iota(jnp.int32, (w, w), 0)
    column = lax.broadcasted_iota(jnp.int32, (w, w), 1)
    value = link[s]
    inside = (row < widths[s]) & (column < widths[2 + s])
    return jnp.where(inside, value, jnp.zeros_like(value))


def copy_body(source, copies):
    value = source[...]
    for i in range(copies.shape[0]):
        copies[i] = value


def product_body(
    w, core, parity, order, limits, inverse, mine, other, keep, give, held, part
):
    blocks, share, _ = mine.shape
    half = blocks * share
    for source, first, start in ((mine, 0, 0), (other, 4, half)):
        inside = inside_limits(limits, first, (share, 4 * w), w)
        for i in range(blocks):
            value = source[order[i]]
            value = jnp.where(inside, value, jnp.zeros_like(value))
            held[start + i * share : start + (i + 1) * share, :] = value
    left = inverse[:, pl.ds(pl.multiple_of(core[0] * half, half), half)]
    right = inverse[:, pl.ds(pl.multiple_of((1 - core[0]) * half, half), half)]
    for k in range(4):
        span = slice(k * w, (k + 1) * w)
        value = (dot(left, held[:half, span]) + dot(right, held[half:, span])).astype(BF16)
        for i in range(part.shape[0]):
            part[i, :, span] = value[i * share : (i + 1) * share]
    for i in range(keep.shape[0]):
        keep[i] = part[PAIR * i + parity[0]]
        give[i] = part[PAIR * i + 1 - parity[0]]


def pair_sum_body(keep, got, sums):
    for i in range(sums.shape[0]):
        sums[i] = (keep[i].astype(F32) + got[i].astype(F32)).astype(BF16)


def column_body(w, place, limits, received, link, widths, column_one, column_two, packed):
    total = reduced(received)
    for s in range(2):
        span = slice(s * w, (s + 1) * w)
        here_one = jnp.where(limits[4 * place[0] + s] > 0, 1.0, 0.0)
        here_two = jnp.where(limits[4 * place[0] + 2 + s] > 0, 1.0, 0.0)
        column = (-(total[:, span] * here_one)).astype(BF16)
        column_one[:, span] = column
        second = total[:, (2 + s) * w : (3 + s) * w] + dot(column, masked_link(w, link, widths, s))
        column_two[:, span] = (-(second * here_two)).astype(BF16)
    for n in range(packed.shape[0]):
        span = slice((n // PAIR) * w, (n // PAIR + 1) * w)
        packed[n, :, :w] = column_one[:, span]
        packed[n, :, w:] = column_two[:, span]


def sums_body(w, place, limits, received, lowers, sums, columns, panels):
    share, sibling = received.shape[1], place[0]
    column = lax.broadcasted_iota(jnp.int32, (share, w), 1)
    for n in range(received.shape[0]):
        rows = slice(n * share, (n + 1) * share)
        columns[rows, :] = received[n]
        for b in range(2):
            value = lowers[n, :, pl.ds(pl.multiple_of((2 * b + sibling) * w, w), w)]
            inside = column < limits[4 * (n // PAIR) + 2 * b + sibling]
            panels[rows, b * w : (b + 1) * w] = jnp.where(inside, value, jnp.zeros_like(value))
    start = pl.multiple_of(place[2] * LANES, LANES)
    low, high = pl.ds(start, LANES), pl.ds(pl.multiple_of(w + start, LANES), LANES)
    sums[0:w, :] = (-dot_t(panels[:, :w], columns[:, low])).astype(BF16)
    sums[w : 2 * w, :] = dot_t(columns[:, :w], panels[:, high]).astype(BF16)
    sums[2 * w :, :] = (-dot_t(panels[:, w:], columns[:, high])).astype(BF16)


def chunk_sum_body(received, copies):
    value = reduced(received).astype(BF16)
    for i in range(copies.shape[0]):
        copies[i] = value


def pivot_body(w, place, one, two, widths, pivot, stack):
    row = lax.broadcasted_iota(jnp.int32, (w, w), 0)
    column = lax.broadcasted_iota(jnp.int32, (w, w), 1)
    lanes = stack.shape[1]
    for b, source, width in (
        (0, one, widths[place[0]]),
        (1, None, 0),
        (2, two, widths[2 + place[0]]),
    ):
        value = jnp.zeros((w, w), F32)
        if source is not None:
            value = jnp.where((row < width) & (column < width), source[place[0]].astype(F32), value)
        for h in range(w // lanes):
            start = (3 * h + b) * w
            stack[start : start + w, :] = value[:, h * lanes : (h + 1) * lanes]
    size = pivot.shape[0]
    pivot[...] = stack[pl.ds(pl.multiple_of(place[1] * size, size), size), :]


def all_sum_body(received, pivot, copies):
    total = (reduced(received) + pivot[...]).astype(BF16)
    for i in range(copies.shape[0]):
        copies[i] = total


def side_by_side(total, b, w):
    span = slice(b * w, (b + 1) * w)
    return jnp.concatenate([total[h, span, :] for h in range(total.shape[0])], axis=1)


def final_body(w, core, mine, other, link, widths, block_one, parent_rows, block_two):
    for total, sibling in ((mine, core[0]), (other, 1 - core[0])):
        tie = masked_link(w, link, widths, sibling)
        block = side_by_side(total, 0, w)
        cross = side_by_side(total, 1, w).astype(F32)
        block_one[sibling] = block
        parent = (-(dot(block, tie) + cross)).astype(BF16)
        parent_rows[sibling] = parent
        rest = side_by_side(total, 2, w).astype(F32) - dot_t(tie, parent)
        block_two[sibling] = rest.astype(BF16)


def local(
    ancestor_inverse,
    panel_one,
    ancestors_one,
    diag_inverse_one,
    panel_two,
    link_two,
    ancestors_two,
    diag_inverse_two,
    widths,
):
    w = diag_inverse_one.shape[-1]
    chips, far_n = lax.axis_size("chip"), lax.axis_size("far")
    planes = far_n * NEAR
    local_rows = ancestor_inverse.shape[0]
    share = panel_one.shape[0]
    chip = lax.axis_index("chip").astype(jnp.int32)
    core = lax.axis_index("core").astype(jnp.int32)
    core_ref = core.reshape(1)
    whole = (share, 4 * w)

    lower = jnp.concatenate([panel_one, panel_two], axis=1)
    places = landing_places(chips, planes)
    pairs = []
    for q in range(chips):
        for k in range(CORES):
            for z in range(planes):
                pairs.append(((q * CORES + k) * planes + z, (places[q][z] * CORES + k) * planes + q))
    moved = lax.ppermute(lower, GRID, pairs)
    parity = lax.axis_index("pair").astype(jnp.int32)
    plane = lax.axis_index("far") * NEAR + lax.axis_index("mid") * PAIR + parity
    order = lax.dynamic_index_in_dim(jnp.array(places, jnp.int32), plane, 0, keepdims=False)
    place = jnp.stack([core, parity * chips + chip, parity])
    flat = (w // LANES, 3 * w, LANES)
    chunk = 3 * w * w // LANES // (chips * PAIR)
    pivot = pl.pallas_call(
        functools.partial(pivot_body, w),
        name="pivot",
        in_specs=[SMEM, VMEM, VMEM, SMEM],
        out_specs=VMEM,
        out_shape=jax.ShapeDtypeStruct((chunk, LANES), F32),
        scratch_shapes=[pltpu.VMEM((3 * w * w // LANES, LANES), F32)],
    )(place, diag_inverse_one, diag_inverse_two, widths)
    ancestors = (ancestors_one, ancestors_two)
    limits = jnp.concatenate(
        [
            column_limits(ancestors, widths, chip * CORES),
            column_limits(ancestors, widths, chip * CORES + 1),
        ]
    )
    away_limits = jnp.concatenate(
        [
            column_limits(ancestors, widths, plane * CORES + core),
            column_limits(ancestors, widths, plane * CORES + 1 - core),
        ]
    )
    moved, order, place, pivot, limits, away_limits = lax.optimization_barrier(
        (moved, order, place, pivot, limits, away_limits)
    )
    (moved,) = kernel_call(copy_body, "copies", [VMEM], [((chips,) + whole, BF16)])(moved)
    mine = exchange(moved, "chip")
    other = swap_cores(mine)

    half = (planes // PAIR,) + whole
    keep, give = pl.pallas_call(
        functools.partial(product_body, w),
        name="product",
        in_specs=[SMEM] * 4 + [VMEM] * 3,
        out_specs=[VMEM] * 2,
        out_shape=[jax.ShapeDtypeStruct(half, BF16)] * 2,
        scratch_shapes=[
            pltpu.VMEM((CORES * chips * share, 4 * w), BF16),
            pltpu.VMEM((planes,) + whole, BF16),
        ],
        compiler_params=pltpu.CompilerParams(vmem_limit_bytes=40 * 1024 * 1024),
    )(core_ref, parity.reshape(1), order, away_limits, ancestor_inverse, mine, other)
    give, late = lax.optimization_barrier((give, lower))
    got = lax.ppermute(give, "pair", [(0, 1), (1, 0)])
    lowers = exchange(jnp.broadcast_to(late[None], (CORES * PAIR,) + whole), ("core", "pair"))
    got, lowers = lax.optimization_barrier((got, lowers))
    (part,) = kernel_call(pair_sum_body, "pair_sum", [VMEM] * 2, [(half, BF16)])(keep, got)
    part = exchange(part, ("far", "mid"))
    column_one, column_two, packed = kernel_call(
        functools.partial(column_body, w),
        "columns",
        [SMEM] * 2 + [VMEM] * 2 + [SMEM],
        [((share, 2 * w), BF16)] * 2 + [((CORES * PAIR, share, 2 * w), BF16)],
    )(place, limits, part, link_two, widths)
    sums = pl.pallas_call(
        functools.partial(sums_body, w),
        name="sums",
        in_specs=[SMEM] * 2 + [VMEM] * 2,
        out_specs=VMEM,
        out_shape=jax.ShapeDtypeStruct(flat[1:], BF16),
        scratch_shapes=[pltpu.VMEM((CORES * PAIR * share, 2 * w), BF16)] * 2,
        compiler_params=pltpu.CompilerParams(vmem_limit_bytes=40 * 1024 * 1024),
    )(place, limits, exchange(packed, ("core", "pair")), lowers)
    sums = exchange(sums.reshape(chips, chunk, LANES), "chip")
    (sums,) = kernel_call(chunk_sum_body, "chunk_sum", [VMEM], [((planes // PAIR, chunk, LANES), BF16)])(
        sums
    )
    sums = exchange(sums, ("far", "mid"))
    (total,) = kernel_call(
        all_sum_body, "all_sum", [VMEM] * 2, [((chips * PAIR, chunk, LANES), BF16)]
    )(sums, pivot)
    mine = exchange(total, ("pair", "chip")).reshape(flat)
    other = swap_cores(mine)
    block_one, parent_rows, block_two = kernel_call(
        functools.partial(final_body, w),
        "final",
        [SMEM, VMEM, VMEM, VMEM, SMEM],
        [((2, w, w), BF16)] * 3,
    )(core_ref, mine, other, link_two, widths)
    return column_one, block_one, column_two, parent_rows, block_two


def solution(mesh):
    rows_n, cols_n = mesh.devices.shape
    sizes = (rows_n // CORES, CORES, cols_n // NEAR, NEAR // PAIR, PAIR)
    fine = Mesh(mesh.devices.reshape(sizes), GRID)
    row, col = GRID[:2], GRID[2:]
    shared = P(GRID, None)
    in_specs = (P(row, col), shared, P(), P(), shared, P(), P(), P(), P())
    out_specs = (shared, P(), shared, P(), P())
    return jax.shard_map(local, mesh=fine, in_specs=in_specs, out_specs=out_specs, check_vma=False)
```

```python
import functools

import jax
import jax.numpy as jnp
from jax import lax
from jax.experimental import pallas as pl
from jax.experimental.pallas import tpu as pltpu
from jax.sharding import Mesh
from jax.sharding import PartitionSpec as P

F32 = jnp.float32
BF16 = jnp.bfloat16
VMEM = pl.BlockSpec(memory_space=pltpu.VMEM)
ANY = pl.BlockSpec(memory_space=pl.ANY)
SMEM = pl.BlockSpec(memory_space=pltpu.SMEM)
NEAR = 4
PAIR = 2
CORES = 2
LANES = 128
GRID = ("chip", "core", "far", "mid", "pair")


def kernel_call(body, name, specs, outs):
    return pl.pallas_call(
        body,
        name=name,
        in_specs=specs,
        out_specs=[VMEM] * len(outs),
        out_shape=[jax.ShapeDtypeStruct(shape, kind) for shape, kind in outs],
        compiler_params=pltpu.CompilerParams(vmem_limit_bytes=40 * 1024 * 1024),
    )


def exchange(blocks, axis):
    return lax.all_to_all(blocks, axis, split_axis=0, concat_axis=0, tiled=True)


def landing_places(chips, planes):
    side = int(chips**0.5)

    def steps(a, b):
        return abs(a // side - b // side) + abs(a % side - b % side)

    places = []
    for q in range(chips):
        far_first = sorted(range(planes), key=lambda z: (-abs(z - q), z))
        close_first = sorted(range(chips), key=lambda p: (steps(p, q), p))
        spots = dict(zip(far_first, close_first))
        places.append([spots[z] for z in range(planes)])
    return places


def swap_cores(block):
    return lax.ppermute(block, "core", [(0, 1), (1, 0)])


def dot(left, right):
    return jnp.dot(left, right, preferred_element_type=F32)


def dot_t(left, right):
    return lax.dot_general(left, right, (((0,), (0,)), ((), ())), preferred_element_type=F32)


def reduced(received):
    total = received[0].astype(F32)
    for i in range(1, received.shape[0]):
        total = total + received[i].astype(F32)
    return total


def column_limits(ancestors, widths, tile):
    here = [jnp.any(table == tile, axis=1) for table in ancestors]
    return jnp.where(jnp.concatenate(here), widths, 0)


def inside_limits(limits, first, shape, w):
    column = lax.broadcasted_iota(jnp.int32, shape, 1)
    limit = jnp.zeros(shape, jnp.int32)
    for k in range(shape[1] // w):
        limit = jnp.where(column >= k * w, limits[first + k] + k * w, limit)
    return column < limit


def masked_link(w, link, widths, s):
    row = lax.broadcasted_iota(jnp.int32, (w, w), 0)
    column = lax.broadcasted_iota(jnp.int32, (w, w), 1)
    value = link[s]
    inside = (row < widths[s]) & (column < widths[2 + s])
    return jnp.where(inside, value, jnp.zeros_like(value))


def copy_body(source, copies):
    value = source[...]
    for i in range(copies.shape[0]):
        copies[i] = value


def product_body(
    w, core, parity, order, limits, inverse, mine, other, keep, give, held, part
):
    blocks, share, _ = mine.shape
    half = blocks * share
    for source, first, start in ((mine, 0, 0), (other, 4, half)):
        inside = inside_limits(limits, first, (share, 4 * w), w)
        for i in range(blocks):
            value = source[order[i]]
            value = jnp.where(inside, value, jnp.zeros_like(value))
            held[start + i * share : start + (i + 1) * share, :] = value
    left = inverse[:, pl.ds(pl.multiple_of(core[0] * half, half), half)]
    right = inverse[:, pl.ds(pl.multiple_of((1 - core[0]) * half, half), half)]
    for k in range(4):
        span = slice(k * w, (k + 1) * w)
        value = (dot(left, held[:half, span]) + dot(right, held[half:, span])).astype(BF16)
        for i in range(part.shape[0]):
            part[i, :, span] = value[i * share : (i + 1) * share]
    for i in range(keep.shape[0]):
        keep[i] = part[PAIR * i + parity[0]]
        give[i] = part[PAIR * i + 1 - parity[0]]


def pair_sum_body(keep, got, sums):
    for i in range(sums.shape[0]):
        sums[i] = (keep[i].astype(F32) + got[i].astype(F32)).astype(BF16)


def column_body(
    w, place, limits, received, panels, link, widths, column_one, column_two, packed
):
    total = reduced(received)
    for s in range(2):
        span = slice(s * w, (s + 1) * w)
        here_one = jnp.where(limits[s] > 0, 1.0, 0.0)
        here_two = jnp.where(limits[2 + s] > 0, 1.0, 0.0)
        column = (-(total[:, span] * here_one)).astype(BF16)
        column_one[:, span] = column
        second = total[:, (2 + s) * w : (3 + s) * w] + dot(column, masked_link(w, link, widths, s))
        column_two[:, span] = (-(second * here_two)).astype(BF16)
    inside = inside_limits(limits, 0, panels.shape, w)
    lower = jnp.where(inside, panels[...], jnp.zeros_like(panels[...]))
    for n in range(packed.shape[0]):
        span = slice((n // PAIR) * w, (n // PAIR + 1) * w)
        packed[n, :, :w] = column_one[:, span]
        packed[n, :, w : 2 * w] = column_two[:, span]
        packed[n, :, 2 * w : 3 * w] = lower[:, span]
        other = slice((2 + n // PAIR) * w, (3 + n // PAIR) * w)
        packed[n, :, 3 * w :] = lower[:, other]


def sums_body(w, place, received, sums, held):
    share = received.shape[1]
    for n in range(received.shape[0]):
        held[n * share : (n + 1) * share, :] = received[n]
    start = pl.multiple_of(place[2] * LANES, LANES)
    low, high = pl.ds(start, LANES), pl.ds(pl.multiple_of(w + start, LANES), LANES)
    late = pl.ds(pl.multiple_of(3 * w + start, LANES), LANES)
    first, second = held[:, 2 * w : 3 * w], held[:, 3 * w :]
    sums[0:w, :] = (-dot_t(first, held[:, low])).astype(BF16)
    sums[w : 2 * w, :] = dot_t(held[:, :w], held[:, late]).astype(BF16)
    sums[2 * w :, :] = (-dot_t(second, held[:, high])).astype(BF16)


def chunk_sum_body(received, copies):
    value = reduced(received).astype(BF16)
    for i in range(copies.shape[0]):
        copies[i] = value


def pivot_body(w, place, one, two, widths, pivot, stack):
    row = lax.broadcasted_iota(jnp.int32, (w, w), 0)
    column = lax.broadcasted_iota(jnp.int32, (w, w), 1)
    lanes = stack.shape[1]
    for b, source, width in (
        (0, one, widths[place[0]]),
        (1, None, 0),
        (2, two, widths[2 + place[0]]),
    ):
        value = jnp.zeros((w, w), F32)
        if source is not None:
            value = jnp.where((row < width) & (column < width), source[place[0]].astype(F32), value)
        for h in range(w // lanes):
            start = (3 * h + b) * w
            stack[start : start + w, :] = value[:, h * lanes : (h + 1) * lanes]
    size = pivot.shape[0]
    pivot[...] = stack[pl.ds(pl.multiple_of(place[1] * size, size), size), :]


def all_sum_body(received, pivot, copies):
    total = (reduced(received) + pivot[...]).astype(BF16)
    for i in range(copies.shape[0]):
        copies[i] = total


def side_by_side(total, b, w):
    span = slice(b * w, (b + 1) * w)
    return jnp.concatenate([total[h, span, :] for h in range(total.shape[0])], axis=1)


def final_body(w, core, mine, other, link, widths, block_one, parent_rows, block_two):
    for total, sibling in ((mine, core[0]), (other, 1 - core[0])):
        tie = masked_link(w, link, widths, sibling)
        block = side_by_side(total, 0, w)
        cross = side_by_side(total, 1, w).astype(F32)
        block_one[sibling] = block
        parent = (-(dot(block, tie) + cross)).astype(BF16)
        parent_rows[sibling] = parent
        rest = side_by_side(total, 2, w).astype(F32) - dot_t(tie, parent)
        block_two[sibling] = rest.astype(BF16)


def local(
    ancestor_inverse,
    panel_one,
    ancestors_one,
    diag_inverse_one,
    panel_two,
    link_two,
    ancestors_two,
    diag_inverse_two,
    widths,
):
    w = diag_inverse_one.shape[-1]
    chips, far_n = lax.axis_size("chip"), lax.axis_size("far")
    planes = far_n * NEAR
    local_rows = ancestor_inverse.shape[0]
    share = panel_one.shape[0]
    chip = lax.axis_index("chip").astype(jnp.int32)
    core = lax.axis_index("core").astype(jnp.int32)
    core_ref = core.reshape(1)
    whole = (share, 4 * w)

    lower = jnp.concatenate([panel_one, panel_two], axis=1)
    places = landing_places(chips, planes)
    pairs = []
    for q in range(chips):
        for k in range(CORES):
            for z in range(planes):
                pairs.append(((q * CORES + k) * planes + z, (places[q][z] * CORES + k) * planes + q))
    moved = lax.ppermute(lower, GRID, pairs)
    parity = lax.axis_index("pair").astype(jnp.int32)
    plane = lax.axis_index("far") * NEAR + lax.axis_index("mid") * PAIR + parity
    order = lax.dynamic_index_in_dim(jnp.array(places, jnp.int32), plane, 0, keepdims=False)
    place = jnp.stack([core, parity * chips + chip, parity])
    flat = (w // LANES, 3 * w, LANES)
    chunk = 3 * w * w // LANES // (chips * PAIR)
    pivot = pl.pallas_call(
        functools.partial(pivot_body, w),
        name="pivot",
        in_specs=[SMEM, VMEM, VMEM, SMEM],
        out_specs=VMEM,
        out_shape=jax.ShapeDtypeStruct((chunk, LANES), F32),
        scratch_shapes=[pltpu.VMEM((3 * w * w // LANES, LANES), F32)],
    )(place, diag_inverse_one, diag_inverse_two, widths)
    ancestors = (ancestors_one, ancestors_two)
    limits = column_limits(ancestors, widths, chip * CORES + core)
    away_limits = jnp.concatenate(
        [
            column_limits(ancestors, widths, plane * CORES + core),
            column_limits(ancestors, widths, plane * CORES + 1 - core),
        ]
    )
    moved, order, place, pivot, limits, away_limits = lax.optimization_barrier(
        (moved, order, place, pivot, limits, away_limits)
    )
    (moved,) = kernel_call(copy_body, "copies", [VMEM], [((chips,) + whole, BF16)])(moved)
    mine = exchange(moved, "chip")
    other = swap_cores(mine)

    half = (planes // PAIR,) + whole
    keep, give = pl.pallas_call(
        functools.partial(product_body, w),
        name="product",
        in_specs=[SMEM] * 4 + [VMEM] * 3,
        out_specs=[VMEM] * 2,
        out_shape=[jax.ShapeDtypeStruct(half, BF16)] * 2,
        scratch_shapes=[
            pltpu.VMEM((CORES * chips * share, 4 * w), BF16),
            pltpu.VMEM((planes,) + whole, BF16),
        ],
        compiler_params=pltpu.CompilerParams(vmem_limit_bytes=40 * 1024 * 1024),
    )(core_ref, parity.reshape(1), order, away_limits, ancestor_inverse, mine, other)
    got = lax.ppermute(give, "pair", [(0, 1), (1, 0)])
    (part,) = kernel_call(pair_sum_body, "pair_sum", [VMEM] * 2, [(half, BF16)])(keep, got)
    part = exchange(part, ("far", "mid"))
    column_one, column_two, packed = kernel_call(
        functools.partial(column_body, w),
        "columns",
        [SMEM] * 2 + [VMEM] * 3 + [SMEM],
        [((share, 2 * w), BF16)] * 2 + [((CORES * PAIR,) + whole, BF16)],
    )(place, limits, part, lower, link_two, widths)
    sums = pl.pallas_call(
        functools.partial(sums_body, w),
        name="sums",
        in_specs=[SMEM, VMEM],
        out_specs=VMEM,
        out_shape=jax.ShapeDtypeStruct(flat[1:], BF16),
        scratch_shapes=[pltpu.VMEM((CORES * PAIR * share, 4 * w), BF16)],
        compiler_params=pltpu.CompilerParams(vmem_limit_bytes=40 * 1024 * 1024),
    )(place, exchange(packed, ("core", "pair")))
    sums = exchange(sums.reshape(chips, chunk, LANES), "chip")
    (sums,) = kernel_call(chunk_sum_body, "chunk_sum", [VMEM], [((planes // PAIR, chunk, LANES), BF16)])(
        sums
    )
    sums = exchange(sums, ("far", "mid"))
    (total,) = kernel_call(
        all_sum_body, "all_sum", [VMEM] * 2, [((chips * PAIR, chunk, LANES), BF16)]
    )(sums, pivot)
    mine = exchange(total, ("pair", "chip")).reshape(flat)
    other = swap_cores(mine)
    block_one, parent_rows, block_two = kernel_call(
        functools.partial(final_body, w),
        "final",
        [SMEM, VMEM, VMEM, VMEM, SMEM],
        [((2, w, w), BF16)] * 3,
    )(core_ref, mine, other, link_two, widths)
    return column_one, block_one, column_two, parent_rows, block_two


def solution(mesh):
    rows_n, cols_n = mesh.devices.shape
    sizes = (rows_n // CORES, CORES, cols_n // NEAR, NEAR // PAIR, PAIR)
    fine = Mesh(mesh.devices.reshape(sizes), GRID)
    row, col = GRID[:2], GRID[2:]
    shared = P(GRID, None)
    in_specs = (P(row, col), shared, P(), P(), shared, P(), P(), P(), P())
    out_specs = (shared, P(), shared, P(), P())
    return jax.shard_map(local, mesh=fine, in_specs=in_specs, out_specs=out_specs, check_vma=False)
```

```python
import functools

import jax
import jax.numpy as jnp
from jax import lax
from jax.experimental import pallas as pl
from jax.experimental.pallas import tpu as pltpu
from jax.sharding import Mesh
from jax.sharding import PartitionSpec as P

F32 = jnp.float32
BF16 = jnp.bfloat16
VMEM = pl.BlockSpec(memory_space=pltpu.VMEM)
ANY = pl.BlockSpec(memory_space=pl.ANY)
SMEM = pl.BlockSpec(memory_space=pltpu.SMEM)
NEAR = 4
PAIR = 2
CORES = 2
LANES = 128
GRID = ("chip", "core", "far", "mid", "pair")


def kernel_call(body, name, specs, outs):
    return pl.pallas_call(
        body,
        name=name,
        in_specs=specs,
        out_specs=[VMEM] * len(outs),
        out_shape=[jax.ShapeDtypeStruct(shape, kind) for shape, kind in outs],
        compiler_params=pltpu.CompilerParams(vmem_limit_bytes=40 * 1024 * 1024),
    )


def exchange(blocks, axis):
    return lax.all_to_all(blocks, axis, split_axis=0, concat_axis=0, tiled=True)


def landing_places(chips, planes):
    side = int(chips**0.5)

    def steps(a, b):
        return abs(a // side - b // side) + abs(a % side - b % side)

    places = []
    for q in range(chips):
        far_first = sorted(range(planes), key=lambda z: (-abs(z - q), z))
        close_first = sorted(range(chips), key=lambda p: (steps(p, q), p))
        spots = dict(zip(far_first, close_first))
        places.append([spots[z] for z in range(planes)])
    return places


def swap_cores(block):
    return lax.ppermute(block, "core", [(0, 1), (1, 0)])


def dot(left, right):
    return jnp.dot(left, right, preferred_element_type=F32)


def dot_t(left, right):
    return lax.dot_general(left, right, (((0,), (0,)), ((), ())), preferred_element_type=F32)


def reduced(received):
    total = received[0].astype(F32)
    for i in range(1, received.shape[0]):
        total = total + received[i].astype(F32)
    return total


def column_limits(ancestors, widths, tile):
    here = [jnp.any(table == tile, axis=1) for table in ancestors]
    return jnp.where(jnp.concatenate(here), widths, 0)


def inside_limits(limits, first, shape, w):
    column = lax.broadcasted_iota(jnp.int32, shape, 1)
    limit = jnp.zeros(shape, jnp.int32)
    for k in range(shape[1] // w):
        limit = jnp.where(column >= k * w, limits[first + k] + k * w, limit)
    return column < limit


def masked_link(w, link, widths, s):
    row = lax.broadcasted_iota(jnp.int32, (w, w), 0)
    column = lax.broadcasted_iota(jnp.int32, (w, w), 1)
    value = link[s]
    inside = (row < widths[s]) & (column < widths[2 + s])
    return jnp.where(inside, value, jnp.zeros_like(value))


def copy_body(source, copies):
    value = source[...]
    for i in range(copies.shape[0]):
        copies[i] = value


def product_body(
    w, core, parity, order, limits, inverse, mine, other, keep, give, held, part
):
    blocks, share, _ = mine.shape
    half = blocks * share
    for source, first, start in ((mine, 0, 0), (other, 4, half)):
        inside = inside_limits(limits, first, (share, 4 * w), w)
        for i in range(blocks):
            value = source[order[i]]
            value = jnp.where(inside, value, jnp.zeros_like(value))
            held[start + i * share : start + (i + 1) * share, :] = value
    left = inverse[:, pl.ds(pl.multiple_of(core[0] * half, half), half)]
    right = inverse[:, pl.ds(pl.multiple_of((1 - core[0]) * half, half), half)]
    for k in range(4):
        span = slice(k * w, (k + 1) * w)
        value = (dot(left, held[:half, span]) + dot(right, held[half:, span])).astype(BF16)
        for i in range(part.shape[0]):
            part[i, :, span] = value[i * share : (i + 1) * share]
    for i in range(keep.shape[0]):
        keep[i] = part[PAIR * i + parity[0]]
        give[i] = part[PAIR * i + 1 - parity[0]]


def pair_sum_body(keep, got, sums):
    for i in range(sums.shape[0]):
        sums[i] = (keep[i].astype(F32) + got[i].astype(F32)).astype(BF16)


def column_body(
    w, place, limits, received, panels, link, widths, packed
):
    total = reduced(received)
    inside = inside_limits(limits, 0, panels.shape, w)
    lower = jnp.where(inside, panels[...], jnp.zeros_like(panels[...]))
    for s in range(2):
        first = slice(s * w, (s + 1) * w)
        second = slice((2 + s) * w, (3 + s) * w)
        here_one = jnp.where(limits[s] > 0, 1.0, 0.0)
        here_two = jnp.where(limits[2 + s] > 0, 1.0, 0.0)
        one = (-(total[:, first] * here_one)).astype(BF16)
        two = total[:, second] + dot(one, masked_link(w, link, widths, s))
        two = (-(two * here_two)).astype(BF16)
        for n in range(s * PAIR, (s + 1) * PAIR):
            packed[n, :, :w] = one
            packed[n, :, w : 2 * w] = two
            packed[n, :, 2 * w : 3 * w] = lower[:, first]
            packed[n, :, 3 * w :] = lower[:, second]


def sums_body(w, place, received, sums, held):
    share = received.shape[1]
    for n in range(received.shape[0]):
        held[n * share : (n + 1) * share, :] = received[n]
    start = pl.multiple_of(place[2] * LANES, LANES)
    low, high = pl.ds(start, LANES), pl.ds(pl.multiple_of(w + start, LANES), LANES)
    late = pl.ds(pl.multiple_of(3 * w + start, LANES), LANES)
    first, second = held[:, 2 * w : 3 * w], held[:, 3 * w :]
    sums[0:w, :] = (-dot_t(first, held[:, low])).astype(BF16)
    sums[w : 2 * w, :] = dot_t(held[:, :w], held[:, late]).astype(BF16)
    sums[2 * w :, :] = (-dot_t(second, held[:, high])).astype(BF16)


def chunk_sum_body(received, copies):
    value = reduced(received).astype(BF16)
    for i in range(copies.shape[0]):
        copies[i] = value


def pivot_body(w, place, one, two, widths, pivot, stack):
    row = lax.broadcasted_iota(jnp.int32, (w, w), 0)
    column = lax.broadcasted_iota(jnp.int32, (w, w), 1)
    lanes = stack.shape[1]
    for b, source, width in (
        (0, one, widths[place[0]]),
        (1, None, 0),
        (2, two, widths[2 + place[0]]),
    ):
        value = jnp.zeros((w, w), F32)
        if source is not None:
            value = jnp.where((row < width) & (column < width), source[place[0]].astype(F32), value)
        for h in range(w // lanes):
            start = (3 * h + b) * w
            stack[start : start + w, :] = value[:, h * lanes : (h + 1) * lanes]
    size = pivot.shape[0]
    pivot[...] = stack[pl.ds(pl.multiple_of(place[1] * size, size), size), :]


def all_sum_body(received, pivot, copies):
    total = (reduced(received) + pivot[...]).astype(BF16)
    for i in range(copies.shape[0]):
        copies[i] = total


def side_by_side(total, b, w):
    span = slice(b * w, (b + 1) * w)
    return jnp.concatenate([total[h, span, :] for h in range(total.shape[0])], axis=1)


def final_body(w, core, mine, other, link, widths, block_one, parent_rows, block_two):
    for total, sibling in ((mine, core[0]), (other, 1 - core[0])):
        tie = masked_link(w, link, widths, sibling)
        block = side_by_side(total, 0, w)
        cross = side_by_side(total, 1, w).astype(F32)
        block_one[sibling] = block
        parent = (-(dot(block, tie) + cross)).astype(BF16)
        parent_rows[sibling] = parent
        rest = side_by_side(total, 2, w).astype(F32) - dot_t(tie, parent)
        block_two[sibling] = rest.astype(BF16)


def local(
    ancestor_inverse,
    panel_one,
    ancestors_one,
    diag_inverse_one,
    panel_two,
    link_two,
    ancestors_two,
    diag_inverse_two,
    widths,
):
    w = diag_inverse_one.shape[-1]
    chips, far_n = lax.axis_size("chip"), lax.axis_size("far")
    planes = far_n * NEAR
    local_rows = ancestor_inverse.shape[0]
    share = panel_one.shape[0]
    chip = lax.axis_index("chip").astype(jnp.int32)
    core = lax.axis_index("core").astype(jnp.int32)
    core_ref = core.reshape(1)
    whole = (share, 4 * w)

    lower = jnp.concatenate([panel_one, panel_two], axis=1)
    places = landing_places(chips, planes)
    pairs = []
    for q in range(chips):
        for k in range(CORES):
            for z in range(planes):
                pairs.append(((q * CORES + k) * planes + z, (places[q][z] * CORES + k) * planes + q))
    moved = lax.ppermute(lower, GRID, pairs)
    parity = lax.axis_index("pair").astype(jnp.int32)
    plane = lax.axis_index("far") * NEAR + lax.axis_index("mid") * PAIR + parity
    order = lax.dynamic_index_in_dim(jnp.array(places, jnp.int32), plane, 0, keepdims=False)
    place = jnp.stack([core, parity * chips + chip, parity])
    flat = (w // LANES, 3 * w, LANES)
    chunk = 3 * w * w // LANES // (chips * PAIR)
    pivot = pl.pallas_call(
        functools.partial(pivot_body, w),
        name="pivot",
        in_specs=[SMEM, VMEM, VMEM, SMEM],
        out_specs=VMEM,
        out_shape=jax.ShapeDtypeStruct((chunk, LANES), F32),
        scratch_shapes=[pltpu.VMEM((3 * w * w // LANES, LANES), F32)],
    )(place, diag_inverse_one, diag_inverse_two, widths)
    ancestors = (ancestors_one, ancestors_two)
    limits = column_limits(ancestors, widths, chip * CORES + core)
    away_limits = jnp.concatenate(
        [
            column_limits(ancestors, widths, plane * CORES + core),
            column_limits(ancestors, widths, plane * CORES + 1 - core),
        ]
    )
    moved, order, place, pivot, limits, away_limits = lax.optimization_barrier(
        (moved, order, place, pivot, limits, away_limits)
    )
    (moved,) = kernel_call(copy_body, "copies", [VMEM], [((chips,) + whole, BF16)])(moved)
    mine = exchange(moved, "chip")
    other = swap_cores(mine)

    half = (planes // PAIR,) + whole
    keep, give = pl.pallas_call(
        functools.partial(product_body, w),
        name="product",
        in_specs=[SMEM] * 4 + [VMEM] * 3,
        out_specs=[VMEM] * 2,
        out_shape=[jax.ShapeDtypeStruct(half, BF16)] * 2,
        scratch_shapes=[
            pltpu.VMEM((CORES * chips * share, 4 * w), BF16),
            pltpu.VMEM((planes,) + whole, BF16),
        ],
        compiler_params=pltpu.CompilerParams(vmem_limit_bytes=40 * 1024 * 1024),
    )(core_ref, parity.reshape(1), order, away_limits, ancestor_inverse, mine, other)
    got = lax.ppermute(give, "pair", [(0, 1), (1, 0)])
    (part,) = kernel_call(pair_sum_body, "pair_sum", [VMEM] * 2, [(half, BF16)])(keep, got)
    part = exchange(part, ("far", "mid"))
    (packed,) = kernel_call(
        functools.partial(column_body, w),
        "columns",
        [SMEM] * 2 + [VMEM] * 3 + [SMEM],
        [((CORES * PAIR,) + whole, BF16)],
    )(place, limits, part, lower, link_two, widths)
    sums = pl.pallas_call(
        functools.partial(sums_body, w),
        name="sums",
        in_specs=[SMEM, VMEM],
        out_specs=VMEM,
        out_shape=jax.ShapeDtypeStruct(flat[1:], BF16),
        scratch_shapes=[pltpu.VMEM((CORES * PAIR * share, 4 * w), BF16)],
        compiler_params=pltpu.CompilerParams(vmem_limit_bytes=40 * 1024 * 1024),
    )(place, exchange(packed, ("core", "pair")))
    sums = exchange(sums.reshape(chips, chunk, LANES), "chip")
    (sums,) = kernel_call(chunk_sum_body, "chunk_sum", [VMEM], [((planes // PAIR, chunk, LANES), BF16)])(
        sums
    )
    sums = exchange(sums, ("far", "mid"))
    (total,) = kernel_call(
        all_sum_body, "all_sum", [VMEM] * 2, [((chips * PAIR, chunk, LANES), BF16)]
    )(sums, pivot)
    mine = exchange(total, ("pair", "chip")).reshape(flat)
    other = swap_cores(mine)
    column_one = jnp.concatenate([packed[0, :, :w], packed[PAIR, :, :w]], axis=1)
    column_two = jnp.concatenate([packed[0, :, w : 2 * w], packed[PAIR, :, w : 2 * w]], axis=1)
    block_one, parent_rows, block_two = kernel_call(
        functools.partial(final_body, w),
        "final",
        [SMEM, VMEM, VMEM, VMEM, SMEM],
        [((2, w, w), BF16)] * 3,
    )(core_ref, mine, other, link_two, widths)
    return column_one, block_one, column_two, parent_rows, block_two


def solution(mesh):
    rows_n, cols_n = mesh.devices.shape
    sizes = (rows_n // CORES, CORES, cols_n // NEAR, NEAR // PAIR, PAIR)
    fine = Mesh(mesh.devices.reshape(sizes), GRID)
    row, col = GRID[:2], GRID[2:]
    shared = P(GRID, None)
    in_specs = (P(row, col), shared, P(), P(), shared, P(), P(), P(), P())
    out_specs = (shared, P(), shared, P(), P())
    return jax.shard_map(local, mesh=fine, in_specs=in_specs, out_specs=out_specs, check_vma=False)
```

```python
import functools

import jax
import jax.numpy as jnp
from jax import lax
from jax.experimental import pallas as pl
from jax.experimental.pallas import tpu as pltpu
from jax.sharding import Mesh
from jax.sharding import PartitionSpec as P

F32 = jnp.float32
BF16 = jnp.bfloat16
VMEM = pl.BlockSpec(memory_space=pltpu.VMEM)
ANY = pl.BlockSpec(memory_space=pl.ANY)
SMEM = pl.BlockSpec(memory_space=pltpu.SMEM)
NEAR = 4
PAIR = 2
CORES = 2
LANES = 128
GRID = ("chip", "core", "far", "mid", "pair")


def kernel_call(body, name, specs, outs):
    return pl.pallas_call(
        body,
        name=name,
        in_specs=specs,
        out_specs=[VMEM] * len(outs),
        out_shape=[jax.ShapeDtypeStruct(shape, kind) for shape, kind in outs],
        compiler_params=pltpu.CompilerParams(vmem_limit_bytes=40 * 1024 * 1024),
    )


def exchange(blocks, axis):
    return lax.all_to_all(blocks, axis, split_axis=0, concat_axis=0, tiled=True)


def landing_places(chips, planes):
    side = int(chips**0.5)

    def steps(a, b):
        return abs(a // side - b // side) + abs(a % side - b % side)

    places = []
    for q in range(chips):
        far_first = sorted(range(planes), key=lambda z: (-abs(z - q), z))
        close_first = sorted(range(chips), key=lambda p: (steps(p, q), p))
        spots = dict(zip(far_first, close_first))
        places.append([spots[z] for z in range(planes)])
    return places


def swap_cores(block):
    return lax.ppermute(block, "core", [(0, 1), (1, 0)])


def dot(left, right):
    return jnp.dot(left, right, preferred_element_type=F32)


def dot_t(left, right):
    return lax.dot_general(left, right, (((0,), (0,)), ((), ())), preferred_element_type=F32)


def reduced(received):
    total = received[0].astype(F32)
    for i in range(1, received.shape[0]):
        total = total + received[i].astype(F32)
    return total


def column_limits(ancestors, widths, tile):
    here = [jnp.any(table == tile, axis=1) for table in ancestors]
    return jnp.where(jnp.concatenate(here), widths, 0)


def inside_limits(limits, first, shape, w):
    column = lax.broadcasted_iota(jnp.int32, shape, 1)
    limit = jnp.zeros(shape, jnp.int32)
    for k in range(shape[1] // w):
        limit = jnp.where(column >= k * w, limits[first + k] + k * w, limit)
    return column < limit


def masked_link(w, link, widths, s):
    row = lax.broadcasted_iota(jnp.int32, (w, w), 0)
    column = lax.broadcasted_iota(jnp.int32, (w, w), 1)
    value = link[s]
    inside = (row < widths[s]) & (column < widths[2 + s])
    return jnp.where(inside, value, jnp.zeros_like(value))


def copy_body(source, copies):
    value = source[...]
    for i in range(copies.shape[0]):
        copies[i] = value


def product_body(
    w, core, parity, order, limits, inverse, mine, other, keep, give, held, part
):
    blocks, share, _ = mine.shape
    half = blocks * share
    for source, first, start in ((mine, 0, 0), (other, 4, half)):
        inside = inside_limits(limits, first, (share, 4 * w), w)
        for i in range(blocks):
            value = source[order[i]]
            value = jnp.where(inside, value, jnp.zeros_like(value))
            held[start + i * share : start + (i + 1) * share, :] = value
    left = inverse[:, pl.ds(pl.multiple_of(core[0] * half, half), half)]
    right = inverse[:, pl.ds(pl.multiple_of((1 - core[0]) * half, half), half)]
    for k in range(4):
        span = slice(k * w, (k + 1) * w)
        value = (dot(left, held[:half, span]) + dot(right, held[half:, span])).astype(BF16)
        for i in range(part.shape[0]):
            part[i, :, span] = value[i * share : (i + 1) * share]
    for i in range(keep.shape[0]):
        keep[i] = part[PAIR * i + parity[0]]
        give[i] = part[PAIR * i + 1 - parity[0]]


def pair_sum_body(keep, got, sums):
    for i in range(sums.shape[0]):
        sums[i] = (keep[i].astype(F32) + got[i].astype(F32)).astype(BF16)


def column_body(
    w, place, limits, received, panels, link, widths, packed
):
    total = reduced(received)
    inside = inside_limits(limits, 0, panels.shape, w)
    lower = jnp.where(inside, panels[...], jnp.zeros_like(panels[...]))
    for s in range(2):
        first = slice(s * w, (s + 1) * w)
        second = slice((2 + s) * w, (3 + s) * w)
        here_one = jnp.where(limits[s] > 0, 1.0, 0.0)
        here_two = jnp.where(limits[2 + s] > 0, 1.0, 0.0)
        one = (-(total[:, first] * here_one)).astype(BF16)
        two = total[:, second] + dot(one, masked_link(w, link, widths, s))
        two = (-(two * here_two)).astype(BF16)
        for n in range(s * PAIR, (s + 1) * PAIR):
            packed[n, :, :w] = one
            packed[n, :, w : 2 * w] = two
            packed[n, :, 2 * w : 3 * w] = lower[:, first]
            packed[n, :, 3 * w :] = lower[:, second]


def sums_body(w, place, received, sums, held):
    share = received.shape[1]
    for n in range(received.shape[0]):
        held[n * share : (n + 1) * share, :] = received[n]
    start = pl.multiple_of(place[2] * LANES, LANES)
    low, high = pl.ds(start, LANES), pl.ds(pl.multiple_of(w + start, LANES), LANES)
    late = pl.ds(pl.multiple_of(3 * w + start, LANES), LANES)
    first, second = held[:, 2 * w : 3 * w], held[:, 3 * w :]
    sums[0:w, :] = (-dot_t(first, held[:, low])).astype(BF16)
    sums[w : 2 * w, :] = dot_t(held[:, :w], held[:, late]).astype(BF16)
    sums[2 * w :, :] = (-dot_t(second, held[:, high])).astype(BF16)


def chunk_sum_body(received, copies):
    value = reduced(received).astype(BF16)
    for i in range(copies.shape[0]):
        copies[i] = value


def pivot_body(w, place, one, two, widths, pivot, stack):
    row = lax.broadcasted_iota(jnp.int32, (w, w), 0)
    column = lax.broadcasted_iota(jnp.int32, (w, w), 1)
    lanes = stack.shape[1]
    for b, source, width in (
        (0, one, widths[place[0]]),
        (1, None, 0),
        (2, two, widths[2 + place[0]]),
    ):
        value = jnp.zeros((w, w), F32)
        if source is not None:
            value = jnp.where((row < width) & (column < width), source[place[0]].astype(F32), value)
        for h in range(w // lanes):
            start = (3 * h + b) * w
            stack[start : start + w, :] = value[:, h * lanes : (h + 1) * lanes]
    size = pivot.shape[0]
    pivot[...] = stack[pl.ds(pl.multiple_of(place[1] * size, size), size), :]


def all_sum_body(received, pivot, copies):
    total = (reduced(received) + pivot[...]).astype(BF16)
    for i in range(copies.shape[0]):
        copies[i] = total


def side_by_side(total, b, w):
    span = slice(b * w, (b + 1) * w)
    return jnp.concatenate([total[h, span, :] for h in range(total.shape[0])], axis=1)


def final_body(w, core, mine, other, link, widths, block_one, parent_rows, block_two):
    for total, sibling in ((mine, core[0]), (other, 1 - core[0])):
        tie = masked_link(w, link, widths, sibling)
        block = side_by_side(total, 0, w)
        cross = side_by_side(total, 1, w).astype(F32)
        block_one[sibling] = block
        parent = (-(dot(block, tie) + cross)).astype(BF16)
        parent_rows[sibling] = parent
        rest = side_by_side(total, 2, w).astype(F32) - dot_t(tie, parent)
        block_two[sibling] = rest.astype(BF16)


def local(
    ancestor_inverse,
    panel_one,
    ancestors_one,
    diag_inverse_one,
    panel_two,
    link_two,
    ancestors_two,
    diag_inverse_two,
    widths,
):
    w = diag_inverse_one.shape[-1]
    chips, far_n = lax.axis_size("chip"), lax.axis_size("far")
    planes = far_n * NEAR
    local_rows = ancestor_inverse.shape[0]
    share = panel_one.shape[0]
    chip = lax.axis_index("chip").astype(jnp.int32)
    core = lax.axis_index("core").astype(jnp.int32)
    core_ref = core.reshape(1)
    whole = (share, 4 * w)

    lower = jnp.concatenate([panel_one, panel_two], axis=1)
    places = landing_places(chips, planes)
    pairs = []
    for q in range(chips):
        for k in range(CORES):
            for z in range(planes):
                pairs.append(((q * CORES + k) * planes + z, (places[q][z] * CORES + k) * planes + q))
    moved = lax.ppermute(lower, GRID, pairs)
    parity = lax.axis_index("pair").astype(jnp.int32)
    plane = lax.axis_index("far") * NEAR + lax.axis_index("mid") * PAIR + parity
    order = lax.dynamic_index_in_dim(jnp.array(places, jnp.int32), plane, 0, keepdims=False)
    place = jnp.stack([core, parity * chips + chip, parity])
    flat = (w // LANES, 3 * w, LANES)
    chunk = 3 * w * w // LANES // (chips * PAIR)
    pivot = pl.pallas_call(
        functools.partial(pivot_body, w),
        name="pivot",
        in_specs=[SMEM, VMEM, VMEM, SMEM],
        out_specs=VMEM,
        out_shape=jax.ShapeDtypeStruct((chunk, LANES), F32),
        scratch_shapes=[pltpu.VMEM((3 * w * w // LANES, LANES), F32)],
    )(place, diag_inverse_one, diag_inverse_two, widths)
    ancestors = (ancestors_one, ancestors_two)
    limits = column_limits(ancestors, widths, chip * CORES + core)
    away_limits = jnp.concatenate(
        [
            column_limits(ancestors, widths, plane * CORES + core),
            column_limits(ancestors, widths, plane * CORES + 1 - core),
        ]
    )
    moved, order, limits, away_limits = lax.optimization_barrier(
        (moved, order, limits, away_limits)
    )
    (moved,) = kernel_call(copy_body, "copies", [VMEM], [((chips,) + whole, BF16)])(moved)
    mine = exchange(moved, "chip")
    other = swap_cores(mine)

    half = (planes // PAIR,) + whole
    keep, give = pl.pallas_call(
        functools.partial(product_body, w),
        name="product",
        in_specs=[SMEM] * 4 + [VMEM] * 3,
        out_specs=[VMEM] * 2,
        out_shape=[jax.ShapeDtypeStruct(half, BF16)] * 2,
        scratch_shapes=[
            pltpu.VMEM((CORES * chips * share, 4 * w), BF16),
            pltpu.VMEM((planes,) + whole, BF16),
        ],
        compiler_params=pltpu.CompilerParams(vmem_limit_bytes=40 * 1024 * 1024),
    )(core_ref, parity.reshape(1), order, away_limits, ancestor_inverse, mine, other)
    got = lax.ppermute(give, "pair", [(0, 1), (1, 0)])
    got, place, pivot = lax.optimization_barrier((got, place, pivot))
    (part,) = kernel_call(pair_sum_body, "pair_sum", [VMEM] * 2, [(half, BF16)])(keep, got)
    part = exchange(part, ("far", "mid"))
    (packed,) = kernel_call(
        functools.partial(column_body, w),
        "columns",
        [SMEM] * 2 + [VMEM] * 3 + [SMEM],
        [((CORES * PAIR,) + whole, BF16)],
    )(place, limits, part, lower, link_two, widths)
    sums = pl.pallas_call(
        functools.partial(sums_body, w),
        name="sums",
        in_specs=[SMEM, VMEM],
        out_specs=VMEM,
        out_shape=jax.ShapeDtypeStruct(flat[1:], BF16),
        scratch_shapes=[pltpu.VMEM((CORES * PAIR * share, 4 * w), BF16)],
        compiler_params=pltpu.CompilerParams(vmem_limit_bytes=40 * 1024 * 1024),
    )(place, exchange(packed, ("core", "pair")))
    sums = exchange(sums.reshape(chips, chunk, LANES), "chip")
    (sums,) = kernel_call(chunk_sum_body, "chunk_sum", [VMEM], [((planes // PAIR, chunk, LANES), BF16)])(
        sums
    )
    sums = exchange(sums, ("far", "mid"))
    (total,) = kernel_call(
        all_sum_body, "all_sum", [VMEM] * 2, [((chips * PAIR, chunk, LANES), BF16)]
    )(sums, pivot)
    mine = exchange(total, ("pair", "chip")).reshape(flat)
    other = swap_cores(mine)
    column_one = jnp.concatenate([packed[0, :, :w], packed[PAIR, :, :w]], axis=1)
    column_two = jnp.concatenate([packed[0, :, w : 2 * w], packed[PAIR, :, w : 2 * w]], axis=1)
    block_one, parent_rows, block_two = kernel_call(
        functools.partial(final_body, w),
        "final",
        [SMEM, VMEM, VMEM, VMEM, SMEM],
        [((2, w, w), BF16)] * 3,
    )(core_ref, mine, other, link_two, widths)
    return column_one, block_one, column_two, parent_rows, block_two


def solution(mesh):
    rows_n, cols_n = mesh.devices.shape
    sizes = (rows_n // CORES, CORES, cols_n // NEAR, NEAR // PAIR, PAIR)
    fine = Mesh(mesh.devices.reshape(sizes), GRID)
    row, col = GRID[:2], GRID[2:]
    shared = P(GRID, None)
    in_specs = (P(row, col), shared, P(), P(), shared, P(), P(), P(), P())
    out_specs = (shared, P(), shared, P(), P())
    return jax.shard_map(local, mesh=fine, in_specs=in_specs, out_specs=out_specs, check_vma=False)
```
